32 devices in a mesh: proc: 8 (over z, y), loss: 2 (over x), vars: 2 (over core).
Axes of the slice: x: 2, y: 2, z: 4, core: 2. Of those that a mesh axis runs over, the one named last changes fastest.
Arguments:
- tokens: bfloat16 [16, 360, 1536], P('proc'), may hold values from -6 to 6
- shift: int32 [1], replicated, may hold values from 0 to 11
- w_qkv: bfloat16 [1536, 3, 16, 96], P(None, None, ('loss', 'vars')), may hold values from -0.15625 to 0.15625
- w_proj: bfloat16 [16, 96, 1536], replicated, may hold values from -0.15625 to 0.15625
- ln_gain: float32 [1536], replicated, may hold values from 0.1 to 1.9
- w_dec: bfloat16 [64, 4, 4, 1536], P(('loss', 'vars')), may hold values from -0.15625 to 0.15625
- prediction: bfloat16 [64, 64, 1440], P(('loss', 'vars'), 'proc'), may hold values from -6 to 6
- target: float32 [64, 64, 1440], P(('loss', 'vars'), 'proc'), may hold values from -12 to 12
- legendre: float32 [128, 64, 384], P('proc'), may hold values from -0.75 to 0.75
Outputs:
- amse: float32 [64], P(('loss', 'vars'))
- field_grad: float32 [64, 64, 1440], P(('loss', 'vars'), 'proc')
- input_grad: bfloat16 [16, 360, 1536], P('proc', None, ('loss', 'vars'))
The draws below stay inside these ranges and needn't reach their ends.
Inputs may be any that keep to these rules, and one draw needn't show every extreme that they name: `shift`: the offset is the same for all tokens.
All inputs are finite; a program needn't handle non-finite values.
Results may differ from the reference program's by a relative error of at most 0.012.
Values may be sent and summed in bfloat16 or wider, within the bound.
A program may use at most 128 MiB of HBM per device.

```python
import math
import jax
import jax.numpy as jnp
from jax import lax

D = 1536
HEADS = 16
HEAD = 96
VARS = 64
LON = 1440
LDEG = 384
WR = 2
WC = 12
TC = 360
TR = 16
LAT = 64
MODES = 128


def shard_levels(own_key, dims, shards, least, largest):
    factor_of, own = 1.0, jax.random.fold_in(own_key, 6)
    for axis_at, blocks in shards:
        steps = jnp.exp(jax.random.uniform(jax.random.fold_in(own, axis_at), (blocks,), jnp.float32, least / len(shards), largest / len(shards)))
        factor_of = factor_of * jnp.repeat(steps, dims[axis_at] // blocks).reshape([-1 if axis == axis_at else 1 for axis in range(len(dims))])
    return factor_of


def gaussian(stream_key, shape, width, reach, shards=(), kind=jnp.bfloat16):
    drawn = jax.random.normal(stream_key, shape, jnp.float32) * width
    if len(shards) > 0:
        drawn = shard_levels(stream_key, shape, shards, -0.22, 0.18) * drawn
    return jnp.clip(drawn, min=-reach, max=reach).astype(kind)


def setup_inputs(seed: int = 0) -> dict:
    key_list = jax.random.split(jax.random.key(seed), 10)
    return {
        "tokens": gaussian(key_list[0], (TR, TC, D), 1.0, 6.0, ((0, 8),)),
        "shift": jax.random.randint(key_list[1], (1,), 0, WC).astype(jnp.int32),
        "w_qkv": gaussian(key_list[2], (D, 3, HEADS, HEAD), D ** -0.5, 0.15625, ((2, 4),)),
        "w_proj": gaussian(key_list[3], (HEADS, HEAD, D), D ** -0.5, 0.15625),
        "ln_gain": jnp.clip(1.0 + 0.18 * jax.random.normal(key_list[4], (D,), jnp.float32), 0.1, 1.9),
        "w_dec": gaussian(key_list[5], (VARS, 4, 4, D), D ** -0.5, 0.15625, ((0, 4),)),
        "prediction": gaussian(key_list[6], (VARS, LAT, LON), 1.0, 6.0, ((0, 4), (1, 8))),
        "target": gaussian(key_list[7], (VARS, LAT, LON), 2.0, 12.0, ((0, 4), (1, 8)), jnp.float32),
        "legendre": gaussian(key_list[8], (MODES, LAT, LDEG), LAT ** -0.5, 0.75, ((0, 8),), jnp.float32),
    }


EPSILON = 1e-06
NORM_EPSILON = 1e-05
HIGHEST = lax.Precision.HIGHEST

def fourier_basis(mode_count):
    column = jnp.arange(LON, dtype=jnp.int32)
    wavenumber = jnp.arange(mode_count, dtype=jnp.int32)
    phase = (column[:, None] * wavenumber[None, :] % LON).astype(jnp.float32) * (2.0 * math.pi / LON)
    norm_factor = 1.0 / math.sqrt(LON)
    return jnp.stack([jnp.cos(phase) * norm_factor, -jnp.sin(phase) * norm_factor])

def amse_terms(power_pred, power_true, crossed):
    amp_pred = jnp.sqrt(power_pred + EPSILON)
    amp_true = jnp.sqrt(power_true + EPSILON)
    return (amp_pred - amp_true) ** 2 + 2.0 * jnp.maximum(power_pred, power_true) * (1.0 - crossed / (amp_pred * amp_true))

def spectral_loss(field_values, target, legendre, fourier):
    fields = jnp.stack([field_values, target])
    spectra = jnp.einsum('fvao,com->fvacm', fields, fourier, precision=HIGHEST)
    harmonics = jnp.einsum('fvacm,mal->fvmcl', spectra, legendre, precision=HIGHEST)
    power_pred = lax.optimization_barrier(jnp.sum(harmonics[0] ** 2, axis=(1, 2)))
    power_true = lax.optimization_barrier(jnp.sum(harmonics[1] ** 2, axis=(1, 2)))
    crossed = lax.optimization_barrier(jnp.sum(harmonics[0] * harmonics[1], axis=(1, 2)))
    per_var = lax.optimization_barrier(jnp.sum(amse_terms(power_pred, power_true, crossed), axis=-1)) / (LDEG * MODES)
    return (jnp.mean(per_var), per_var)

def norm_parts(rolled, ln_gain):
    values = rolled.astype(jnp.float32)
    centre = lax.optimization_barrier(jnp.mean(values, axis=-1, keepdims=True))
    centred = values - centre
    variance = lax.optimization_barrier(jnp.mean(centred * centred, axis=-1, keepdims=True))
    inv_std = lax.rsqrt(variance + NORM_EPSILON)
    normed = centred * inv_std
    return (normed, inv_std, (normed * ln_gain).astype(jnp.bfloat16))

def norm_backward(grad_normed, normed, inv_std, ln_gain):
    scaled = grad_normed * ln_gain
    return inv_std * (scaled - lax.optimization_barrier(jnp.mean(scaled, axis=-1, keepdims=True)) - normed * lax.optimization_barrier(jnp.mean(scaled * normed, axis=-1, keepdims=True)))

def to_windows(values):
    row_count, col_count = (values.shape[0], values.shape[1])
    trailing = values.shape[2:]
    shaped = values.reshape((row_count // WR, WR, col_count // WC, WC) + trailing)
    shaped = jnp.moveaxis(shaped, 2, 1)
    return shaped.reshape((row_count // WR * (col_count // WC), WR * WC) + trailing)

def from_windows(values, row_count, col_count):
    trailing = values.shape[2:]
    shaped = values.reshape((row_count // WR, col_count // WC, WR, WC) + trailing)
    shaped = jnp.moveaxis(shaped, 1, 2)
    return shaped.reshape((row_count, col_count) + trailing)

def window_backward(queries, key_win, value_win, grad_out):
    score_scale = HEAD ** (-0.5)
    scores = jnp.einsum('nihe,njhe->nhij', queries.astype(jnp.float32), key_win.astype(jnp.float32)) * score_scale
    weights = jnp.exp(scores)
    weights = weights / lax.optimization_barrier(jnp.sum(weights, axis=-1, keepdims=True))
    rounded = weights.astype(jnp.bfloat16)
    grad_values = jnp.einsum('nhij,nihe->njhe', rounded.astype(jnp.float32), grad_out.astype(jnp.float32)).astype(jnp.bfloat16)
    grad_weights = jnp.einsum('nihe,njhe->nhij', grad_out.astype(jnp.float32), value_win.astype(jnp.float32))
    grad_scores = weights * (grad_weights - lax.optimization_barrier(jnp.sum(weights * grad_weights, axis=-1, keepdims=True)))
    score_round = (grad_scores * score_scale).astype(jnp.bfloat16)
    grad_queries = jnp.einsum('nhij,njhe->nihe', score_round.astype(jnp.float32), key_win.astype(jnp.float32)).astype(jnp.bfloat16)
    grad_keys = jnp.einsum('nhij,nihe->njhe', score_round.astype(jnp.float32), queries.astype(jnp.float32)).astype(jnp.bfloat16)
    return (grad_queries, grad_keys, grad_values)

def reference(tokens, shift, w_qkv, w_proj, ln_gain, w_dec, prediction, target, legendre):
    fourier = fourier_basis(MODES)
    pred_field = prediction.astype(jnp.float32)

    def total_loss(field_values):
        return spectral_loss(field_values, target, legendre, fourier)[0]
    amse = spectral_loss(pred_field, target, legendre, fourier)[1]
    field_grad = jax.grad(total_loss)(pred_field) * (LAT * LON)
    grad_round = field_grad.astype(jnp.bfloat16)
    row_count, col_count = (tokens.shape[0], tokens.shape[1])
    grad_tiles = grad_round.reshape(VARS, row_count, 4, col_count, 4)
    token_grad = jnp.einsum('vrato,vaod->rtd', grad_tiles.astype(jnp.float32), w_dec.astype(jnp.float32))
    offset = shift[0]
    rolled_grad = jnp.roll(token_grad, -offset, axis=1)
    normed, inv_std, norm_out = norm_parts(jnp.roll(tokens, -offset, axis=1), ln_gain)
    projected = jnp.einsum('rtd,dkhe->rtkhe', norm_out.astype(jnp.float32), w_qkv.astype(jnp.float32)).astype(jnp.bfloat16)
    grad_out = jnp.einsum('rtd,hed->rthe', rolled_grad, w_proj.astype(jnp.float32), precision=HIGHEST).astype(jnp.bfloat16)
    grad_queries, grad_keys, grad_values = window_backward(to_windows(projected[:, :, 0]), to_windows(projected[:, :, 1]), to_windows(projected[:, :, 2]), to_windows(grad_out))
    stacked = jnp.stack([from_windows(grad_queries, row_count, col_count), from_windows(grad_keys, row_count, col_count), from_windows(grad_values, row_count, col_count)], axis=2)
    grad_normed = jnp.einsum('rtkhe,dkhe->rtd', stacked.astype(jnp.float32), w_qkv.astype(jnp.float32))
    summed = rolled_grad + norm_backward(grad_normed, normed, inv_std, ln_gain)
    input_grad = jnp.roll(summed, offset, axis=1).astype(jnp.bfloat16)
    return (amse, field_grad, input_grad)
```

```python
import functools
import math

import jax
import jax.numpy as jnp
import numpy as np
from jax import lax
from jax.experimental import pallas as pl
from jax.experimental.pallas import tpu as pltpu
from jax.sharding import PartitionSpec as P

HEAD = 96
VARS = 64
LON = 1440
LDEG = 384
WR = 2
WC = 12

EPSILON = 1e-06
NORM_EPSILON = 1e-05
HIGHEST = lax.Precision.HIGHEST
MESH = pl.DeviceIdType.MESH
F32 = jnp.float32
BF16 = jnp.bfloat16
VMEM = pl.BlockSpec(memory_space=pltpu.VMEM)
NT = (((1,), (1,)), ((), ()))


def fourier_basis(mode_count):
    column = np.arange(LON, dtype=np.int64)
    wavenumber = np.arange(mode_count, dtype=np.int64)
    phase = (column[:, None] * wavenumber[None, :] % LON) * (2.0 * math.pi / LON)
    return np.stack([np.cos(phase), -np.sin(phase)]) / math.sqrt(LON)


def amse_terms(power_pred, power_true, crossed):
    amp_pred = jnp.sqrt(power_pred + EPSILON)
    amp_true = jnp.sqrt(power_true + EPSILON)
    return (amp_pred - amp_true) ** 2 + 2.0 * jnp.maximum(power_pred, power_true) * (
        1.0 - crossed / (amp_pred * amp_true)
    )


def place(axis, index, sizes):
    proc, loss, var = (lax.axis_index(name) for name in ("proc", "loss", "vars"))
    if axis == "proc":
        return (index, loss, var)
    if axis == "loss":
        return (proc, index, var)
    if axis == "vars":
        return (proc, loss, index)
    return (proc, index // sizes["vars"], lax.rem(index, sizes["vars"]))


def rank(axis, sizes):
    if axis == "group":
        return lax.axis_index("loss") * sizes["vars"] + lax.axis_index("vars")
    return lax.axis_index(axis)


def greet(pairs):
    barrier = pltpu.get_barrier_semaphore()
    for device in pairs:
        pl.semaphore_signal(barrier, inc=1, device_id=device, device_id_type=MESH)
    pl.semaphore_wait(barrier, len(pairs))


def exchange_kernel(axis, count, sizes, spread, x_ref, out_ref, send, recv, own):
    me = rank(axis, sizes)
    peers = [lax.rem(me + k, count) for k in range(1, count)]
    greet([place(axis, peer, sizes) for peer in peers])
    copies = []
    for k, peer in enumerate(peers):
        copies.append(
            pltpu.make_async_remote_copy(
                src_ref=x_ref if spread else x_ref.at[peer],
                dst_ref=out_ref.at[k + 1] if spread else out_ref.at[me],
                send_sem=send.at[k],
                recv_sem=recv.at[k],
                device_id=place(axis, peer, sizes),
                device_id_type=MESH,
            )
        )
        copies[-1].start()
    if spread:
        local = pltpu.make_async_copy(x_ref, out_ref.at[0], own)
    else:
        local = pltpu.make_async_copy(x_ref.at[me], out_ref.at[me], own)
    local.start()
    local.wait()
    for copy in copies:
        copy.wait()


def exchange(x, axis, sizes, collective_id, spread=False):
    count = sizes["loss"] * sizes["vars"] if axis == "group" else sizes[axis]
    shape = (count,) + x.shape if spread else x.shape
    return pl.pallas_call(
        functools.partial(exchange_kernel, axis, count, sizes, spread),
        out_shape=jax.ShapeDtypeStruct(shape, x.dtype),
        in_specs=[VMEM],
        out_specs=VMEM,
        scratch_shapes=[
            pltpu.SemaphoreType.DMA((count - 1,)),
            pltpu.SemaphoreType.DMA((count - 1,)),
            pltpu.SemaphoreType.DMA,
        ],
        compiler_params=pltpu.CompilerParams(
            collective_id=collective_id, has_side_effects=True
        ),
        name="exchange_%d" % collective_id,
    )(x)


def harmonics_kernel(modes, var_count, spectra_ref, legendre_ref, harm_ref, power_ref):
    half = 2 * var_count
    sums = [jnp.zeros((half, LDEG), F32) for _ in range(3)]
    for m in range(modes):
        harm = jnp.dot(
            spectra_ref[m], legendre_ref[m], precision=HIGHEST, preferred_element_type=F32
        )
        harm_ref[m] = harm
        pred, true = harm[:half], harm[half:]
        sums = [sums[0] + pred * pred, sums[1] + true * true, sums[2] + pred * true]
    for i in range(3):
        power_ref[i] = sums[i][:var_count] + sums[i][var_count:]


def harmonics(spectra, legendre):
    modes, rows, _ = spectra.shape
    var_count = rows // 4
    return pl.pallas_call(
        functools.partial(harmonics_kernel, modes, var_count),
        out_shape=(
            jax.ShapeDtypeStruct((modes, rows, LDEG), F32),
            jax.ShapeDtypeStruct((3, var_count, LDEG), F32),
        ),
        in_specs=[VMEM, VMEM],
        out_specs=(VMEM, VMEM),
        name="harmonics",
    )(spectra, legendre)


def spectral_kernel(
    modes,
    sizes,
    var_count,
    weight,
    spectra_ref,
    legendre_ref,
    terms_ref,
    banded_ref,
    coeff_ref,
    harm,
    power,
    parts,
    acc,
    rows,
    outgoing,
    narrow,
    sa,
    ra,
    sb,
    rb,
    sc,
    rc,
    sd,
    rd,
):
    procs = sizes["proc"]
    group_count = sizes["loss"] * sizes["vars"]
    me, team = rank("proc", sizes), rank("group", sizes)
    peers = [lax.rem(me + k, procs) for k in range(1, procs)]
    mates = [lax.rem(team + k, group_count) for k in range(1, group_count)]
    greet(
        [place("proc", peer, sizes) for peer in peers]
        + [place("group", mate, sizes) for mate in mates]
    )
    half = 2 * var_count
    each = var_count // procs

    def copy(src, dst, send, recv, device):
        return pltpu.make_async_remote_copy(
            src_ref=src,
            dst_ref=dst,
            send_sem=send,
            recv_sem=recv,
            device_id=device,
            device_id_type=MESH,
        )

    sums = [jnp.zeros((half, LDEG), F32) for _ in range(3)]
    for m in range(modes):
        value = jnp.dot(
            spectra_ref[m], legendre_ref[m], precision=HIGHEST, preferred_element_type=F32
        )
        harm[m] = value
        pred, true = value[:half], value[half:]
        sums = [sums[0] + pred * pred, sums[1] + true * true, sums[2] + pred * true]
    for i in range(3):
        total = sums[i][:var_count] + sums[i][var_count:]
        for p in range(procs):
            power[p, i * each : (i + 1) * each] = total[p * each : (p + 1) * each]

    sent = [
        copy(power.at[peer], parts.at[k], sa.at[k], ra.at[k], place("proc", peer, sizes))
        for k, peer in enumerate(peers)
    ]
    for made in sent:
        made.start()
    for made in sent:
        made.wait()
    total = power[me]
    for k in range(procs - 1):
        total = total + parts[k]
    powers = [total[i * each : (i + 1) * each] for i in range(3)]
    terms, pullback = jax.vjp(amse_terms, *powers)
    grad_pred, _, grad_cross = pullback(jnp.full((each, LDEG), weight, F32))
    acc[...] = jnp.concatenate([2.0 * grad_pred, grad_cross, terms], axis=0)
    terms_ref[me] = acc[...]
    sent = [
        copy(acc, terms_ref.at[me], sb.at[k], rb.at[k], place("proc", peer, sizes))
        for k, peer in enumerate(peers)
    ]
    for made in sent:
        made.start()
    for made in sent:
        made.wait()
    gp = jnp.concatenate([terms_ref[p, :each] for p in range(procs)] * 2, axis=0)
    gc = jnp.concatenate([terms_ref[p, each : 2 * each] for p in range(procs)] * 2, axis=0)

    lats = legendre_ref.shape[1]
    own = lats // procs
    for m in range(modes):
        value = harm[m]
        grad = gp * value[:half] + gc * value[half:]
        rows[m * half : (m + 1) * half, :lats] = lax.dot_general(
            grad, legendre_ref[m], NT, precision=HIGHEST, preferred_element_type=F32
        )
    by_var = [rows[pl.ds(v, 2 * modes, stride=var_count), :] for v in range(var_count)]
    for q in range(procs):
        outgoing[q] = jnp.concatenate(
            [
                by_var[v][:, q * own + 4 * r : q * own + 4 * r + 4]
                for r in range(own // 4)
                for v in range(var_count)
            ],
            axis=1,
        )
    sent = [
        copy(outgoing.at[peer], banded_ref.at[me], sc.at[k], rc.at[k], place("proc", peer, sizes))
        for k, peer in enumerate(peers)
    ]
    for made in sent:
        made.start()
    banded_ref[me] = outgoing[me]

    passed = []
    for k in range(procs):
        source = lax.rem(me + procs - k, procs)
        if k > 0:
            sent[k - 1].wait_recv()
        value = banded_ref[source].astype(BF16)
        narrow[source] = value
        coeff_ref[0, source] = value
        for j, mate in enumerate(mates):
            passed.append(
                copy(
                    narrow.at[source],
                    coeff_ref.at[j + 1, source],
                    sd.at[k, j],
                    rd.at[k, j],
                    place("group", mate, sizes),
                )
            )
            passed[-1].start()
    for made in sent:
        made.wait_send()
    for made in passed:
        made.wait()


def spectral(spectra, legendre, sizes, weight, collective_id):
    procs = sizes["proc"]
    group_count = sizes["loss"] * sizes["vars"]
    modes, rows, lats = spectra.shape
    var_count = rows // 4
    each = var_count // procs
    block = (procs, 2 * modes, var_count * lats // procs)
    dma = pltpu.SemaphoreType.DMA
    return pl.pallas_call(
        functools.partial(spectral_kernel, modes, sizes, var_count, weight),
        out_shape=(
            jax.ShapeDtypeStruct((procs, 3 * each, LDEG), F32),
            jax.ShapeDtypeStruct(block, F32),
            jax.ShapeDtypeStruct((group_count,) + block, BF16),
        ),
        in_specs=[VMEM, VMEM],
        out_specs=(VMEM, VMEM, VMEM),
        scratch_shapes=[
            pltpu.VMEM((modes, rows, LDEG), F32),
            pltpu.VMEM((procs, 3 * each, LDEG), F32),
            pltpu.VMEM((procs - 1, 3 * each, LDEG), F32),
            pltpu.VMEM((3 * each, LDEG), F32),
            pltpu.VMEM((2 * modes * var_count, pl.cdiv(lats, 128) * 128), F32),
            pltpu.VMEM(block, F32),
            pltpu.VMEM(block, BF16),
        ]
        + [dma((procs - 1,)) for _ in range(6)]
        + [dma((procs, group_count - 1)) for _ in range(2)],
        compiler_params=pltpu.CompilerParams(
            collective_id=collective_id, has_side_effects=True
        ),
        name="spectral",
    )(spectra, legendre)


def attention_kernel(
    heads,
    cols,
    blocks,
    sizes,
    f_ref,
    coeff_ref,
    mix_ref,
    proj_ref,
    tok_ref,
    gain_ref,
    w_ref,
    out_ref,
    part,
    kept,
    got,
    mid,
    far,
    s1,
    r1,
    s2,
    r2,
):
    loss_count, var_count = sizes["loss"], sizes["vars"]
    loss, var = lax.axis_index("loss"), lax.axis_index("vars")
    near = [lax.rem(var + k, var_count) for k in range(1, var_count)]
    away = [lax.rem(loss + k, loss_count) for k in range(1, loss_count)]
    step = pl.program_id(0)
    rows = WR * cols

    @pl.when(step == 0)
    def _():
        greet(
            [place("vars", peer, sizes) for peer in near]
            + [place("loss", peer, sizes) for peer in away]
        )

    def near_copies(b):
        return [
            pltpu.make_async_remote_copy(
                src_ref=part.at[b, peer],
                dst_ref=got.at[b, k],
                send_sem=s1.at[b, k],
                recv_sem=r1.at[b, k],
                device_id=place("vars", peer, sizes),
                device_id_type=MESH,
            )
            for k, peer in enumerate(near)
        ]

    def away_copies(b):
        return [
            pltpu.make_async_remote_copy(
                src_ref=mid.at[b, peer],
                dst_ref=far.at[b, k],
                send_sem=s2.at[b, k],
                recv_sem=r2.at[b, k],
                device_id=place("loss", peer, sizes),
                device_id_type=MESH,
            )
            for k, peer in enumerate(away)
        ]

    def pass_on(b):
        for made in near_copies(b):
            made.wait()
        for j in range(loss_count):
            value = part[b, var, j].astype(F32)
            for k in range(var_count - 1):
                value = value + got[b, k, j].astype(F32)
            mid[b, j] = value.astype(BF16)
        for made in away_copies(b):
            made.start()

    pieces = []
    for o in range(4):
        y = jnp.dot(f_ref[o], coeff_ref[0], preferred_element_type=F32)
        half = y.shape[1] // WR
        pieces.append(
            jnp.concatenate([y[:, r * half : (r + 1) * half] for r in range(WR)], axis=0).astype(BF16)
        )
    tiles = jnp.concatenate(pieces, axis=1)
    mixed = jnp.dot(tiles, mix_ref[...], preferred_element_type=F32)
    width = heads * HEAD
    grad_out = mixed[:, :width].astype(BF16)
    kept[step] = mixed[:, width:]

    window_i = lax.rem(lax.broadcasted_iota(jnp.int32, (rows, rows), 0), cols) // WC
    window_j = lax.rem(lax.broadcasted_iota(jnp.int32, (rows, rows), 1), cols) // WC
    same = window_i == window_j
    scale = HEAD ** (-0.5)
    grads = [[], [], []]
    for h in range(heads):
        q, k, v = (
            proj_ref[0, :, (i * heads + h) * HEAD : (i * heads + h + 1) * HEAD] for i in range(3)
        )
        go = grad_out[:, h * HEAD : (h + 1) * HEAD]
        scores = lax.dot_general(q, k, NT, preferred_element_type=F32) * scale
        weights = jnp.where(same, jnp.exp(scores), 0.0)
        weights = weights / jnp.sum(weights, axis=-1, keepdims=True)
        rounded = weights.astype(BF16)
        first = (((0,), (0,)), ((), ()))
        grads[2].append(
            lax.dot_general(rounded, go, first, preferred_element_type=F32).astype(BF16)
        )
        grad_weights = lax.dot_general(go, v, NT, preferred_element_type=F32)
        inner = jnp.sum(weights * grad_weights, axis=-1, keepdims=True)
        score_round = (weights * (grad_weights - inner) * scale).astype(BF16)
        grads[0].append(jnp.dot(score_round, k, preferred_element_type=F32).astype(BF16))
        grads[1].append(
            lax.dot_general(score_round, q, first, preferred_element_type=F32).astype(BF16)
        )
    stacked = jnp.concatenate(grads[0] + grads[1] + grads[2], axis=1)
    grad_normed = lax.dot_general(stacked, w_ref[...], NT, preferred_element_type=F32)

    values = tok_ref[0].astype(F32)
    centred = values - jnp.mean(values, axis=-1, keepdims=True)
    inv_std = lax.rsqrt(jnp.mean(centred * centred, axis=-1, keepdims=True) + NORM_EPSILON)
    normed = centred * inv_std
    scaled = grad_normed * gain_ref[...]
    local = inv_std * (
        scaled
        - jnp.mean(scaled, axis=-1, keepdims=True)
        - normed * jnp.mean(scaled * normed, axis=-1, keepdims=True)
    )
    local = local.astype(BF16)
    share = local.shape[1] // (loss_count * var_count)
    for l in range(loss_count):
        for v in range(var_count):
            at = (l * var_count + v) * share
            part[step, v, l] = local[:, at : at + share]
    for made in near_copies(step):
        made.start()

    @pl.when(step > 0)
    def _():
        pass_on(step - 1)

    @pl.when(step == blocks - 1)
    def _():
        pass_on(blocks - 1)
        for b in range(blocks):
            for made in away_copies(b):
                made.wait()
            value = kept[b] + mid[b, loss].astype(F32)
            for k in range(loss_count - 1):
                value = value + far[b, k].astype(F32)
            out_ref[b] = value.astype(BF16)


def attention_backward(f_rolled, coeff, mix, projected, tokens, gain, w_flat, sizes, collective_id):
    blocks, rows, model = tokens.shape
    pairs = coeff.shape[0]
    cols = rows // WR
    per_pair = blocks // pairs
    depth = f_rolled.shape[2]
    width = projected.shape[2] // 3
    heads = width // HEAD
    loss_count, var_count = sizes["loss"], sizes["vars"]
    share = model // (loss_count * var_count)

    def whole(shape):
        return pl.BlockSpec(shape, lambda b: (0,) * len(shape))

    def per_block(shape):
        return pl.BlockSpec((1,) + shape, lambda b: (b,) + (0,) * len(shape))

    return pl.pallas_call(
        functools.partial(attention_kernel, heads, cols, blocks, sizes),
        grid=(blocks,),
        in_specs=[
            pl.BlockSpec((4, cols, depth), lambda b: (0, lax.rem(b, per_pair), 0)),
            pl.BlockSpec((1,) + coeff.shape[1:], lambda b: (b // per_pair, 0, 0)),
            whole(mix.shape),
            per_block((rows, 3 * width)),
            per_block((rows, model)),
            whole(gain.shape),
            whole(w_flat.shape),
        ],
        out_specs=whole((blocks, rows, share)),
        out_shape=jax.ShapeDtypeStruct((blocks, rows, share), BF16),
        scratch_shapes=[
            pltpu.VMEM((blocks, var_count, loss_count, rows, share), BF16),
            pltpu.VMEM((blocks, rows, share), F32),
            pltpu.VMEM((blocks, var_count - 1, loss_count, rows, share), BF16),
            pltpu.VMEM((blocks, loss_count, rows, share), BF16),
            pltpu.VMEM((blocks, loss_count - 1, rows, share), BF16),
            pltpu.SemaphoreType.DMA((blocks, var_count - 1)),
            pltpu.SemaphoreType.DMA((blocks, var_count - 1)),
            pltpu.SemaphoreType.DMA((blocks, loss_count - 1)),
            pltpu.SemaphoreType.DMA((blocks, loss_count - 1)),
        ],
        compiler_params=pltpu.CompilerParams(
            collective_id=collective_id, has_side_effects=True
        ),
        name="attention_backward",
    )(f_rolled, coeff, mix, projected, tokens, gain, w_flat)


def body_general(tokens, shift, w_qkv, w_proj, ln_gain, w_dec, prediction, target, legendre):
    sizes = {name: lax.axis_size(name) for name in ("proc", "loss", "vars")}
    procs = sizes["proc"]
    groups = (sizes["loss"], sizes["vars"])
    group_count = groups[0] * groups[1]
    modes = legendre.shape[0]
    lat_all = legendre.shape[1]
    modes_all = modes * procs
    var_count, lats = prediction.shape[0], prediction.shape[1]
    basis = fourier_basis(modes_all)
    row_count, col_count, model = tokens.shape
    offset = shift[0]
    head_local = w_qkv.shape[2]
    width = head_local * HEAD
    share = model // group_count

    ordered = basis.transpose(2, 0, 1).reshape(-1, LON)
    to_modes = jnp.asarray(ordered, F32)
    fields = jnp.concatenate([prediction.astype(F32), target]).reshape(-1, LON)
    spectra = lax.dot_general(to_modes, fields, NT, precision=HIGHEST)
    at_owner = exchange(spectra.reshape(procs, 2 * modes, -1), "proc", sizes, 1)
    at_owner = at_owner.reshape(procs, modes, 2, 2, var_count, lats).transpose(1, 3, 2, 4, 0, 5)
    at_owner = at_owner.reshape(modes, 4 * var_count, lat_all)
    weight_grad = lat_all * LON / (VARS * LDEG * modes_all)
    if var_count % procs == 0:
        terms, banded, coeff = spectral(at_owner, legendre, sizes, weight_grad, 2)
        each = var_count // procs
        degree_terms = terms[:, 2 * each :].reshape(var_count, LDEG)
    else:
        harm, power = harmonics(at_owner, legendre)
        power = lax.psum(power, "proc")
        degree_terms, pullback = jax.vjp(amse_terms, power[0], power[1], power[2])
        grad_pred, _, grad_cross = pullback(jnp.full(degree_terms.shape, weight_grad, F32))
        harm = harm.reshape(modes, 2, 2, var_count, LDEG)
        grad_harm = 2.0 * grad_pred * harm[:, 0] + grad_cross * harm[:, 1]
        grad_spectra = jnp.einsum("mcvl,mal->mcva", grad_harm, legendre, precision=HIGHEST)
        grad_spectra = grad_spectra.reshape(modes, 2, var_count, procs, lats // 4, 4)
        grad_spectra = grad_spectra.transpose(3, 0, 1, 4, 2, 5).reshape(procs, 2 * modes, -1)
        banded = exchange(grad_spectra, "proc", sizes, 3)
        coeff = exchange(banded.astype(BF16), "group", sizes, 4, spread=True)
    amse = jnp.sum(degree_terms, axis=-1) / (LDEG * modes_all)
    pairs = row_count // WR
    banded = banded.reshape(2 * modes_all, row_count, var_count, 4).transpose(0, 2, 1, 3)
    coeff = coeff.reshape(group_count, 2 * modes_all, pairs, WR, 4 * var_count)
    coeff = coeff.transpose(2, 1, 3, 0, 4).reshape(pairs, 2 * modes_all, -1)

    field_grad = lax.dot_general(
        banded.reshape(2 * modes_all, -1),
        to_modes,
        (((0,), (0,)), ((), ())),
        precision=HIGHEST,
    ).reshape(var_count, lats, LON)

    decoder = w_dec.transpose(2, 0, 1, 3).reshape(4 * var_count * 4, model)
    through = lax.dot_general(
        decoder, w_proj.reshape(-1, model), NT, preferred_element_type=F32
    ).astype(BF16)
    mix = jnp.concatenate(
        [
            through.reshape(-1, group_count, width),
            decoder.reshape(-1, group_count, share),
        ],
        axis=2,
    ).transpose(1, 0, 2)
    me = rank("group", sizes)
    received = [lax.dynamic_index_in_dim(mix, me, 0, keepdims=False)]
    for k in range(1, group_count):
        block = lax.dynamic_index_in_dim(mix, lax.rem(me + k, group_count), 0, keepdims=False)
        ring = [(g, (g + k) % group_count) for g in range(group_count)]
        received.append(lax.ppermute(block, ("loss", "vars"), ring))
    mix = jnp.stack(received)
    mix = mix.reshape(group_count, 4, 4 * var_count, width + share).transpose(1, 0, 2, 3)
    mix = mix.reshape(-1, width + share)

    cols = 120
    split = (pairs, WR, col_count // cols, cols)
    rolled = jnp.roll(tokens, -offset, axis=1)
    rolled = rolled.reshape(split + (model,)).transpose(0, 2, 1, 3, 4)
    rolled = rolled.reshape(-1, WR * cols, model)
    values = rolled.astype(F32)
    centred = values - jnp.mean(values, axis=-1, keepdims=True)
    inv_std = lax.rsqrt(jnp.mean(centred * centred, axis=-1, keepdims=True) + NORM_EPSILON)
    norm_out = (centred * inv_std * ln_gain).astype(BF16)
    w_flat = w_qkv.reshape(model, 3 * width)
    projected = jnp.einsum(
        "brd,dk->brk", norm_out, w_flat, preferred_element_type=F32
    ).astype(BF16)
    by_column = jnp.asarray(ordered.T.reshape(col_count, 4, -1).transpose(1, 0, 2), BF16)
    f_rolled = jnp.roll(by_column, -offset, axis=1)
    summed = attention_backward(
        f_rolled, coeff, mix, projected, rolled, ln_gain.reshape(1, model), w_flat, sizes, 6
    )
    summed = summed.reshape(pairs, col_count // cols, WR, cols, share).transpose(0, 2, 1, 3, 4)
    input_grad = jnp.roll(summed.reshape(row_count, col_count, share), offset, axis=1)
    return (amse, field_grad, input_grad)


def spread_kernel(
    sizes,
    dims,
    weight,
    shift_ref,
    pred_hbm,
    target_hbm,
    basis_hbm,
    legendre_hbm,
    dec_hbm,
    wproj_hbm,
    tok_hbm,
    gain_hbm,
    w_hbm,
    fg_ref,
    amse_ref,
    coeff_ref,
    mix_ref,
    proj_ref,
    rolled_ref,
    pred_in,
    target_in,
    basis,
    legendre_in,
    dec_in,
    wproj,
    tok_in,
    gain,
    w_in,
    y_out,
    y_in,
    x_wide,
    leg,
    harm,
    power,
    parts,
    acc,
    terms_in,
    g_wide,
    g_out,
    mix_out,
    wide,
    norm_out,
    loads,
    sy,
    ry,
    sa,
    ra,
    sb,
    rb,
    sc,
    rc,
    sd,
    rd,
    sm,
    rm,
):
    procs, modes, var_count, lats = dims["procs"], dims["modes"], dims["vars"], dims["lats"]
    group_count = sizes["loss"] * sizes["vars"]
    lat_all = procs * lats
    each = var_count // procs
    half = 2 * var_count
    fold = 128 // half
    strips = lats // fold
    me, team = rank("proc", sizes), rank("group", sizes)
    peers = [lax.rem(me + k, procs) for k in range(1, procs)]
    mates = [lax.rem(team + k, group_count) for k in range(1, group_count)]
    barrier = pltpu.get_barrier_semaphore()
    places = [place("proc", peer, sizes) for peer in peers]
    mate_places = [place("group", mate, sizes) for mate in mates]
    for device in places + mate_places:
        pl.semaphore_signal(barrier, inc=1, device_id=device, device_id_type=MESH)

    pairs_in = [
        (pred_hbm, pred_in),
        (target_hbm, target_in),
        (basis_hbm, basis),
        (dec_hbm, dec_in),
        (wproj_hbm, wproj),
        (legendre_hbm, legendre_in),
        (tok_hbm, tok_in),
        (gain_hbm, gain),
        (w_hbm, w_in),
    ]
    load = [
        pltpu.make_async_copy(src, dst, loads.at[i]) for i, (src, dst) in enumerate(pairs_in)
    ]
    for made in load:
        made.start()

    def copy(src, dst, send, recv, device):
        return pltpu.make_async_remote_copy(
            src_ref=src,
            dst_ref=dst,
            send_sem=send,
            recv_sem=recv,
            device_id=device,
            device_id_type=MESH,
        )

    def permutation(count, source):
        i = lax.broadcasted_iota(jnp.int32, (count, count), 0)
        j = lax.broadcasted_iota(jnp.int32, (count, count), 1)
        return jnp.where(i == source(j), 1.0, 0.0).astype(BF16)

    load[0].wait()
    load[1].wait()
    load[2].wait()
    both = [pred_in[...], target_in[...].astype(BF16)]
    y = [
        lax.dot_general(basis[0], field, NT, preferred_element_type=F32)
        + lax.dot_general(basis[1], field, NT, preferred_element_type=F32)
        for field in both
    ]
    y = jnp.concatenate(y, axis=1).astype(BF16)
    by_lat = permutation(lats * half, lambda j: lax.rem(j, half) * lats + j // half)
    y = jnp.dot(y, by_lat, preferred_element_type=F32)
    for p in range(procs):
        y_out[p] = y[p * 2 * modes : (p + 1) * 2 * modes].astype(BF16)
    pl.semaphore_wait(barrier, procs + group_count - 2)
    sent_y = [
        copy(y_out.at[peer], y_in.at[me], sy.at[k], ry.at[k], places[k])
        for k, peer in enumerate(peers)
    ]
    for made in sent_y:
        made.start()
    y_in[me] = y_out[me]

    load[3].wait()
    count = dec_in.shape[0]
    i = lax.broadcasted_iota(jnp.int32, (count, count), 0)
    j = lax.broadcasted_iota(jnp.int32, (count, count), 1)
    o, a, v = i // (4 * var_count), lax.rem(i // var_count, 4), lax.rem(i, var_count)
    order = jnp.where(j == v * 16 + a * 4 + o, 1.0, 0.0).astype(BF16)
    decoder = jnp.dot(order, dec_in[...], preferred_element_type=F32).astype(BF16)
    load[4].wait()
    share = decoder.shape[1] // group_count
    width = wproj.shape[0] // group_count
    for g in range(group_count):
        through = lax.dot_general(
            decoder, wproj[g * width : (g + 1) * width], NT, preferred_element_type=F32
        ).astype(BF16)
        for o in range(4):
            at = o * 4 * var_count
            mix_out[g, o, :, :width] = through[at : at + 4 * var_count]
            mix_out[g, o, :, width:] = decoder[
                at : at + 4 * var_count, g * share : (g + 1) * share
            ]
    sent_mix = [
        copy(mix_out.at[mate], mix_ref.at[:, k + 1], sm.at[k], rm.at[k], mate_places[k])
        for k, mate in enumerate(mates)
    ]
    for made in sent_mix:
        made.start()
    for o in range(4):
        mix_ref[o, 0] = mix_out[team, o]

    load[5].wait()
    i = lax.broadcasted_iota(jnp.int32, (lat_all, lat_all), 0)
    j = lax.broadcasted_iota(jnp.int32, (lat_all, lat_all), 1)
    tall = lat_all // fold
    by_fold = jnp.where(j == lax.rem(i, tall) * fold + i // tall, 1.0, 0.0).astype(BF16)
    for m in range(modes):
        leg[m] = jnp.dot(
            by_fold, legendre_in[m].astype(BF16), preferred_element_type=F32
        ).astype(BF16)

    row_count, col_count = tok_in.shape[0], tok_in.shape[1]
    offset = lax.rem(shift_ref[0], col_count)
    load[6].wait()
    load[7].wait()
    load[8].wait()
    cols = proj_ref.shape[1] // WR

    def roll(b):
        i = lax.broadcasted_iota(jnp.int32, (cols, col_count), 0) + (b * cols + offset)
        j = lax.broadcasted_iota(jnp.int32, (cols, col_count), 1)
        pick = jnp.where((i == j) | (i == j + col_count), 1.0, 0.0).astype(BF16)
        for r in range(row_count):
            wide[b, r * cols : (r + 1) * cols] = jnp.dot(
                pick, tok_in[r], preferred_element_type=F32
            )

    def normalise(b):
        step = 48
        for at in range(0, WR * cols, step):
            rows = slice(at, at + step)
            values = wide[b, rows]
            rolled_ref[b, rows] = values.astype(BF16)
            centred = values - jnp.mean(values, axis=-1, keepdims=True)
            inv_std = lax.rsqrt(
                jnp.mean(centred * centred, axis=-1, keepdims=True) + NORM_EPSILON
            )
            norm_out[b, rows] = (centred * inv_std * gain[...]).astype(BF16)

    def project(b):
        proj_ref[b] = lax.dot_general(
            norm_out[b], w_in[...], NT, preferred_element_type=F32
        ).astype(BF16)

    blocks = proj_ref.shape[0]
    for b in range(blocks):
        roll(b)
        normalise(b)

    for made in sent_y:
        made.wait()
    for p in range(procs):
        for h in range(strips):
            at = (p * strips + h) * 2 * modes
            x_wide[at : at + 2 * modes] = y_in[p, :, h * 128 : (h + 1) * 128].astype(F32)
    power_sums = [jnp.zeros((var_count, LDEG), F32) for _ in range(3)]
    for m in range(modes):
        z = [
            x_wide[pl.ds(c * modes + m, tall, stride=2 * modes), :] for c in range(2)
        ]
        x = jnp.concatenate(
            [
                jnp.concatenate([z[c][:, f * half : (f + 1) * half] for c in range(2)], axis=1)
                for f in range(fold)
            ],
            axis=0,
        ).astype(BF16)
        value = lax.dot_general(
            x, leg[m], (((0,), (0,)), ((), ())), preferred_element_type=F32
        )
        harm[m] = value
        for c in range(2):
            pred = value[c * half : c * half + var_count]
            true = value[c * half + var_count : (c + 1) * half]
            power_sums = [
                power_sums[0] + pred * pred,
                power_sums[1] + true * true,
                power_sums[2] + pred * true,
            ]
    for i in range(3):
        for p in range(procs):
            power[p, i * each : (i + 1) * each] = power_sums[i][p * each : (p + 1) * each]
    sent = [
        copy(power.at[peer], parts.at[k], sa.at[k], ra.at[k], places[k])
        for k, peer in enumerate(peers)
    ]
    for made in sent:
        made.start()
    project(0)
    for made in sent:
        made.wait()
    total = power[me]
    for k in range(procs - 1):
        total = total + parts[k]
    powers = [total[i * each : (i + 1) * each] for i in range(3)]
    terms, pullback = jax.vjp(amse_terms, *powers)
    grad_pred, _, grad_cross = pullback(jnp.full((each, LDEG), weight, F32))
    acc[...] = jnp.concatenate([2.0 * grad_pred, grad_cross, terms], axis=0)
    terms_in[me] = acc[...]
    sent = [
        copy(acc, terms_in.at[me], sb.at[k], rb.at[k], places[k])
        for k, peer in enumerate(peers)
    ]
    for made in sent:
        made.start()
    for b in range(1, blocks):
        project(b)
    for made in sent:
        made.wait()
    gp = jnp.concatenate([terms_in[p, :each] for p in range(procs)], axis=0)
    gc = jnp.concatenate([terms_in[p, each : 2 * each] for p in range(procs)], axis=0)

    for m in range(modes):
        value = harm[m]
        grad = jnp.concatenate(
            [
                gp * value[c * half : c * half + var_count]
                + gc * value[c * half + var_count : (c + 1) * half]
                for c in range(2)
            ],
            axis=0,
        ).astype(BF16)
        g_wide[m * lat_all : (m + 1) * lat_all, :half] = lax.dot_general(
            leg[m], grad, NT, preferred_element_type=F32
        )
    for q in range(procs):
        pieces = []
        for a in range(lats):
            at = (a % fold) * (lat_all // fold) + q * strips + a // fold
            pieces.append(g_wide[pl.ds(at, modes, stride=lat_all), :])
        g_out[q] = jnp.concatenate(
            [
                jnp.concatenate(
                    [piece[:, c * var_count : (c + 1) * var_count] for piece in pieces], axis=1
                )
                for c in range(2)
            ],
            axis=0,
        ).astype(BF16)
    sent = [
        copy(g_out.at[peer], coeff_ref.at[0, me], sc.at[k], rc.at[k], places[k])
        for k, peer in enumerate(peers)
    ]
    for made in sent:
        made.start()
    coeff_ref[0, me] = g_out[me]
    for p in range(procs):
        amse_ref[p * each : (p + 1) * each] = jnp.broadcast_to(
            jnp.sum(terms_in[p, 2 * each :], axis=-1, keepdims=True) / dims["terms"],
            (each, 128),
        )

    passed = []
    for k in range(procs):
        source = lax.rem(me + procs - k, procs)
        if k > 0:
            sent[k - 1].wait_recv()
        for j in range(group_count - 1):
            passed.append(
                copy(
                    coeff_ref.at[0, source],
                    coeff_ref.at[j + 1, source],
                    sd.at[k, j],
                    rd.at[k, j],
                    mate_places[j],
                )
            )
            passed[-1].start()
    own = jnp.concatenate([coeff_ref[0, p] for p in range(procs)], axis=0)
    by_var = permutation(lats * var_count, lambda j: lax.rem(j, lats) * var_count + j // lats)
    own = jnp.dot(own, by_var, preferred_element_type=F32).astype(BF16)
    first = (((0,), (0,)), ((), ()))
    grid = lax.dot_general(own, basis[0], first, preferred_element_type=F32)
    fg_ref[...] = grid + lax.dot_general(own, basis[1], first, preferred_element_type=F32)
    for made in sent:
        made.wait_send()
    for made in passed:
        made.wait()
    for made in sent_mix:
        made.wait()


def spread(shift, pred, target, basis, legendre, dec, wproj, tokens, gain, w, sizes, cols, weight, collective_id):
    procs = sizes["proc"]
    group_count = sizes["loss"] * sizes["vars"]
    modes, lat_all, _ = legendre.shape
    lats = lat_all // procs
    var_count = pred.shape[0] // lats
    each = var_count // procs
    half = 2 * var_count
    row_count, col_count, model = tokens.shape
    blocks = row_count // WR * col_count // cols
    width = wproj.shape[0] // group_count
    share = model // group_count
    dims = {
        "procs": procs,
        "modes": modes,
        "vars": var_count,
        "lats": lats,
        "terms": LDEG * modes * procs,
    }
    dma = pltpu.SemaphoreType.DMA
    ANY = pl.BlockSpec(memory_space=pl.ANY)
    return pl.pallas_call(
        functools.partial(spread_kernel, sizes, dims, weight),
        out_shape=(
            jax.ShapeDtypeStruct((var_count * lats, LON), F32),
            jax.ShapeDtypeStruct((var_count, 128), F32),
            jax.ShapeDtypeStruct((group_count, procs, 2 * modes, var_count * lats), BF16),
            jax.ShapeDtypeStruct((4, group_count, 4 * var_count, width + share), BF16),
            jax.ShapeDtypeStruct((blocks, WR * cols, w.shape[0]), BF16),
            jax.ShapeDtypeStruct((blocks, WR * cols, model), BF16),
        ),
        in_specs=[pl.BlockSpec(memory_space=pltpu.SMEM)] + [ANY] * 9,
        out_specs=(VMEM,) * 6,
        scratch_shapes=[
            pltpu.VMEM(pred.shape, pred.dtype),
            pltpu.VMEM(target.shape, target.dtype),
            pltpu.VMEM(basis.shape, basis.dtype),
            pltpu.VMEM(legendre.shape, legendre.dtype),
            pltpu.VMEM(dec.shape, dec.dtype),
            pltpu.VMEM(wproj.shape, wproj.dtype),
            pltpu.VMEM(tokens.shape, tokens.dtype),
            pltpu.VMEM(gain.shape, gain.dtype),
            pltpu.VMEM(w.shape, w.dtype),
            pltpu.VMEM((procs, 2 * modes, lats * half), BF16),
            pltpu.VMEM((procs, 2 * modes, lats * half), BF16),
            pltpu.VMEM((procs * lats * half // 128 * 2 * modes, 128), F32),
            pltpu.VMEM(legendre.shape, BF16),
            pltpu.VMEM((modes, 2 * half, LDEG), F32),
            pltpu.VMEM((procs, 3 * each, LDEG), F32),
            pltpu.VMEM((procs - 1, 3 * each, LDEG), F32),
            pltpu.VMEM((3 * each, LDEG), F32),
            pltpu.VMEM((procs, 3 * each, LDEG), F32),
            pltpu.VMEM((modes * lat_all, 128), F32),
            pltpu.VMEM((procs, 2 * modes, var_count * lats), BF16),
            pltpu.VMEM((group_count, 4, 4 * var_count, width + share), BF16),
            pltpu.VMEM((blocks, WR * cols, model), F32),
            pltpu.VMEM((blocks, WR * cols, model), BF16),
            dma((9,)),
        ]
        + [dma((procs - 1,)) for _ in range(8)]
        + [dma((procs, group_count - 1)) for _ in range(2)]
        + [dma((group_count - 1,)) for _ in range(2)],
        compiler_params=pltpu.CompilerParams(
            collective_id=collective_id,
            has_side_effects=True,
            vmem_limit_bytes=56 * 1024 * 1024,
        ),
        name="spread",
    )(shift, pred, target, basis, legendre, dec, wproj, tokens, gain, w)


def layer_kernel(
    heads,
    cols,
    blocks,
    sizes,
    f_ref,
    coeff_ref,
    mix_ref,
    proj_ref,
    tok_ref,
    gain_ref,
    w_ref,
    out_ref,
    part,
    kept,
    got,
    mid,
    far,
    by_row,
    s1,
    r1,
    s2,
    r2,
):
    loss_count, var_count = sizes["loss"], sizes["vars"]
    loss, var = lax.axis_index("loss"), lax.axis_index("vars")
    near = [lax.rem(var + k, var_count) for k in range(1, var_count)]
    away = [lax.rem(loss + k, loss_count) for k in range(1, loss_count)]
    step = pl.program_id(0)
    rows = WR * cols

    @pl.when(step == 0)
    def _():
        greet(
            [place("vars", peer, sizes) for peer in near]
            + [place("loss", peer, sizes) for peer in away]
        )
        groups, procs = coeff_ref.shape[0], coeff_ref.shape[1]
        deep, band = coeff_ref.shape[2], coeff_ref.shape[3] // WR
        for g in range(groups):
            for p in range(procs):
                for r in range(WR):
                    at = (r * groups + g) * band
                    by_row[p * deep : (p + 1) * deep, at : at + band] = coeff_ref[
                        g, p, :, r * band : (r + 1) * band
                    ]

    def near_copies(b):
        return [
            pltpu.make_async_remote_copy(
                src_ref=part.at[b, peer],
                dst_ref=got.at[b, k],
                send_sem=s1.at[b, k],
                recv_sem=r1.at[b, k],
                device_id=place("vars", peer, sizes),
                device_id_type=MESH,
            )
            for k, peer in enumerate(near)
        ]

    def away_copies(b):
        return [
            pltpu.make_async_remote_copy(
                src_ref=mid.at[b, peer],
                dst_ref=far.at[b, k],
                send_sem=s2.at[b, k],
                recv_sem=r2.at[b, k],
                device_id=place("loss", peer, sizes),
                device_id_type=MESH,
            )
            for k, peer in enumerate(away)
        ]

    def pass_on(b):
        for made in near_copies(b):
            made.wait()
        for j in range(loss_count):
            value = part[b, var, j].astype(F32)
            for k in range(var_count - 1):
                value = value + got[b, k, j].astype(F32)
            mid[b, j] = value.astype(BF16)
        for made in away_copies(b):
            made.start()

    pieces = []
    for o in range(4):
        y = jnp.dot(f_ref[o, 0], by_row[...], preferred_element_type=F32)
        half = y.shape[1] // WR
        pieces.append(
            jnp.concatenate([y[:, r * half : (r + 1) * half] for r in range(WR)], axis=0).astype(BF16)
        )
    tiles = jnp.concatenate(pieces, axis=1)
    mixed = jnp.dot(tiles, mix_ref[...], preferred_element_type=F32)
    width = heads * HEAD
    grad_out = mixed[:, :width].astype(BF16)
    kept[step] = mixed[:, width:]

    window_i = lax.rem(lax.broadcasted_iota(jnp.int32, (rows, rows), 0), cols) // WC
    window_j = lax.rem(lax.broadcasted_iota(jnp.int32, (rows, rows), 1), cols) // WC
    same = window_i == window_j
    scale = HEAD ** (-0.5)
    grads = [[], [], []]
    for h in range(heads):
        q, k, v = (
            proj_ref[0, :, (i * heads + h) * HEAD : (i * heads + h + 1) * HEAD] for i in range(3)
        )
        go = grad_out[:, h * HEAD : (h + 1) * HEAD]
        scores = lax.dot_general(q, k, NT, preferred_element_type=F32) * scale
        weights = jnp.where(same, jnp.exp(scores), 0.0)
        weights = weights / jnp.sum(weights, axis=-1, keepdims=True)
        rounded = weights.astype(BF16)
        first = (((0,), (0,)), ((), ()))
        grads[2].append(
            lax.dot_general(rounded, go, first, preferred_element_type=F32).astype(BF16)
        )
        grad_weights = lax.dot_general(go, v, NT, preferred_element_type=F32)
        inner = jnp.sum(weights * grad_weights, axis=-1, keepdims=True)
        score_round = (weights * (grad_weights - inner) * scale).astype(BF16)
        grads[0].append(jnp.dot(score_round, k, preferred_element_type=F32).astype(BF16))
        grads[1].append(
            lax.dot_general(score_round, q, first, preferred_element_type=F32).astype(BF16)
        )
    stacked = jnp.concatenate(grads[0] + grads[1] + grads[2], axis=1)
    grad_normed = jnp.dot(stacked, w_ref[...], preferred_element_type=F32)

    values = tok_ref[0].astype(F32)
    centred = values - jnp.mean(values, axis=-1, keepdims=True)
    inv_std = lax.rsqrt(jnp.mean(centred * centred, axis=-1, keepdims=True) + NORM_EPSILON)
    normed = centred * inv_std
    scaled = grad_normed * gain_ref[...]
    local = inv_std * (
        scaled
        - jnp.mean(scaled, axis=-1, keepdims=True)
        - normed * jnp.mean(scaled * normed, axis=-1, keepdims=True)
    )
    local = local.astype(BF16)
    share = local.shape[1] // (loss_count * var_count)
    for l in range(loss_count):
        for v in range(var_count):
            at = (l * var_count + v) * share
            part[step, v, l] = local[:, at : at + share]
    for made in near_copies(step):
        made.start()

    @pl.when(step > 0)
    def _():
        pass_on(step - 1)

    @pl.when(step == blocks - 1)
    def _():
        pass_on(blocks - 1)
        for b in range(blocks):
            for made in away_copies(b):
                made.wait()
            value = kept[b] + mid[b, loss].astype(F32)
            for k in range(loss_count - 1):
                value = value + far[b, k].astype(F32)
            out_ref[b] = value.astype(BF16)


def layer_backward(f_rolled, coeff, mix, projected, tokens, gain, w_flat, sizes, collective_id):
    blocks, rows, model = tokens.shape
    cols = rows // WR
    depth = f_rolled.shape[3]
    width = projected.shape[2] // 3
    heads = width // HEAD
    loss_count, var_count = sizes["loss"], sizes["vars"]
    share = model // (loss_count * var_count)

    def whole(shape):
        return pl.BlockSpec(shape, lambda b: (0,) * len(shape))

    def per_block(shape):
        return pl.BlockSpec((1,) + shape, lambda b: (b,) + (0,) * len(shape))

    return pl.pallas_call(
        functools.partial(layer_kernel, heads, cols, blocks, sizes),
        grid=(blocks,),
        in_specs=[
            pl.BlockSpec((4, 1, cols, depth), lambda b: (0, b, 0, 0)),
            whole(coeff.shape),
            whole(mix.shape),
            per_block((rows, 3 * width)),
            per_block((rows, model)),
            whole(gain.shape),
            whole(w_flat.shape),
        ],
        out_specs=whole((blocks, rows, share)),
        out_shape=jax.ShapeDtypeStruct((blocks, rows, share), BF16),
        scratch_shapes=[
            pltpu.VMEM((blocks, var_count, loss_count, rows, share), BF16),
            pltpu.VMEM((blocks, rows, share), F32),
            pltpu.VMEM((blocks, var_count - 1, loss_count, rows, share), BF16),
            pltpu.VMEM((blocks, loss_count, rows, share), BF16),
            pltpu.VMEM((blocks, loss_count - 1, rows, share), BF16),
            pltpu.VMEM((depth, math.prod(coeff.shape) // depth), BF16),
            pltpu.SemaphoreType.DMA((blocks, var_count - 1)),
            pltpu.SemaphoreType.DMA((blocks, var_count - 1)),
            pltpu.SemaphoreType.DMA((blocks, loss_count - 1)),
            pltpu.SemaphoreType.DMA((blocks, loss_count - 1)),
        ],
        compiler_params=pltpu.CompilerParams(
            collective_id=collective_id, has_side_effects=True
        ),
        name="layer_backward",
    )(f_rolled, coeff, mix, projected, tokens, gain, w_flat)


def body(tokens, shift, w_qkv, w_proj, ln_gain, w_dec, prediction, target, legendre):
    sizes = {name: lax.axis_size(name) for name in ("proc", "loss", "vars")}
    procs = sizes["proc"]
    group_count = sizes["loss"] * sizes["vars"]
    modes, lat_all, _ = legendre.shape
    var_count, lats = prediction.shape[0], prediction.shape[1]
    row_count, col_count, model = tokens.shape
    cols = 120
    fits = (
        row_count == WR
        and lats == 8
        and var_count == 16
        and modes == 16
        and lat_all == procs * lats
        and var_count % procs == 0
    )
    if not fits:
        return body_general(
            tokens, shift, w_qkv, w_proj, ln_gain, w_dec, prediction, target, legendre
        )
    modes_all = modes * procs
    offset = shift[0]
    width = w_qkv.shape[2] * HEAD
    share = model // group_count
    weight = lat_all * LON / (VARS * LDEG * modes_all)
    rows = fourier_basis(modes_all).transpose(0, 2, 1).reshape(2, procs, modes, LON)
    rows = rows.transpose(1, 0, 2, 3).reshape(2 * modes_all, LON).astype(np.float32)
    high = rows.astype(jnp.bfloat16)
    low = (rows - high.astype(np.float32)).astype(jnp.bfloat16)
    w_flat = w_qkv.transpose(1, 2, 3, 0).reshape(3 * width, model)
    gain = ln_gain.reshape(1, model)
    field_grad, amse, coeff, mix, projected, rolled = spread(
        shift,
        prediction.reshape(-1, LON),
        target.reshape(-1, LON),
        jnp.asarray(np.stack([high, low])),
        legendre,
        w_dec.reshape(-1, model),
        w_proj.reshape(-1, model),
        tokens,
        gain,
        w_flat,
        sizes,
        cols,
        weight,
        7,
    )
    by_column = jnp.asarray(rows.T.reshape(col_count, 4, -1).transpose(1, 0, 2), BF16)
    f_rolled = jnp.roll(by_column, -offset, axis=1)
    f_rolled = f_rolled.reshape(4, col_count // cols, cols, -1)
    summed = layer_backward(
        f_rolled,
        coeff,
        mix.reshape(-1, width + share),
        projected,
        rolled,
        gain,
        w_flat,
        sizes,
        8,
    )
    summed = summed.reshape(col_count // cols, WR, cols, share).transpose(1, 0, 2, 3)
    input_grad = jnp.roll(summed.reshape(row_count, col_count, share), offset, axis=1)
    return (amse[:, 0], field_grad.reshape(var_count, lats, LON), input_grad)


def solution(mesh):
    return jax.shard_map(
        body,
        mesh=mesh,
        in_specs=(
            P("proc", None, None),
            P(),
            P(None, None, ("loss", "vars"), None),
            P(),
            P(),
            P(("loss", "vars"), None, None, None),
            P(("loss", "vars"), "proc", None),
            P(("loss", "vars"), "proc", None),
            P("proc", None, None),
        ),
        out_specs=(
            P(("loss", "vars")),
            P(("loss", "vars"), "proc", None),
            P("proc", None, ("loss", "vars")),
        ),
        check_vma=False,
    )
```

```python
import functools
import math
import types

import jax
import jax.numpy as jnp
import numpy as np
from jax import lax
from jax.experimental import pallas as pl
from jax.experimental.pallas import tpu as pltpu
from jax.sharding import PartitionSpec as P

HEAD = 96
VARS = 64
LON = 1440
LDEG = 384
WR = 2
WC = 12

EPSILON = 1e-06
NORM_EPSILON = 1e-05
HIGHEST = lax.Precision.HIGHEST
MESH = pl.DeviceIdType.MESH
F32 = jnp.float32
BF16 = jnp.bfloat16
VMEM = pl.BlockSpec(memory_space=pltpu.VMEM)
NT = (((1,), (1,)), ((), ()))


def fourier_basis(mode_count):
    column = np.arange(LON, dtype=np.int64)
    wavenumber = np.arange(mode_count, dtype=np.int64)
    phase = (column[:, None] * wavenumber[None, :] % LON) * (2.0 * math.pi / LON)
    return np.stack([np.cos(phase), -np.sin(phase)]) / math.sqrt(LON)


def amse_terms(power_pred, power_true, crossed):
    amp_pred = jnp.sqrt(power_pred + EPSILON)
    amp_true = jnp.sqrt(power_true + EPSILON)
    return (amp_pred - amp_true) ** 2 + 2.0 * jnp.maximum(power_pred, power_true) * (
        1.0 - crossed / (amp_pred * amp_true)
    )


def place(axis, index, sizes):
    proc, loss, var = (lax.axis_index(name) for name in ("proc", "loss", "vars"))
    if axis == "proc":
        return (index, loss, var)
    if axis == "loss":
        return (proc, index, var)
    if axis == "vars":
        return (proc, loss, index)
    return (proc, index // sizes["vars"], lax.rem(index, sizes["vars"]))


def rank(axis, sizes):
    if axis == "group":
        return lax.axis_index("loss") * sizes["vars"] + lax.axis_index("vars")
    return lax.axis_index(axis)


def greet(pairs):
    barrier = pltpu.get_barrier_semaphore()
    for device in pairs:
        pl.semaphore_signal(barrier, inc=1, device_id=device, device_id_type=MESH)
    pl.semaphore_wait(barrier, len(pairs))


def exchange_kernel(axis, count, sizes, spread, x_ref, out_ref, send, recv, own):
    me = rank(axis, sizes)
    peers = [lax.rem(me + k, count) for k in range(1, count)]
    greet([place(axis, peer, sizes) for peer in peers])
    copies = []
    for k, peer in enumerate(peers):
        copies.append(
            pltpu.make_async_remote_copy(
                src_ref=x_ref if spread else x_ref.at[peer],
                dst_ref=out_ref.at[k + 1] if spread else out_ref.at[me],
                send_sem=send.at[k],
                recv_sem=recv.at[k],
                device_id=place(axis, peer, sizes),
                device_id_type=MESH,
            )
        )
        copies[-1].start()
    if spread:
        local = pltpu.make_async_copy(x_ref, out_ref.at[0], own)
    else:
        local = pltpu.make_async_copy(x_ref.at[me], out_ref.at[me], own)
    local.start()
    local.wait()
    for copy in copies:
        copy.wait()


def exchange(x, axis, sizes, collective_id, spread=False):
    count = sizes["loss"] * sizes["vars"] if axis == "group" else sizes[axis]
    shape = (count,) + x.shape if spread else x.shape
    return pl.pallas_call(
        functools.partial(exchange_kernel, axis, count, sizes, spread),
        out_shape=jax.ShapeDtypeStruct(shape, x.dtype),
        in_specs=[VMEM],
        out_specs=VMEM,
        scratch_shapes=[
            pltpu.SemaphoreType.DMA((count - 1,)),
            pltpu.SemaphoreType.DMA((count - 1,)),
            pltpu.SemaphoreType.DMA,
        ],
        compiler_params=pltpu.CompilerParams(
            collective_id=collective_id, has_side_effects=True
        ),
        name="exchange_%d" % collective_id,
    )(x)


def harmonics_kernel(modes, var_count, spectra_ref, legendre_ref, harm_ref, power_ref):
    half = 2 * var_count
    sums = [jnp.zeros((half, LDEG), F32) for _ in range(3)]
    for m in range(modes):
        harm = jnp.dot(
            spectra_ref[m], legendre_ref[m], precision=HIGHEST, preferred_element_type=F32
        )
        harm_ref[m] = harm
        pred, true = harm[:half], harm[half:]
        sums = [sums[0] + pred * pred, sums[1] + true * true, sums[2] + pred * true]
    for i in range(3):
        power_ref[i] = sums[i][:var_count] + sums[i][var_count:]


def harmonics(spectra, legendre):
    modes, rows, _ = spectra.shape
    var_count = rows // 4
    return pl.pallas_call(
        functools.partial(harmonics_kernel, modes, var_count),
        out_shape=(
            jax.ShapeDtypeStruct((modes, rows, LDEG), F32),
            jax.ShapeDtypeStruct((3, var_count, LDEG), F32),
        ),
        in_specs=[VMEM, VMEM],
        out_specs=(VMEM, VMEM),
        name="harmonics",
    )(spectra, legendre)


def spectral_kernel(
    modes,
    sizes,
    var_count,
    weight,
    spectra_ref,
    legendre_ref,
    terms_ref,
    banded_ref,
    coeff_ref,
    harm,
    power,
    parts,
    acc,
    rows,
    outgoing,
    narrow,
    sa,
    ra,
    sb,
    rb,
    sc,
    rc,
    sd,
    rd,
):
    procs = sizes["proc"]
    group_count = sizes["loss"] * sizes["vars"]
    me, team = rank("proc", sizes), rank("group", sizes)
    peers = [lax.rem(me + k, procs) for k in range(1, procs)]
    mates = [lax.rem(team + k, group_count) for k in range(1, group_count)]
    greet(
        [place("proc", peer, sizes) for peer in peers]
        + [place("group", mate, sizes) for mate in mates]
    )
    half = 2 * var_count
    each = var_count // procs

    def copy(src, dst, send, recv, device):
        return pltpu.make_async_remote_copy(
            src_ref=src,
            dst_ref=dst,
            send_sem=send,
            recv_sem=recv,
            device_id=device,
            device_id_type=MESH,
        )

    sums = [jnp.zeros((half, LDEG), F32) for _ in range(3)]
    for m in range(modes):
        value = jnp.dot(
            spectra_ref[m], legendre_ref[m], precision=HIGHEST, preferred_element_type=F32
        )
        harm[m] = value
        pred, true = value[:half], value[half:]
        sums = [sums[0] + pred * pred, sums[1] + true * true, sums[2] + pred * true]
    for i in range(3):
        total = sums[i][:var_count] + sums[i][var_count:]
        for p in range(procs):
            power[p, i * each : (i + 1) * each] = total[p * each : (p + 1) * each]

    sent = [
        copy(power.at[peer], parts.at[k], sa.at[k], ra.at[k], place("proc", peer, sizes))
        for k, peer in enumerate(peers)
    ]
    for made in sent:
        made.start()
    for made in sent:
        made.wait()
    total = power[me]
    for k in range(procs - 1):
        total = total + parts[k]
    powers = [total[i * each : (i + 1) * each] for i in range(3)]
    terms, pullback = jax.vjp(amse_terms, *powers)
    grad_pred, _, grad_cross = pullback(jnp.full((each, LDEG), weight, F32))
    acc[...] = jnp.concatenate([2.0 * grad_pred, grad_cross, terms], axis=0)
    terms_ref[me] = acc[...]
    sent = [
        copy(acc, terms_ref.at[me], sb.at[k], rb.at[k], place("proc", peer, sizes))
        for k, peer in enumerate(peers)
    ]
    for made in sent:
        made.start()
    for made in sent:
        made.wait()
    gp = jnp.concatenate([terms_ref[p, :each] for p in range(procs)] * 2, axis=0)
    gc = jnp.concatenate([terms_ref[p, each : 2 * each] for p in range(procs)] * 2, axis=0)

    lats = legendre_ref.shape[1]
    own = lats // procs
    for m in range(modes):
        value = harm[m]
        grad = gp * value[:half] + gc * value[half:]
        rows[m * half : (m + 1) * half, :lats] = lax.dot_general(
            grad, legendre_ref[m], NT, precision=HIGHEST, preferred_element_type=F32
        )
    by_var = [rows[pl.ds(v, 2 * modes, stride=var_count), :] for v in range(var_count)]
    for q in range(procs):
        outgoing[q] = jnp.concatenate(
            [
                by_var[v][:, q * own + 4 * r : q * own + 4 * r + 4]
                for r in range(own // 4)
                for v in range(var_count)
            ],
            axis=1,
        )
    sent = [
        copy(outgoing.at[peer], banded_ref.at[me], sc.at[k], rc.at[k], place("proc", peer, sizes))
        for k, peer in enumerate(peers)
    ]
    for made in sent:
        made.start()
    banded_ref[me] = outgoing[me]

    passed = []
    for k in range(procs):
        source = lax.rem(me + procs - k, procs)
        if k > 0:
            sent[k - 1].wait_recv()
        value = banded_ref[source].astype(BF16)
        narrow[source] = value
        coeff_ref[0, source] = value
        for j, mate in enumerate(mates):
            passed.append(
                copy(
                    narrow.at[source],
                    coeff_ref.at[j + 1, source],
                    sd.at[k, j],
                    rd.at[k, j],
                    place("group", mate, sizes),
                )
            )
            passed[-1].start()
    for made in sent:
        made.wait_send()
    for made in passed:
        made.wait()


def spectral(spectra, legendre, sizes, weight, collective_id):
    procs = sizes["proc"]
    group_count = sizes["loss"] * sizes["vars"]
    modes, rows, lats = spectra.shape
    var_count = rows // 4
    each = var_count // procs
    block = (procs, 2 * modes, var_count * lats // procs)
    dma = pltpu.SemaphoreType.DMA
    return pl.pallas_call(
        functools.partial(spectral_kernel, modes, sizes, var_count, weight),
        out_shape=(
            jax.ShapeDtypeStruct((procs, 3 * each, LDEG), F32),
            jax.ShapeDtypeStruct(block, F32),
            jax.ShapeDtypeStruct((group_count,) + block, BF16),
        ),
        in_specs=[VMEM, VMEM],
        out_specs=(VMEM, VMEM, VMEM),
        scratch_shapes=[
            pltpu.VMEM((modes, rows, LDEG), F32),
            pltpu.VMEM((procs, 3 * each, LDEG), F32),
            pltpu.VMEM((procs - 1, 3 * each, LDEG), F32),
            pltpu.VMEM((3 * each, LDEG), F32),
            pltpu.VMEM((2 * modes * var_count, pl.cdiv(lats, 128) * 128), F32),
            pltpu.VMEM(block, F32),
            pltpu.VMEM(block, BF16),
        ]
        + [dma((procs - 1,)) for _ in range(6)]
        + [dma((procs, group_count - 1)) for _ in range(2)],
        compiler_params=pltpu.CompilerParams(
            collective_id=collective_id, has_side_effects=True
        ),
        name="spectral",
    )(spectra, legendre)


def attention_kernel(
    heads,
    cols,
    blocks,
    sizes,
    f_ref,
    coeff_ref,
    mix_ref,
    proj_ref,
    tok_ref,
    gain_ref,
    w_ref,
    out_ref,
    part,
    kept,
    got,
    mid,
    far,
    s1,
    r1,
    s2,
    r2,
):
    loss_count, var_count = sizes["loss"], sizes["vars"]
    loss, var = lax.axis_index("loss"), lax.axis_index("vars")
    near = [lax.rem(var + k, var_count) for k in range(1, var_count)]
    away = [lax.rem(loss + k, loss_count) for k in range(1, loss_count)]
    step = pl.program_id(0)
    rows = WR * cols

    @pl.when(step == 0)
    def _():
        greet(
            [place("vars", peer, sizes) for peer in near]
            + [place("loss", peer, sizes) for peer in away]
        )

    def near_copies(b):
        return [
            pltpu.make_async_remote_copy(
                src_ref=part.at[b, peer],
                dst_ref=got.at[b, k],
                send_sem=s1.at[b, k],
                recv_sem=r1.at[b, k],
                device_id=place("vars", peer, sizes),
                device_id_type=MESH,
            )
            for k, peer in enumerate(near)
        ]

    def away_copies(b):
        return [
            pltpu.make_async_remote_copy(
                src_ref=mid.at[b, peer],
                dst_ref=far.at[b, k],
                send_sem=s2.at[b, k],
                recv_sem=r2.at[b, k],
                device_id=place("loss", peer, sizes),
                device_id_type=MESH,
            )
            for k, peer in enumerate(away)
        ]

    def pass_on(b):
        for made in near_copies(b):
            made.wait()
        for j in range(loss_count):
            value = part[b, var, j].astype(F32)
            for k in range(var_count - 1):
                value = value + got[b, k, j].astype(F32)
            mid[b, j] = value.astype(BF16)
        for made in away_copies(b):
            made.start()

    pieces = []
    for o in range(4):
        y = jnp.dot(f_ref[o], coeff_ref[0], preferred_element_type=F32)
        half = y.shape[1] // WR
        pieces.append(
            jnp.concatenate([y[:, r * half : (r + 1) * half] for r in range(WR)], axis=0).astype(BF16)
        )
    tiles = jnp.concatenate(pieces, axis=1)
    mixed = jnp.dot(tiles, mix_ref[...], preferred_element_type=F32)
    width = heads * HEAD
    grad_out = mixed[:, :width].astype(BF16)
    kept[step] = mixed[:, width:]

    window_i = lax.rem(lax.broadcasted_iota(jnp.int32, (rows, rows), 0), cols) // WC
    window_j = lax.rem(lax.broadcasted_iota(jnp.int32, (rows, rows), 1), cols) // WC
    same = window_i == window_j
    scale = HEAD ** (-0.5)
    grads = [[], [], []]
    for h in range(heads):
        q, k, v = (
            proj_ref[0, :, (i * heads + h) * HEAD : (i * heads + h + 1) * HEAD] for i in range(3)
        )
        go = grad_out[:, h * HEAD : (h + 1) * HEAD]
        scores = lax.dot_general(q, k, NT, preferred_element_type=F32) * scale
        weights = jnp.where(same, jnp.exp(scores), 0.0)
        weights = weights / jnp.sum(weights, axis=-1, keepdims=True)
        rounded = weights.astype(BF16)
        first = (((0,), (0,)), ((), ()))
        grads[2].append(
            lax.dot_general(rounded, go, first, preferred_element_type=F32).astype(BF16)
        )
        grad_weights = lax.dot_general(go, v, NT, preferred_element_type=F32)
        inner = jnp.sum(weights * grad_weights, axis=-1, keepdims=True)
        score_round = (weights * (grad_weights - inner) * scale).astype(BF16)
        grads[0].append(jnp.dot(score_round, k, preferred_element_type=F32).astype(BF16))
        grads[1].append(
            lax.dot_general(score_round, q, first, preferred_element_type=F32).astype(BF16)
        )
    stacked = jnp.concatenate(grads[0] + grads[1] + grads[2], axis=1)
    grad_normed = lax.dot_general(stacked, w_ref[...], NT, preferred_element_type=F32)

    values = tok_ref[0].astype(F32)
    centred = values - jnp.mean(values, axis=-1, keepdims=True)
    inv_std = lax.rsqrt(jnp.mean(centred * centred, axis=-1, keepdims=True) + NORM_EPSILON)
    normed = centred * inv_std
    scaled = grad_normed * gain_ref[...]
    local = inv_std * (
        scaled
        - jnp.mean(scaled, axis=-1, keepdims=True)
        - normed * jnp.mean(scaled * normed, axis=-1, keepdims=True)
    )
    local = local.astype(BF16)
    share = local.shape[1] // (loss_count * var_count)
    for l in range(loss_count):
        for v in range(var_count):
            at = (l * var_count + v) * share
            part[step, v, l] = local[:, at : at + share]
    for made in near_copies(step):
        made.start()

    @pl.when(step > 0)
    def _():
        pass_on(step - 1)

    @pl.when(step == blocks - 1)
    def _():
        pass_on(blocks - 1)
        for b in range(blocks):
            for made in away_copies(b):
                made.wait()
            value = mid[b, loss].astype(F32)
            for k in range(loss_count - 1):
                value = value + far[b, k].astype(F32)
            out_ref[b] = value.astype(BF16)


def attention_backward(f_rolled, coeff, mix, projected, tokens, gain, w_flat, sizes, collective_id):
    blocks, rows, model = tokens.shape
    pairs = coeff.shape[0]
    cols = rows // WR
    per_pair = blocks // pairs
    depth = f_rolled.shape[2]
    width = projected.shape[2] // 3
    heads = width // HEAD
    loss_count, var_count = sizes["loss"], sizes["vars"]
    share = model // (loss_count * var_count)

    def whole(shape):
        return pl.BlockSpec(shape, lambda b: (0,) * len(shape))

    def per_block(shape):
        return pl.BlockSpec((1,) + shape, lambda b: (b,) + (0,) * len(shape))

    return pl.pallas_call(
        functools.partial(attention_kernel, heads, cols, blocks, sizes),
        grid=(blocks,),
        in_specs=[
            pl.BlockSpec((4, cols, depth), lambda b: (0, lax.rem(b, per_pair), 0)),
            pl.BlockSpec((1,) + coeff.shape[1:], lambda b: (b // per_pair, 0, 0)),
            whole(mix.shape),
            per_block((rows, 3 * width)),
            per_block((rows, model)),
            whole(gain.shape),
            whole(w_flat.shape),
        ],
        out_specs=whole((blocks, rows, share)),
        out_shape=jax.ShapeDtypeStruct((blocks, rows, share), BF16),
        scratch_shapes=[
            pltpu.VMEM((blocks, var_count, loss_count, rows, share), BF16),
            pltpu.VMEM((blocks, rows, share), F32),
            pltpu.VMEM((blocks, var_count - 1, loss_count, rows, share), BF16),
            pltpu.VMEM((blocks, loss_count, rows, share), BF16),
            pltpu.VMEM((blocks, loss_count - 1, rows, share), BF16),
            pltpu.SemaphoreType.DMA((blocks, var_count - 1)),
            pltpu.SemaphoreType.DMA((blocks, var_count - 1)),
            pltpu.SemaphoreType.DMA((blocks, loss_count - 1)),
            pltpu.SemaphoreType.DMA((blocks, loss_count - 1)),
        ],
        compiler_params=pltpu.CompilerParams(
            collective_id=collective_id, has_side_effects=True
        ),
        name="attention_backward",
    )(f_rolled, coeff, mix, projected, tokens, gain, w_flat)


def body_general(tokens, shift, w_qkv, w_proj, ln_gain, w_dec, prediction, target, legendre):
    sizes = {name: lax.axis_size(name) for name in ("proc", "loss", "vars")}
    procs = sizes["proc"]
    groups = (sizes["loss"], sizes["vars"])
    group_count = groups[0] * groups[1]
    modes = legendre.shape[0]
    lat_all = legendre.shape[1]
    modes_all = modes * procs
    var_count, lats = prediction.shape[0], prediction.shape[1]
    basis = fourier_basis(modes_all)
    row_count, col_count, model = tokens.shape
    offset = shift[0]
    head_local = w_qkv.shape[2]
    width = head_local * HEAD
    share = model // group_count

    ordered = basis.transpose(2, 0, 1).reshape(-1, LON)
    to_modes = jnp.asarray(ordered, F32)
    fields = jnp.concatenate([prediction.astype(F32), target]).reshape(-1, LON)
    spectra = lax.dot_general(to_modes, fields, NT, precision=HIGHEST)
    at_owner = exchange(spectra.reshape(procs, 2 * modes, -1), "proc", sizes, 1)
    at_owner = at_owner.reshape(procs, modes, 2, 2, var_count, lats).transpose(1, 3, 2, 4, 0, 5)
    at_owner = at_owner.reshape(modes, 4 * var_count, lat_all)
    weight_grad = lat_all * LON / (VARS * LDEG * modes_all)
    if var_count % procs == 0:
        terms, banded, coeff = spectral(at_owner, legendre, sizes, weight_grad, 2)
        each = var_count // procs
        degree_terms = terms[:, 2 * each :].reshape(var_count, LDEG)
    else:
        harm, power = harmonics(at_owner, legendre)
        power = lax.psum(power, "proc")
        degree_terms, pullback = jax.vjp(amse_terms, power[0], power[1], power[2])
        grad_pred, _, grad_cross = pullback(jnp.full(degree_terms.shape, weight_grad, F32))
        harm = harm.reshape(modes, 2, 2, var_count, LDEG)
        grad_harm = 2.0 * grad_pred * harm[:, 0] + grad_cross * harm[:, 1]
        grad_spectra = jnp.einsum("mcvl,mal->mcva", grad_harm, legendre, precision=HIGHEST)
        grad_spectra = grad_spectra.reshape(modes, 2, var_count, procs, lats // 4, 4)
        grad_spectra = grad_spectra.transpose(3, 0, 1, 4, 2, 5).reshape(procs, 2 * modes, -1)
        banded = exchange(grad_spectra, "proc", sizes, 3)
        coeff = exchange(banded.astype(BF16), "group", sizes, 4, spread=True)
    amse = jnp.sum(degree_terms, axis=-1) / (LDEG * modes_all)
    pairs = row_count // WR
    banded = banded.reshape(2 * modes_all, row_count, var_count, 4).transpose(0, 2, 1, 3)
    coeff = coeff.reshape(group_count, 2 * modes_all, pairs, WR, 4 * var_count)
    coeff = coeff.transpose(2, 1, 3, 0, 4).reshape(pairs, 2 * modes_all, -1)

    field_grad = lax.dot_general(
        banded.reshape(2 * modes_all, -1),
        to_modes,
        (((0,), (0,)), ((), ())),
        precision=HIGHEST,
    ).reshape(var_count, lats, LON)

    decoder = w_dec.transpose(2, 0, 1, 3).reshape(4 * var_count * 4, model)
    through = lax.dot_general(
        decoder, w_proj.reshape(-1, model), NT, preferred_element_type=F32
    ).astype(BF16)
    mix = jnp.concatenate(
        [
            through.reshape(-1, group_count, width),
            decoder.reshape(-1, group_count, share),
        ],
        axis=2,
    ).transpose(1, 0, 2)
    me = rank("group", sizes)
    received = [lax.dynamic_index_in_dim(mix, me, 0, keepdims=False)]
    for k in range(1, group_count):
        block = lax.dynamic_index_in_dim(mix, lax.rem(me + k, group_count), 0, keepdims=False)
        ring = [(g, (g + k) % group_count) for g in range(group_count)]
        received.append(lax.ppermute(block, ("loss", "vars"), ring))
    mix = jnp.stack(received)
    mix = mix.reshape(group_count, 4, 4 * var_count, width + share).transpose(1, 0, 2, 3)
    mix = mix.reshape(-1, width + share)

    cols = 120
    split = (pairs, WR, col_count // cols, cols)
    rolled = jnp.roll(tokens, -offset, axis=1)
    rolled = rolled.reshape(split + (model,)).transpose(0, 2, 1, 3, 4)
    rolled = rolled.reshape(-1, WR * cols, model)
    values = rolled.astype(F32)
    centred = values - jnp.mean(values, axis=-1, keepdims=True)
    inv_std = lax.rsqrt(jnp.mean(centred * centred, axis=-1, keepdims=True) + NORM_EPSILON)
    norm_out = (centred * inv_std * ln_gain).astype(BF16)
    w_flat = w_qkv.reshape(model, 3 * width)
    projected = jnp.einsum(
        "brd,dk->brk", norm_out, w_flat, preferred_element_type=F32
    ).astype(BF16)
    by_column = jnp.asarray(ordered.T.reshape(col_count, 4, -1).transpose(1, 0, 2), BF16)
    f_rolled = jnp.roll(by_column, -offset, axis=1)
    summed = attention_backward(
        f_rolled, coeff, mix, projected, rolled, ln_gain.reshape(1, model), w_flat, sizes, 6
    )
    summed = summed.reshape(pairs, col_count // cols, WR, cols, share).transpose(0, 2, 1, 3, 4)
    input_grad = jnp.roll(summed.reshape(row_count, col_count, share), offset, axis=1)
    return (amse, field_grad, input_grad)


def fused_kernel(sizes, dims, names, *refs):
    ref = types.SimpleNamespace(**dict(zip(names, refs)))
    procs, modes, var_count, lats = dims.procs, dims.modes, dims.vars, dims.lats
    loss_count, core_count = sizes["loss"], sizes["vars"]
    group_count = loss_count * core_count
    lat_all = procs * lats
    each = var_count // procs
    half = 2 * var_count
    fold = 128 // half
    strips = lats // fold
    blocks, cols, heads = dims.blocks, dims.cols, dims.heads
    rows = WR * cols
    width, share = heads * HEAD, dims.share
    me, team = rank("proc", sizes), rank("group", sizes)
    loss, core = lax.axis_index("loss"), lax.axis_index("vars")
    peers = [lax.rem(me + k, procs) for k in range(1, procs)]
    mates = [lax.rem(team + k, group_count) for k in range(1, group_count)]
    near = [lax.rem(core + k, core_count) for k in range(1, core_count)]
    away = [lax.rem(loss + k, loss_count) for k in range(1, loss_count)]
    first = (((0,), (0,)), ((), ()))

    barrier = pltpu.get_barrier_semaphore()
    places = [place("proc", peer, sizes) for peer in peers]
    mate_places = [place("group", mate, sizes) for mate in mates]
    for device in places + mate_places:
        pl.semaphore_signal(barrier, inc=1, device_id=device, device_id_type=MESH)

    load = {}
    for i, name in enumerate(dims.loads):
        load[name] = pltpu.make_async_copy(
            getattr(ref, name + "_hbm"), getattr(ref, name), ref.load_sems.at[i]
        )
        load[name].start()
    load = types.SimpleNamespace(**load)

    def copy(src, dst, send, recv, device):
        return pltpu.make_async_remote_copy(
            src_ref=src,
            dst_ref=dst,
            send_sem=send,
            recv_sem=recv,
            device_id=device,
            device_id_type=MESH,
        )

    def permutation(count, source):
        i = lax.broadcasted_iota(jnp.int32, (count, count), 0)
        j = lax.broadcasted_iota(jnp.int32, (count, count), 1)
        return jnp.where(i == source(j), 1.0, 0.0).astype(BF16)

    y_out, y_in, basis = ref.y_out, ref.y_in, ref.basis
    by_lat = permutation(lats * half, lambda j: lax.rem(j, half) * lats + j // half)
    load.basis.wait()
    load.pred.wait()
    load.target.wait()
    y = [
        lax.dot_general(basis[0], field, NT, preferred_element_type=F32)
        + lax.dot_general(basis[1], field, NT, preferred_element_type=F32)
        for field in (ref.pred[...], ref.target[...].astype(BF16))
    ]
    y = jnp.concatenate(y, axis=1).astype(BF16)
    y = jnp.dot(y, by_lat, preferred_element_type=F32)
    for p in range(procs):
        y_out[p] = y[p * 2 * modes : (p + 1) * 2 * modes].astype(BF16)
    pl.semaphore_wait(barrier, procs + group_count - 2)
    sent_y = [
        copy(y_out.at[peer], y_in.at[me], ref.sy.at[k], ref.ry.at[k], places[k])
        for k, peer in enumerate(peers)
    ]
    for made in sent_y:
        made.start()
    y_in[me] = y_out[me]

    wproj, mix_out, mix = ref.wproj, ref.mix_out, ref.mix
    count = 16 * var_count
    i = lax.broadcasted_iota(jnp.int32, (count, count), 0)
    j = lax.broadcasted_iota(jnp.int32, (count, count), 1)
    o, a, v = i // (4 * var_count), lax.rem(i // var_count, 4), lax.rem(i, var_count)
    order = jnp.where(j == v * 16 + a * 4 + o, 1.0, 0.0).astype(BF16)
    load.dec.wait()
    decoder = jnp.dot(
        order, ref.dec[...].reshape(count, -1), preferred_element_type=F32
    ).astype(BF16)
    ref.decoder[...] = decoder
    load.wproj.wait()
    for g in range(group_count):
        through = lax.dot_general(
            decoder, wproj[g * width : (g + 1) * width], NT, preferred_element_type=F32
        ).astype(BF16)
        for o in range(4):
            at = o * 4 * var_count
            mix_out[g, o] = through[at : at + 4 * var_count]
    sent_mix = [
        copy(
            mix_out.at[mate], mix.at[:, k + 1], ref.sm.at[k], ref.rm.at[k], mate_places[k]
        )
        for k, mate in enumerate(mates)
    ]
    for made in sent_mix:
        made.start()
    for o in range(4):
        mix[o, 0] = mix_out[team, o]

    leg, legendre = ref.leg, ref.legendre
    i = lax.broadcasted_iota(jnp.int32, (lat_all, lat_all), 0)
    j = lax.broadcasted_iota(jnp.int32, (lat_all, lat_all), 1)
    tall = lat_all // fold
    by_fold = jnp.where(j == lax.rem(i, tall) * fold + i // tall, 1.0, 0.0).astype(BF16)
    load.legendre.wait()
    for m in range(modes):
        leg[m] = jnp.dot(
            by_fold, legendre[m].astype(BF16), preferred_element_type=F32
        ).astype(BF16)

    tokens, wide, norm_out, qkv = ref.tokens, ref.wide, ref.norm_out, ref.qkv
    inv, w_flat, columns, f_rolled = ref.inv, ref.w, ref.columns, ref.f_rolled
    row_count, col_count = tokens.shape[0], tokens.shape[1]
    offset = lax.rem(ref.shift[0], col_count)
    for made in (load.tokens, load.gain, load.w, load.columns):
        made.wait()
    gain = jnp.concatenate(
        [ref.gain[i : i + 1] for i in range(ref.gain.shape[0])], axis=1
    )

    def roll(b):
        i = lax.broadcasted_iota(jnp.int32, (cols, col_count), 0) + (b * cols + offset)
        j = lax.broadcasted_iota(jnp.int32, (cols, col_count), 1)
        pick = jnp.where((i == j) | (i == j + col_count), 1.0, 0.0).astype(BF16)
        for r in range(row_count):
            wide[b, r * cols : (r + 1) * cols] = jnp.dot(
                pick, tokens[r], preferred_element_type=F32
            )
        for o in range(4):
            f_rolled[b, o] = jnp.dot(pick, columns[o], preferred_element_type=F32).astype(BF16)

    def normalise(b):
        step = 48
        for at in range(0, rows, step):
            part_rows = slice(at, at + step)
            values = wide[b, part_rows]
            centred = values - jnp.mean(values, axis=-1, keepdims=True)
            inv_std = lax.rsqrt(
                jnp.mean(centred * centred, axis=-1, keepdims=True) + NORM_EPSILON
            )
            normed = centred * inv_std
            wide[b, part_rows] = normed
            inv[b, part_rows] = jnp.broadcast_to(inv_std, (step, 128))
            norm_out[b, part_rows] = (normed * gain).astype(BF16)

    def project(b):
        projected = lax.dot_general(
            norm_out[b], w_flat[...], NT, preferred_element_type=F32
        ).astype(BF16)
        for i in range(3 * heads):
            qkv[b, i] = projected[:, i * HEAD : (i + 1) * HEAD]

    scale = HEAD ** (-0.5)
    soft = ref.soft
    window_i = lax.rem(lax.broadcasted_iota(jnp.int32, (rows, rows), 0), cols) // WC
    window_j = lax.rem(lax.broadcasted_iota(jnp.int32, (rows, rows), 1), cols) // WC
    same = window_i == window_j

    def attend(b):
        for h in range(heads):
            scores = (
                lax.dot_general(qkv[b, h], qkv[b, heads + h], NT, preferred_element_type=F32)
                * scale
            )
            weights = jnp.where(same, jnp.exp(scores), 0.0)
            soft[b, h] = weights / jnp.sum(weights, axis=-1, keepdims=True)

    back = ref.back

    def unroll(b):
        i = lax.broadcasted_iota(jnp.int32, (col_count, rows), 0)
        j = lax.broadcasted_iota(jnp.int32, (col_count, rows), 1)
        for r in range(WR):
            to = j - r * cols + b * cols + offset
            here = (j // cols == r) & ((to == i) | (to == i + col_count))
            back[b, r] = jnp.where(here, 1.0, 0.0).astype(BF16)

    for b in range(blocks):
        roll(b)

    x_wide, harm, power, parts = ref.x_wide, ref.harm, ref.power, ref.parts
    for made in sent_y:
        made.wait()
    for p in range(procs):
        for h in range(strips):
            at = (p * strips + h) * 2 * modes
            x_wide[at : at + 2 * modes] = y_in[p, :, h * 128 : (h + 1) * 128].astype(F32)
    power_sums = [jnp.zeros((var_count, LDEG), F32) for _ in range(3)]
    for m in range(modes):
        z = [x_wide[pl.ds(c * modes + m, tall, stride=2 * modes), :] for c in range(2)]
        x = jnp.concatenate(
            [
                jnp.concatenate([z[c][:, f * half : (f + 1) * half] for c in range(2)], axis=1)
                for f in range(fold)
            ],
            axis=0,
        ).astype(BF16)
        value = lax.dot_general(x, leg[m], first, preferred_element_type=F32)
        harm[m] = value
        for c in range(2):
            pred = value[c * half : c * half + var_count]
            true = value[c * half + var_count : (c + 1) * half]
            power_sums = [
                power_sums[0] + pred * pred,
                power_sums[1] + true * true,
                power_sums[2] + pred * true,
            ]
    for i in range(3):
        for p in range(procs):
            power[p, i * each : (i + 1) * each] = power_sums[i][p * each : (p + 1) * each]
    sent = [
        copy(power.at[peer], parts.at[k], ref.sa.at[k], ref.ra.at[k], places[k])
        for k, peer in enumerate(peers)
    ]
    for made in sent:
        made.start()
    for b in range(blocks):
        normalise(b)
    for b in range(blocks):
        project(b)
    for made in sent:
        made.wait()
    acc, terms_in = ref.acc, ref.terms_in
    total = power[me]
    for k in range(procs - 1):
        total = total + parts[k]
    powers = [total[i * each : (i + 1) * each] for i in range(3)]
    terms, pullback = jax.vjp(amse_terms, *powers)
    grad_pred, _, grad_cross = pullback(jnp.full((each, LDEG), dims.weight, F32))
    acc[...] = jnp.concatenate([2.0 * grad_pred, grad_cross, terms], axis=0)
    terms_in[me] = acc[...]
    sent = [
        copy(acc, terms_in.at[me], ref.sb.at[k], ref.rb.at[k], places[k])
        for k, peer in enumerate(peers)
    ]
    for made in sent:
        made.start()
    attend(0)
    attend(1)
    for made in sent:
        made.wait()
    gp = jnp.concatenate([terms_in[p, :each] for p in range(procs)], axis=0)
    gc = jnp.concatenate([terms_in[p, each : 2 * each] for p in range(procs)], axis=0)

    g_wide, g_out, coeff = ref.g_wide, ref.g_out, ref.coeff
    for m in range(modes):
        value = harm[m]
        grad = jnp.concatenate(
            [
                gp * value[c * half : c * half + var_count]
                + gc * value[c * half + var_count : (c + 1) * half]
                for c in range(2)
            ],
            axis=0,
        ).astype(BF16)
        g_wide[m * lat_all : (m + 1) * lat_all, :half] = lax.dot_general(
            leg[m], grad, NT, preferred_element_type=F32
        )
    for q in range(procs):
        pieces = []
        for a in range(lats):
            at = (a % fold) * tall + q * strips + a // fold
            pieces.append(g_wide[pl.ds(at, modes, stride=lat_all), :])
        g_out[q] = jnp.concatenate(
            [
                jnp.concatenate(
                    [piece[:, c * var_count : (c + 1) * var_count] for piece in pieces], axis=1
                )
                for c in range(2)
            ],
            axis=0,
        ).astype(BF16)
    sent = [
        copy(g_out.at[peer], coeff.at[0, me], ref.sc.at[k], ref.rc.at[k], places[k])
        for k, peer in enumerate(peers)
    ]
    for made in sent:
        made.start()
    coeff[0, me] = g_out[me]
    for b in range(2, blocks):
        attend(b)
    for b in range(blocks):
        unroll(b)
    on_row = lax.broadcasted_iota(jnp.int32, (each, var_count), 0)
    on_col = lax.broadcasted_iota(jnp.int32, (each, var_count), 1)
    amse = jnp.zeros((1, var_count), F32)
    for p in range(procs):
        sums = jnp.sum(terms_in[p, 2 * each :], axis=-1, keepdims=True) / dims.terms
        spots = jnp.where(on_col == on_row + p * each, sums, 0.0)
        amse = amse + jnp.sum(spots, axis=0, keepdims=True)
    ref.amse[...] = amse

    passed = []
    for k in range(procs):
        source = lax.rem(me + procs - k, procs)
        if k > 0:
            sent[k - 1].wait_recv()
        for j in range(group_count - 1):
            passed.append(
                copy(
                    coeff.at[0, source],
                    coeff.at[j + 1, source],
                    ref.sd.at[k, j],
                    ref.rd.at[k, j],
                    mate_places[j],
                )
            )
            passed[-1].start()
    own = jnp.concatenate([coeff[0, p] for p in range(procs)], axis=0)
    by_var = permutation(lats * var_count, lambda j: lax.rem(j, lats) * var_count + j // lats)
    own = jnp.dot(own, by_var, preferred_element_type=F32).astype(BF16)
    grid = lax.dot_general(own, basis[0], first, preferred_element_type=F32)
    ref.field_grad[...] = grid + lax.dot_general(
        own, basis[1], first, preferred_element_type=F32
    )
    for made in sent:
        made.wait_send()
    for made in passed:
        made.wait()
    for made in sent_mix:
        made.wait()

    by_row = ref.by_row
    deep, band = 2 * modes, lats // WR * var_count
    for g in range(group_count):
        for p in range(procs):
            for r in range(WR):
                at = (r * group_count + g) * band
                by_row[p * deep : (p + 1) * deep, at : at + band] = coeff[
                    g, p, :, r * band : (r + 1) * band
                ]

    part, got, mid, far = ref.part, ref.got, ref.mid, ref.far
    grad_wide, direct = ref.grad_wide, ref.direct
    cuts = dims.cuts

    def near_copies(b, c):
        at = pl.ds(cuts[c][0], cuts[c][1])
        return [
            copy(
                part.at[b, peer, :, at],
                got.at[b, k, :, at],
                ref.s1.at[b, c, k],
                ref.r1.at[b, c, k],
                place("vars", peer, sizes),
            )
            for k, peer in enumerate(near)
        ]

    def away_copies(b, c):
        at = pl.ds(cuts[c][0], cuts[c][1])
        return [
            copy(
                mid.at[b, peer, at],
                far.at[b, k, at],
                ref.s2.at[b, c, k],
                ref.r2.at[b, c, k],
                place("loss", peer, sizes),
            )
            for k, peer in enumerate(away)
        ]

    def pass_on(b, c):
        for made in near_copies(b, c):
            made.wait()
        at = pl.ds(cuts[c][0], cuts[c][1])
        for j in range(loss_count):
            value = part[b, core, j, at].astype(F32)
            for k in range(core_count - 1):
                value = value + got[b, k, j, at].astype(F32)
            mid[b, j, at] = value.astype(BF16)
        for made in away_copies(b, c):
            made.start()

    mixer = mix[...].reshape(-1, width)
    span = 4 * var_count

    def block(b, carry):
        pieces = []
        for o in range(4):
            y = jnp.dot(f_rolled[b, o], by_row[...], preferred_element_type=F32)
            wide_span = y.shape[1] // WR
            pieces.append(
                jnp.concatenate(
                    [y[:, r * wide_span : (r + 1) * wide_span] for r in range(WR)], axis=0
                ).astype(BF16)
            )
        tiles = jnp.concatenate(pieces, axis=1)
        grad_out = jnp.dot(tiles, mixer, preferred_element_type=F32).astype(BF16)
        own_tiles = jnp.concatenate([piece[:, :span] for piece in pieces], axis=1)
        direct[...] = jnp.dot(own_tiles, ref.decoder[...], preferred_element_type=F32)

        @pl.when(b > 0)
        def _():
            for c in range(len(cuts)):
                pass_on(b - 1, c)

        grads = [[], [], []]
        for h in range(heads):
            q, k, v = (qkv[b, i * heads + h] for i in range(3))
            go = grad_out[:, h * HEAD : (h + 1) * HEAD]
            weights = soft[b, h]
            grads[2].append(
                lax.dot_general(
                    weights.astype(BF16), go, first, preferred_element_type=F32
                ).astype(BF16)
            )
            grad_weights = lax.dot_general(go, v, NT, preferred_element_type=F32)
            inner = jnp.sum(weights * grad_weights, axis=-1, keepdims=True)
            score_round = (weights * (grad_weights - inner) * scale).astype(BF16)
            grads[0].append(jnp.dot(score_round, k, preferred_element_type=F32).astype(BF16))
            grads[1].append(
                lax.dot_general(score_round, q, first, preferred_element_type=F32).astype(BF16)
            )
        stacked = jnp.concatenate(grads[0] + grads[1] + grads[2], axis=1)
        grad_wide[...] = jnp.dot(stacked, w_flat[...], preferred_element_type=F32)
        for c, (start, size) in enumerate(cuts):
            at = start
            while at < start + size:
                step = min(48, start + size - at)
                scaled = grad_wide[at : at + step] * gain
                normed = wide[b, at : at + step]
                local = inv[b, at : at + step, :1] * (
                    scaled
                    - jnp.mean(scaled, axis=-1, keepdims=True)
                    - normed * jnp.mean(scaled * normed, axis=-1, keepdims=True)
                )
                local = (local + direct[at : at + step]).astype(BF16)
                for l in range(loss_count):
                    for v in range(core_count):
                        lane = (l * core_count + v) * share
                        part[b, v, l, at : at + step] = local[:, lane : lane + share]
                at += step
            for made in near_copies(b, c):
                made.start()
        return carry

    lax.fori_loop(0, blocks, block, 0)
    for c in range(len(cuts)):
        pass_on(blocks - 1, c)
    outs = [jnp.zeros((col_count, share), F32) for _ in range(WR)]
    for b in range(blocks):
        for c in range(len(cuts)):
            for made in away_copies(b, c):
                made.wait()
        value = mid[b, loss].astype(F32)
        for k in range(loss_count - 1):
            value = value + far[b, k].astype(F32)
        value = value.astype(BF16)
        for r in range(WR):
            outs[r] = outs[r] + jnp.dot(back[b, r], value, preferred_element_type=F32)
    for r in range(WR):
        ref.input_grad[r] = outs[r].astype(BF16)


def fused(shift, inputs, sizes, cols, weight, lats, collective_id):
    procs = sizes["proc"]
    loss_count, core_count = sizes["loss"], sizes["vars"]
    group_count = loss_count * core_count
    modes, lat_all, _ = inputs.legendre.shape
    var_count = inputs.pred.shape[0] // lats
    each = var_count // procs
    half = 2 * var_count
    row_count, col_count, model = inputs.tokens.shape
    blocks = row_count // WR * col_count // cols
    rows = WR * cols
    width = inputs.wproj.shape[0] // group_count
    heads = width // HEAD
    share = model // group_count
    cut = rows // 2 // 16 * 16 + 16 if rows // 2 % 16 else rows // 2
    cuts = ((0, cut), (cut, rows - cut))
    dims = types.SimpleNamespace(
        procs=procs,
        modes=modes,
        vars=var_count,
        lats=lats,
        blocks=blocks,
        cols=cols,
        heads=heads,
        share=share,
        weight=weight,
        terms=LDEG * modes * procs,
        loads=tuple(vars(inputs)),
        cuts=cuts,
    )
    dma = pltpu.SemaphoreType.DMA
    band = lats * var_count
    outs = dict(
        amse=((1, var_count), F32),
        field_grad=((var_count * lats, LON), F32),
        input_grad=((row_count, col_count, share), BF16),
    )
    scratch = dict(
        y_out=((procs, 2 * modes, lats * half), BF16),
        y_in=((procs, 2 * modes, lats * half), BF16),
        x_wide=((procs * lats * half // 128 * 2 * modes, 128), F32),
        leg=(inputs.legendre.shape, BF16),
        harm=((modes, 2 * half, LDEG), F32),
        power=((procs, 3 * each, LDEG), F32),
        parts=((procs - 1, 3 * each, LDEG), F32),
        acc=((3 * each, LDEG), F32),
        terms_in=((procs, 3 * each, LDEG), F32),
        g_wide=((modes * lat_all, 128), F32),
        g_out=((procs, 2 * modes, band), BF16),
        coeff=((group_count, procs, 2 * modes, band), BF16),
        by_row=((2 * modes * procs, group_count * band), BF16),
        mix_out=((group_count, 4, 4 * var_count, width), BF16),
        mix=((4, group_count, 4 * var_count, width), BF16),
        wide=((blocks, rows, model), F32),
        inv=((blocks, rows, 128), F32),
        norm_out=((blocks, rows, model), BF16),
        qkv=((blocks, 3 * heads, rows, HEAD), BF16),
        soft=((blocks, heads, rows, rows), F32),
        f_rolled=((blocks, 4, cols, 2 * modes * procs), BF16),
        back=((blocks, WR, col_count, rows), BF16),
        grad_wide=((rows, model), F32),
        part=((blocks, core_count, loss_count, rows, share), BF16),
        direct=((rows, model), F32),
        decoder=((16 * var_count, model), BF16),
        got=((blocks, core_count - 1, loss_count, rows, share), BF16),
        mid=((blocks, loss_count, rows, share), BF16),
        far=((blocks, loss_count - 1, rows, share), BF16),
    )
    ring, spread, mates = (procs - 1,), (procs, group_count - 1), (group_count - 1,)
    near, away = (blocks, len(cuts), core_count - 1), (blocks, len(cuts), loss_count - 1)
    sems = dict(load_sems=(len(vars(inputs)),))
    sems.update(sy=ring, ry=ring, sa=ring, ra=ring, sb=ring, rb=ring, sc=ring, rc=ring)
    sems.update(sd=spread, rd=spread, sm=mates, rm=mates)
    sems.update(s1=near, r1=near, s2=away, r2=away)
    names = ["shift"] + [name + "_hbm" for name in vars(inputs)] + list(outs) + list(vars(inputs))
    names += list(scratch) + list(sems)
    return pl.pallas_call(
        functools.partial(fused_kernel, sizes, dims, tuple(names)),
        out_shape=tuple(jax.ShapeDtypeStruct(shape, kind) for shape, kind in outs.values()),
        in_specs=[pl.BlockSpec(memory_space=pltpu.SMEM)]
        + [pl.BlockSpec(memory_space=pl.ANY)] * len(vars(inputs)),
        out_specs=(VMEM,) * len(outs),
        scratch_shapes=[pltpu.VMEM(x.shape, x.dtype) for x in vars(inputs).values()]
        + [pltpu.VMEM(shape, kind) for shape, kind in scratch.values()]
        + [dma(shape) for shape in sems.values()],
        compiler_params=pltpu.CompilerParams(
            collective_id=collective_id,
            has_side_effects=True,
            vmem_limit_bytes=60 * 1024 * 1024,
        ),
        name="fused",
    )(shift, *vars(inputs).values())


def settle_kernel(count, *refs):
    for i in range(count):
        refs[count + i][...] = refs[i][...]


def settle(*arrays):
    count = len(arrays)
    return pl.pallas_call(
        functools.partial(settle_kernel, count),
        out_shape=tuple(jax.ShapeDtypeStruct(x.shape, x.dtype) for x in arrays),
        in_specs=[VMEM] * count,
        out_specs=(VMEM,) * count,
        name="settle",
    )(*arrays)


def body(tokens, shift, w_qkv, w_proj, ln_gain, w_dec, prediction, target, legendre):
    sizes = {name: lax.axis_size(name) for name in ("proc", "loss", "vars")}
    procs = sizes["proc"]
    group_count = sizes["loss"] * sizes["vars"]
    modes, lat_all, _ = legendre.shape
    var_count, lats = prediction.shape[0], prediction.shape[1]
    row_count, col_count, model = tokens.shape
    cols = 120
    fits = (
        row_count == WR
        and lats == 8
        and var_count == 16
        and modes == 16
        and lat_all == procs * lats
        and var_count % procs == 0
        and model % (128 * group_count) == 0
    )
    if not fits:
        return body_general(
            tokens, shift, w_qkv, w_proj, ln_gain, w_dec, prediction, target, legendre
        )
    modes_all = modes * procs
    weight = lat_all * LON / (VARS * LDEG * modes_all)
    rows = fourier_basis(modes_all).transpose(0, 2, 1).reshape(2, procs, modes, LON)
    rows = rows.transpose(1, 0, 2, 3).reshape(2 * modes_all, LON).astype(np.float32)
    high = rows.astype(jnp.bfloat16)
    low = (rows - high.astype(np.float32)).astype(jnp.bfloat16)
    inputs = types.SimpleNamespace(
        basis=jnp.asarray(np.stack([high, low])),
        pred=prediction.reshape(-1, LON),
        target=target.reshape(-1, LON),
        dec=w_dec.reshape(-1, 4, model),
        wproj=w_proj.reshape(-1, model),
        legendre=legendre,
        tokens=tokens,
        columns=jnp.asarray(rows.T.reshape(col_count, 4, -1).transpose(1, 0, 2), BF16),
        gain=ln_gain.reshape(-1, 128),
        w=w_qkv.transpose(1, 2, 3, 0).reshape(-1, model),
    )
    amse, field_grad, input_grad = settle(
        *fused(shift, inputs, sizes, cols, weight, lats, 7)
    )
    return (amse.reshape(-1), field_grad.reshape(var_count, lats, LON), input_grad)


def solution(mesh):
    return jax.shard_map(
        body,
        mesh=mesh,
        in_specs=(
            P("proc", None, None),
            P(),
            P(None, None, ("loss", "vars"), None),
            P(),
            P(),
            P(("loss", "vars"), None, None, None),
            P(("loss", "vars"), "proc", None),
            P(("loss", "vars"), "proc", None),
            P("proc", None, None),
        ),
        out_specs=(
            P(("loss", "vars")),
            P(("loss", "vars"), "proc", None),
            P("proc", None, ("loss", "vars")),
        ),
        check_vma=False,
    )
```

```python
import functools
import math
import types

import jax
import jax.numpy as jnp
import numpy as np
from jax import lax
from jax.experimental import pallas as pl
from jax.experimental.pallas import tpu as pltpu
from jax.sharding import PartitionSpec as P

HEAD = 96
VARS = 64
LON = 1440
LDEG = 384
WR = 2
WC = 12

EPSILON = 1e-06
NORM_EPSILON = 1e-05
HIGHEST = lax.Precision.HIGHEST
MESH = pl.DeviceIdType.MESH
F32 = jnp.float32
BF16 = jnp.bfloat16
VMEM = pl.BlockSpec(memory_space=pltpu.VMEM)
NT = (((1,), (1,)), ((), ()))


def fourier_basis(mode_count):
    column = np.arange(LON, dtype=np.int64)
    wavenumber = np.arange(mode_count, dtype=np.int64)
    phase = (column[:, None] * wavenumber[None, :] % LON) * (2.0 * math.pi / LON)
    return np.stack([np.cos(phase), -np.sin(phase)]) / math.sqrt(LON)


def amse_terms(power_pred, power_true, crossed):
    amp_pred = jnp.sqrt(power_pred + EPSILON)
    amp_true = jnp.sqrt(power_true + EPSILON)
    return (amp_pred - amp_true) ** 2 + 2.0 * jnp.maximum(power_pred, power_true) * (
        1.0 - crossed / (amp_pred * amp_true)
    )


def place(axis, index, sizes):
    proc, loss, var = (lax.axis_index(name) for name in ("proc", "loss", "vars"))
    if axis == "proc":
        return (index, loss, var)
    if axis == "loss":
        return (proc, index, var)
    if axis == "vars":
        return (proc, loss, index)
    return (proc, index // sizes["vars"], lax.rem(index, sizes["vars"]))


def rank(axis, sizes):
    if axis == "group":
        return lax.axis_index("loss") * sizes["vars"] + lax.axis_index("vars")
    return lax.axis_index(axis)


def greet(pairs):
    barrier = pltpu.get_barrier_semaphore()
    for device in pairs:
        pl.semaphore_signal(barrier, inc=1, device_id=device, device_id_type=MESH)
    pl.semaphore_wait(barrier, len(pairs))


def exchange_kernel(axis, count, sizes, spread, x_ref, out_ref, send, recv, own):
    me = rank(axis, sizes)
    peers = [lax.rem(me + k, count) for k in range(1, count)]
    greet([place(axis, peer, sizes) for peer in peers])
    copies = []
    for k, peer in enumerate(peers):
        copies.append(
            pltpu.make_async_remote_copy(
                src_ref=x_ref if spread else x_ref.at[peer],
                dst_ref=out_ref.at[k + 1] if spread else out_ref.at[me],
                send_sem=send.at[k],
                recv_sem=recv.at[k],
                device_id=place(axis, peer, sizes),
                device_id_type=MESH,
            )
        )
        copies[-1].start()
    if spread:
        local = pltpu.make_async_copy(x_ref, out_ref.at[0], own)
    else:
        local = pltpu.make_async_copy(x_ref.at[me], out_ref.at[me], own)
    local.start()
    local.wait()
    for copy in copies:
        copy.wait()


def exchange(x, axis, sizes, collective_id, spread=False):
    count = sizes["loss"] * sizes["vars"] if axis == "group" else sizes[axis]
    shape = (count,) + x.shape if spread else x.shape
    return pl.pallas_call(
        functools.partial(exchange_kernel, axis, count, sizes, spread),
        out_shape=jax.ShapeDtypeStruct(shape, x.dtype),
        in_specs=[VMEM],
        out_specs=VMEM,
        scratch_shapes=[
            pltpu.SemaphoreType.DMA((count - 1,)),
            pltpu.SemaphoreType.DMA((count - 1,)),
            pltpu.SemaphoreType.DMA,
        ],
        compiler_params=pltpu.CompilerParams(
            collective_id=collective_id, has_side_effects=True
        ),
        name="exchange_%d" % collective_id,
    )(x)


def harmonics_kernel(modes, var_count, spectra_ref, legendre_ref, harm_ref, power_ref):
    half = 2 * var_count
    sums = [jnp.zeros((half, LDEG), F32) for _ in range(3)]
    for m in range(modes):
        harm = jnp.dot(
            spectra_ref[m], legendre_ref[m], precision=HIGHEST, preferred_element_type=F32
        )
        harm_ref[m] = harm
        pred, true = harm[:half], harm[half:]
        sums = [sums[0] + pred * pred, sums[1] + true * true, sums[2] + pred * true]
    for i in range(3):
        power_ref[i] = sums[i][:var_count] + sums[i][var_count:]


def harmonics(spectra, legendre):
    modes, rows, _ = spectra.shape
    var_count = rows // 4
    return pl.pallas_call(
        functools.partial(harmonics_kernel, modes, var_count),
        out_shape=(
            jax.ShapeDtypeStruct((modes, rows, LDEG), F32),
            jax.ShapeDtypeStruct((3, var_count, LDEG), F32),
        ),
        in_specs=[VMEM, VMEM],
        out_specs=(VMEM, VMEM),
        name="harmonics",
    )(spectra, legendre)


def spectral_kernel(
    modes,
    sizes,
    var_count,
    weight,
    spectra_ref,
    legendre_ref,
    terms_ref,
    banded_ref,
    coeff_ref,
    harm,
    power,
    parts,
    acc,
    rows,
    outgoing,
    narrow,
    sa,
    ra,
    sb,
    rb,
    sc,
    rc,
    sd,
    rd,
):
    procs = sizes["proc"]
    group_count = sizes["loss"] * sizes["vars"]
    me, team = rank("proc", sizes), rank("group", sizes)
    peers = [lax.rem(me + k, procs) for k in range(1, procs)]
    mates = [lax.rem(team + k, group_count) for k in range(1, group_count)]
    greet(
        [place("proc", peer, sizes) for peer in peers]
        + [place("group", mate, sizes) for mate in mates]
    )
    half = 2 * var_count
    each = var_count // procs

    def copy(src, dst, send, recv, device):
        return pltpu.make_async_remote_copy(
            src_ref=src,
            dst_ref=dst,
            send_sem=send,
            recv_sem=recv,
            device_id=device,
            device_id_type=MESH,
        )

    sums = [jnp.zeros((half, LDEG), F32) for _ in range(3)]
    for m in range(modes):
        value = jnp.dot(
            spectra_ref[m], legendre_ref[m], precision=HIGHEST, preferred_element_type=F32
        )
        harm[m] = value
        pred, true = value[:half], value[half:]
        sums = [sums[0] + pred * pred, sums[1] + true * true, sums[2] + pred * true]
    for i in range(3):
        total = sums[i][:var_count] + sums[i][var_count:]
        for p in range(procs):
            power[p, i * each : (i + 1) * each] = total[p * each : (p + 1) * each]

    sent = [
        copy(power.at[peer], parts.at[k], sa.at[k], ra.at[k], place("proc", peer, sizes))
        for k, peer in enumerate(peers)
    ]
    for made in sent:
        made.start()
    for made in sent:
        made.wait()
    total = power[me]
    for k in range(procs - 1):
        total = total + parts[k]
    powers = [total[i * each : (i + 1) * each] for i in range(3)]
    terms, pullback = jax.vjp(amse_terms, *powers)
    grad_pred, _, grad_cross = pullback(jnp.full((each, LDEG), weight, F32))
    acc[...] = jnp.concatenate([2.0 * grad_pred, grad_cross, terms], axis=0)
    terms_ref[me] = acc[...]
    sent = [
        copy(acc, terms_ref.at[me], sb.at[k], rb.at[k], place("proc", peer, sizes))
        for k, peer in enumerate(peers)
    ]
    for made in sent:
        made.start()
    for made in sent:
        made.wait()
    gp = jnp.concatenate([terms_ref[p, :each] for p in range(procs)] * 2, axis=0)
    gc = jnp.concatenate([terms_ref[p, each : 2 * each] for p in range(procs)] * 2, axis=0)

    lats = legendre_ref.shape[1]
    own = lats // procs
    for m in range(modes):
        value = harm[m]
        grad = gp * value[:half] + gc * value[half:]
        rows[m * half : (m + 1) * half, :lats] = lax.dot_general(
            grad, legendre_ref[m], NT, precision=HIGHEST, preferred_element_type=F32
        )
    by_var = [rows[pl.ds(v, 2 * modes, stride=var_count), :] for v in range(var_count)]
    for q in range(procs):
        outgoing[q] = jnp.concatenate(
            [
                by_var[v][:, q * own + 4 * r : q * own + 4 * r + 4]
                for r in range(own // 4)
                for v in range(var_count)
            ],
            axis=1,
        )
    sent = [
        copy(outgoing.at[peer], banded_ref.at[me], sc.at[k], rc.at[k], place("proc", peer, sizes))
        for k, peer in enumerate(peers)
    ]
    for made in sent:
        made.start()
    banded_ref[me] = outgoing[me]

    passed = []
    for k in range(procs):
        source = lax.rem(me + procs - k, procs)
        if k > 0:
            sent[k - 1].wait_recv()
        value = banded_ref[source].astype(BF16)
        narrow[source] = value
        coeff_ref[0, source] = value
        for j, mate in enumerate(mates):
            passed.append(
                copy(
                    narrow.at[source],
                    coeff_ref.at[j + 1, source],
                    sd.at[k, j],
                    rd.at[k, j],
                    place("group", mate, sizes),
                )
            )
            passed[-1].start()
    for made in sent:
        made.wait_send()
    for made in passed:
        made.wait()


def spectral(spectra, legendre, sizes, weight, collective_id):
    procs = sizes["proc"]
    group_count = sizes["loss"] * sizes["vars"]
    modes, rows, lats = spectra.shape
    var_count = rows // 4
    each = var_count // procs
    block = (procs, 2 * modes, var_count * lats // procs)
    dma = pltpu.SemaphoreType.DMA
    return pl.pallas_call(
        functools.partial(spectral_kernel, modes, sizes, var_count, weight),
        out_shape=(
            jax.ShapeDtypeStruct((procs, 3 * each, LDEG), F32),
            jax.ShapeDtypeStruct(block, F32),
            jax.ShapeDtypeStruct((group_count,) + block, BF16),
        ),
        in_specs=[VMEM, VMEM],
        out_specs=(VMEM, VMEM, VMEM),
        scratch_shapes=[
            pltpu.VMEM((modes, rows, LDEG), F32),
            pltpu.VMEM((procs, 3 * each, LDEG), F32),
            pltpu.VMEM((procs - 1, 3 * each, LDEG), F32),
            pltpu.VMEM((3 * each, LDEG), F32),
            pltpu.VMEM((2 * modes * var_count, pl.cdiv(lats, 128) * 128), F32),
            pltpu.VMEM(block, F32),
            pltpu.VMEM(block, BF16),
        ]
        + [dma((procs - 1,)) for _ in range(6)]
        + [dma((procs, group_count - 1)) for _ in range(2)],
        compiler_params=pltpu.CompilerParams(
            collective_id=collective_id, has_side_effects=True
        ),
        name="spectral",
    )(spectra, legendre)


def attention_kernel(
    heads,
    cols,
    blocks,
    sizes,
    f_ref,
    coeff_ref,
    mix_ref,
    proj_ref,
    tok_ref,
    gain_ref,
    w_ref,
    out_ref,
    part,
    kept,
    got,
    mid,
    far,
    s1,
    r1,
    s2,
    r2,
):
    loss_count, var_count = sizes["loss"], sizes["vars"]
    loss, var = lax.axis_index("loss"), lax.axis_index("vars")
    near = [lax.rem(var + k, var_count) for k in range(1, var_count)]
    away = [lax.rem(loss + k, loss_count) for k in range(1, loss_count)]
    step = pl.program_id(0)
    rows = WR * cols

    @pl.when(step == 0)
    def _():
        greet(
            [place("vars", peer, sizes) for peer in near]
            + [place("loss", peer, sizes) for peer in away]
        )

    def near_copies(b):
        return [
            pltpu.make_async_remote_copy(
                src_ref=part.at[b, peer],
                dst_ref=got.at[b, k],
                send_sem=s1.at[b, k],
                recv_sem=r1.at[b, k],
                device_id=place("vars", peer, sizes),
                device_id_type=MESH,
            )
            for k, peer in enumerate(near)
        ]

    def away_copies(b):
        return [
            pltpu.make_async_remote_copy(
                src_ref=mid.at[b, peer],
                dst_ref=far.at[b, k],
                send_sem=s2.at[b, k],
                recv_sem=r2.at[b, k],
                device_id=place("loss", peer, sizes),
                device_id_type=MESH,
            )
            for k, peer in enumerate(away)
        ]

    def pass_on(b):
        for made in near_copies(b):
            made.wait()
        for j in range(loss_count):
            value = part[b, var, j].astype(F32)
            for k in range(var_count - 1):
                value = value + got[b, k, j].astype(F32)
            mid[b, j] = value.astype(BF16)
        for made in away_copies(b):
            made.start()

    pieces = []
    for o in range(4):
        y = jnp.dot(f_ref[o], coeff_ref[0], preferred_element_type=F32)
        half = y.shape[1] // WR
        pieces.append(
            jnp.concatenate([y[:, r * half : (r + 1) * half] for r in range(WR)], axis=0).astype(BF16)
        )
    tiles = jnp.concatenate(pieces, axis=1)
    mixed = jnp.dot(tiles, mix_ref[...], preferred_element_type=F32)
    width = heads * HEAD
    grad_out = mixed[:, :width].astype(BF16)
    kept[step] = mixed[:, width:]

    window_i = lax.rem(lax.broadcasted_iota(jnp.int32, (rows, rows), 0), cols) // WC
    window_j = lax.rem(lax.broadcasted_iota(jnp.int32, (rows, rows), 1), cols) // WC
    same = window_i == window_j
    scale = HEAD ** (-0.5)
    grads = [[], [], []]
    for h in range(heads):
        q, k, v = (
            proj_ref[0, :, (i * heads + h) * HEAD : (i * heads + h + 1) * HEAD] for i in range(3)
        )
        go = grad_out[:, h * HEAD : (h + 1) * HEAD]
        scores = lax.dot_general(q, k, NT, preferred_element_type=F32) * scale
        weights = jnp.where(same, jnp.exp(scores), 0.0)
        weights = weights / jnp.sum(weights, axis=-1, keepdims=True)
        rounded = weights.astype(BF16)
        first = (((0,), (0,)), ((), ()))
        grads[2].append(
            lax.dot_general(rounded, go, first, preferred_element_type=F32).astype(BF16)
        )
        grad_weights = lax.dot_general(go, v, NT, preferred_element_type=F32)
        inner = jnp.sum(weights * grad_weights, axis=-1, keepdims=True)
        score_round = (weights * (grad_weights - inner) * scale).astype(BF16)
        grads[0].append(jnp.dot(score_round, k, preferred_element_type=F32).astype(BF16))
        grads[1].append(
            lax.dot_general(score_round, q, first, preferred_element_type=F32).astype(BF16)
        )
    stacked = jnp.concatenate(grads[0] + grads[1] + grads[2], axis=1)
    grad_normed = lax.dot_general(stacked, w_ref[...], NT, preferred_element_type=F32)

    values = tok_ref[0].astype(F32)
    centred = values - jnp.mean(values, axis=-1, keepdims=True)
    inv_std = lax.rsqrt(jnp.mean(centred * centred, axis=-1, keepdims=True) + NORM_EPSILON)
    normed = centred * inv_std
    scaled = grad_normed * gain_ref[...]
    local = inv_std * (
        scaled
        - jnp.mean(scaled, axis=-1, keepdims=True)
        - normed * jnp.mean(scaled * normed, axis=-1, keepdims=True)
    )
    local = local.astype(BF16)
    share = local.shape[1] // (loss_count * var_count)
    for l in range(loss_count):
        for v in range(var_count):
            at = (l * var_count + v) * share
            part[step, v, l] = local[:, at : at + share]
    for made in near_copies(step):
        made.start()

    @pl.when(step > 0)
    def _():
        pass_on(step - 1)

    @pl.when(step == blocks - 1)
    def _():
        pass_on(blocks - 1)
        for b in range(blocks):
            for made in away_copies(b):
                made.wait()
            value = mid[b, loss].astype(F32)
            for k in range(loss_count - 1):
                value = value + far[b, k].astype(F32)
            out_ref[b] = value.astype(BF16)


def attention_backward(f_rolled, coeff, mix, projected, tokens, gain, w_flat, sizes, collective_id):
    blocks, rows, model = tokens.shape
    pairs = coeff.shape[0]
    cols = rows // WR
    per_pair = blocks // pairs
    depth = f_rolled.shape[2]
    width = projected.shape[2] // 3
    heads = width // HEAD
    loss_count, var_count = sizes["loss"], sizes["vars"]
    share = model // (loss_count * var_count)

    def whole(shape):
        return pl.BlockSpec(shape, lambda b: (0,) * len(shape))

    def per_block(shape):
        return pl.BlockSpec((1,) + shape, lambda b: (b,) + (0,) * len(shape))

    return pl.pallas_call(
        functools.partial(attention_kernel, heads, cols, blocks, sizes),
        grid=(blocks,),
        in_specs=[
            pl.BlockSpec((4, cols, depth), lambda b: (0, lax.rem(b, per_pair), 0)),
            pl.BlockSpec((1,) + coeff.shape[1:], lambda b: (b // per_pair, 0, 0)),
            whole(mix.shape),
            per_block((rows, 3 * width)),
            per_block((rows, model)),
            whole(gain.shape),
            whole(w_flat.shape),
        ],
        out_specs=whole((blocks, rows, share)),
        out_shape=jax.ShapeDtypeStruct((blocks, rows, share), BF16),
        scratch_shapes=[
            pltpu.VMEM((blocks, var_count, loss_count, rows, share), BF16),
            pltpu.VMEM((blocks, rows, share), F32),
            pltpu.VMEM((blocks, var_count - 1, loss_count, rows, share), BF16),
            pltpu.VMEM((blocks, loss_count, rows, share), BF16),
            pltpu.VMEM((blocks, loss_count - 1, rows, share), BF16),
            pltpu.SemaphoreType.DMA((blocks, var_count - 1)),
            pltpu.SemaphoreType.DMA((blocks, var_count - 1)),
            pltpu.SemaphoreType.DMA((blocks, loss_count - 1)),
            pltpu.SemaphoreType.DMA((blocks, loss_count - 1)),
        ],
        compiler_params=pltpu.CompilerParams(
            collective_id=collective_id, has_side_effects=True
        ),
        name="attention_backward",
    )(f_rolled, coeff, mix, projected, tokens, gain, w_flat)


def body_general(tokens, shift, w_qkv, w_proj, ln_gain, w_dec, prediction, target, legendre):
    sizes = {name: lax.axis_size(name) for name in ("proc", "loss", "vars")}
    procs = sizes["proc"]
    groups = (sizes["loss"], sizes["vars"])
    group_count = groups[0] * groups[1]
    modes = legendre.shape[0]
    lat_all = legendre.shape[1]
    modes_all = modes * procs
    var_count, lats = prediction.shape[0], prediction.shape[1]
    basis = fourier_basis(modes_all)
    row_count, col_count, model = tokens.shape
    offset = shift[0]
    head_local = w_qkv.shape[2]
    width = head_local * HEAD
    share = model // group_count

    ordered = basis.transpose(2, 0, 1).reshape(-1, LON)
    to_modes = jnp.asarray(ordered, F32)
    fields = jnp.concatenate([prediction.astype(F32), target]).reshape(-1, LON)
    spectra = lax.dot_general(to_modes, fields, NT, precision=HIGHEST)
    at_owner = exchange(spectra.reshape(procs, 2 * modes, -1), "proc", sizes, 1)
    at_owner = at_owner.reshape(procs, modes, 2, 2, var_count, lats).transpose(1, 3, 2, 4, 0, 5)
    at_owner = at_owner.reshape(modes, 4 * var_count, lat_all)
    weight_grad = lat_all * LON / (VARS * LDEG * modes_all)
    if var_count % procs == 0:
        terms, banded, coeff = spectral(at_owner, legendre, sizes, weight_grad, 2)
        each = var_count // procs
        degree_terms = terms[:, 2 * each :].reshape(var_count, LDEG)
    else:
        harm, power = harmonics(at_owner, legendre)
        power = lax.psum(power, "proc")
        degree_terms, pullback = jax.vjp(amse_terms, power[0], power[1], power[2])
        grad_pred, _, grad_cross = pullback(jnp.full(degree_terms.shape, weight_grad, F32))
        harm = harm.reshape(modes, 2, 2, var_count, LDEG)
        grad_harm = 2.0 * grad_pred * harm[:, 0] + grad_cross * harm[:, 1]
        grad_spectra = jnp.einsum("mcvl,mal->mcva", grad_harm, legendre, precision=HIGHEST)
        grad_spectra = grad_spectra.reshape(modes, 2, var_count, procs, lats // 4, 4)
        grad_spectra = grad_spectra.transpose(3, 0, 1, 4, 2, 5).reshape(procs, 2 * modes, -1)
        banded = exchange(grad_spectra, "proc", sizes, 3)
        coeff = exchange(banded.astype(BF16), "group", sizes, 4, spread=True)
    amse = jnp.sum(degree_terms, axis=-1) / (LDEG * modes_all)
    pairs = row_count // WR
    banded = banded.reshape(2 * modes_all, row_count, var_count, 4).transpose(0, 2, 1, 3)
    coeff = coeff.reshape(group_count, 2 * modes_all, pairs, WR, 4 * var_count)
    coeff = coeff.transpose(2, 1, 3, 0, 4).reshape(pairs, 2 * modes_all, -1)

    field_grad = lax.dot_general(
        banded.reshape(2 * modes_all, -1),
        to_modes,
        (((0,), (0,)), ((), ())),
        precision=HIGHEST,
    ).reshape(var_count, lats, LON)

    decoder = w_dec.transpose(2, 0, 1, 3).reshape(4 * var_count * 4, model)
    through = lax.dot_general(
        decoder, w_proj.reshape(-1, model), NT, preferred_element_type=F32
    ).astype(BF16)
    mix = jnp.concatenate(
        [
            through.reshape(-1, group_count, width),
            decoder.reshape(-1, group_count, share),
        ],
        axis=2,
    ).transpose(1, 0, 2)
    me = rank("group", sizes)
    received = [lax.dynamic_index_in_dim(mix, me, 0, keepdims=False)]
    for k in range(1, group_count):
        block = lax.dynamic_index_in_dim(mix, lax.rem(me + k, group_count), 0, keepdims=False)
        ring = [(g, (g + k) % group_count) for g in range(group_count)]
        received.append(lax.ppermute(block, ("loss", "vars"), ring))
    mix = jnp.stack(received)
    mix = mix.reshape(group_count, 4, 4 * var_count, width + share).transpose(1, 0, 2, 3)
    mix = mix.reshape(-1, width + share)

    cols = 120
    split = (pairs, WR, col_count // cols, cols)
    rolled = jnp.roll(tokens, -offset, axis=1)
    rolled = rolled.reshape(split + (model,)).transpose(0, 2, 1, 3, 4)
    rolled = rolled.reshape(-1, WR * cols, model)
    values = rolled.astype(F32)
    centred = values - jnp.mean(values, axis=-1, keepdims=True)
    inv_std = lax.rsqrt(jnp.mean(centred * centred, axis=-1, keepdims=True) + NORM_EPSILON)
    norm_out = (centred * inv_std * ln_gain).astype(BF16)
    w_flat = w_qkv.reshape(model, 3 * width)
    projected = jnp.einsum(
        "brd,dk->brk", norm_out, w_flat, preferred_element_type=F32
    ).astype(BF16)
    by_column = jnp.asarray(ordered.T.reshape(col_count, 4, -1).transpose(1, 0, 2), BF16)
    f_rolled = jnp.roll(by_column, -offset, axis=1)
    summed = attention_backward(
        f_rolled, coeff, mix, projected, rolled, ln_gain.reshape(1, model), w_flat, sizes, 6
    )
    summed = summed.reshape(pairs, col_count // cols, WR, cols, share).transpose(0, 2, 1, 3, 4)
    input_grad = jnp.roll(summed.reshape(row_count, col_count, share), offset, axis=1)
    return (amse, field_grad, input_grad)


def fused_kernel(sizes, dims, names, *refs):
    ref = types.SimpleNamespace(**dict(zip(names, refs)))
    procs, modes, var_count, lats = dims.procs, dims.modes, dims.vars, dims.lats
    loss_count, core_count = sizes["loss"], sizes["vars"]
    group_count = loss_count * core_count
    lat_all = procs * lats
    each = var_count // procs
    half = 2 * var_count
    fold = 128 // half
    strips = lats // fold
    blocks, cols, heads = dims.blocks, dims.cols, dims.heads
    rows = WR * cols
    width, share = heads * HEAD, dims.share
    me, team = rank("proc", sizes), rank("group", sizes)
    loss, core = lax.axis_index("loss"), lax.axis_index("vars")
    peers = [lax.rem(me + k, procs) for k in range(1, procs)]
    mates = [lax.rem(team + k, group_count) for k in range(1, group_count)]
    near = [lax.rem(core + k, core_count) for k in range(1, core_count)]
    away = [lax.rem(loss + k, loss_count) for k in range(1, loss_count)]
    first = (((0,), (0,)), ((), ()))

    barrier = pltpu.get_barrier_semaphore()
    places = [place("proc", peer, sizes) for peer in peers]
    mate_places = [place("group", mate, sizes) for mate in mates]
    cross_places = [(peer, 1 - loss, core) for peer in [me] + peers]
    for device in places + mate_places + cross_places[1:]:
        pl.semaphore_signal(barrier, inc=1, device_id=device, device_id_type=MESH)

    load = {}
    for i, name in enumerate(dims.loads):
        load[name] = pltpu.make_async_copy(
            getattr(ref, name + "_hbm"), getattr(ref, name), ref.load_sems.at[i]
        )
        load[name].start()
    load = types.SimpleNamespace(**load)

    def copy(src, dst, send, recv, device):
        return pltpu.make_async_remote_copy(
            src_ref=src,
            dst_ref=dst,
            send_sem=send,
            recv_sem=recv,
            device_id=device,
            device_id_type=MESH,
        )

    def permutation(count, source):
        i = lax.broadcasted_iota(jnp.int32, (count, count), 0)
        j = lax.broadcasted_iota(jnp.int32, (count, count), 1)
        return jnp.where(i == source(j), 1.0, 0.0).astype(BF16)

    y_out, y_in, basis = ref.y_out, ref.y_in, ref.basis
    by_lat = permutation(lats * half, lambda j: lax.rem(j, half) * lats + j // half)
    load.basis.wait()
    load.pred.wait()
    load.target.wait()
    both = jnp.concatenate([ref.pred[...], ref.target[...].astype(BF16)], axis=0)
    y = lax.dot_general(basis[0], both, NT, preferred_element_type=F32)
    y = y + lax.dot_general(basis[1], both, NT, preferred_element_type=F32)
    y = y.astype(BF16)
    y = jnp.dot(y, by_lat, preferred_element_type=F32)
    for p in range(procs):
        y_out[p] = y[p * 2 * modes : (p + 1) * 2 * modes].astype(BF16)
    pl.semaphore_wait(barrier, 2 * procs + group_count - 3)
    sent_y = [
        copy(y_out.at[peer], y_in.at[me], ref.sy.at[k], ref.ry.at[k], places[k])
        for k, peer in enumerate(peers)
    ]
    for made in sent_y:
        made.start()
    y_in[me] = y_out[me]

    wproj, mix_out, mix = ref.wproj, ref.mix_out, ref.mix
    count = 16 * var_count
    i = lax.broadcasted_iota(jnp.int32, (count, count), 0)
    j = lax.broadcasted_iota(jnp.int32, (count, count), 1)
    o, a, v = i // (4 * var_count), lax.rem(i // var_count, 4), lax.rem(i, var_count)
    order = jnp.where(j == v * 16 + a * 4 + o, 1.0, 0.0).astype(BF16)
    load.dec.wait()
    decoder = jnp.dot(
        order, ref.dec[...].reshape(count, -1), preferred_element_type=F32
    ).astype(BF16)
    ref.decoder[...] = decoder
    load.wproj.wait()
    for g in range(group_count):
        through = lax.dot_general(
            decoder, wproj[g * width : (g + 1) * width], NT, preferred_element_type=F32
        ).astype(BF16)
        for o in range(4):
            at = o * 4 * var_count
            mix_out[g, o] = through[at : at + 4 * var_count]
    sent_mix = [
        copy(
            mix_out.at[mate], mix.at[:, k + 1], ref.sm.at[k], ref.rm.at[k], mate_places[k]
        )
        for k, mate in enumerate(mates)
    ]
    for made in sent_mix:
        made.start()
    for o in range(4):
        mix[o, 0] = mix_out[team, o]

    leg, legendre = ref.leg, ref.legendre
    i = lax.broadcasted_iota(jnp.int32, (lat_all, lat_all), 0)
    j = lax.broadcasted_iota(jnp.int32, (lat_all, lat_all), 1)
    tall = lat_all // fold
    by_fold = jnp.where(j == lax.rem(i, tall) * fold + i // tall, 1.0, 0.0).astype(BF16)
    load.legendre.wait()
    for m in range(modes):
        leg[m] = jnp.dot(
            by_fold, legendre[m].astype(BF16), preferred_element_type=F32
        ).astype(BF16)

    tokens, wide, norm_out, qkv = ref.tokens, ref.wide, ref.norm_out, ref.qkv
    inv, w_flat, columns, f_rolled = ref.inv, ref.w, ref.columns, ref.f_rolled
    row_count, col_count = tokens.shape[0], tokens.shape[1]
    offset = lax.rem(ref.shift[0], col_count)
    for made in (load.tokens, load.gain, load.w, load.columns):
        made.wait()
    gain = jnp.concatenate(
        [ref.gain[i : i + 1] for i in range(ref.gain.shape[0])], axis=1
    )

    def roll(b):
        i = lax.broadcasted_iota(jnp.int32, (cols, col_count), 0) + (b * cols + offset)
        j = lax.broadcasted_iota(jnp.int32, (cols, col_count), 1)
        pick = jnp.where((i == j) | (i == j + col_count), 1.0, 0.0).astype(BF16)
        for r in range(row_count):
            wide[b, r * cols : (r + 1) * cols] = jnp.dot(
                pick, tokens[r], preferred_element_type=F32
            )
        for o in range(4):
            f_rolled[b, o] = jnp.dot(pick, columns[o], preferred_element_type=F32).astype(BF16)

    def normalise(b):
        step = 48
        for at in range(0, rows, step):
            part_rows = slice(at, at + step)
            values = wide[b, part_rows]
            centred = values - jnp.mean(values, axis=-1, keepdims=True)
            inv_std = lax.rsqrt(
                jnp.mean(centred * centred, axis=-1, keepdims=True) + NORM_EPSILON
            )
            normed = centred * inv_std
            wide[b, part_rows] = normed
            inv[b, part_rows] = jnp.broadcast_to(inv_std, (step, 128))
            norm_out[b, part_rows] = (normed * gain).astype(BF16)

    def project(b):
        projected = lax.dot_general(
            norm_out[b], w_flat[...], NT, preferred_element_type=F32
        ).astype(BF16)
        for i in range(3 * heads):
            qkv[b, i] = projected[:, i * HEAD : (i + 1) * HEAD]

    scale = HEAD ** (-0.5)
    soft = ref.soft
    window_i = lax.rem(lax.broadcasted_iota(jnp.int32, (rows, rows), 0), cols) // WC
    window_j = lax.rem(lax.broadcasted_iota(jnp.int32, (rows, rows), 1), cols) // WC
    same = window_i == window_j

    def attend(b):
        for h in range(heads):
            scores = (
                lax.dot_general(qkv[b, h], qkv[b, heads + h], NT, preferred_element_type=F32)
                * scale
            )
            weights = jnp.where(same, jnp.exp(scores), 0.0)
            soft[b, h] = weights / jnp.sum(weights, axis=-1, keepdims=True)

    back = ref.back

    def unroll(b):
        i = lax.broadcasted_iota(jnp.int32, (col_count, rows), 0)
        j = lax.broadcasted_iota(jnp.int32, (col_count, rows), 1)
        for r in range(WR):
            to = j - r * cols + b * cols + offset
            here = (j // cols == r) & ((to == i) | (to == i + col_count))
            back[b, r] = jnp.where(here, 1.0, 0.0).astype(BF16)

    for b in range(blocks):
        roll(b)

    x_wide, harm, power, parts = ref.x_wide, ref.harm, ref.power, ref.parts
    for made in sent_y:
        made.wait()
    for p in range(procs):
        for h in range(strips):
            at = (p * strips + h) * 2 * modes
            x_wide[at : at + 2 * modes] = y_in[p, :, h * 128 : (h + 1) * 128].astype(F32)
    power_sums = [jnp.zeros((var_count, LDEG), F32) for _ in range(3)]
    for m in range(modes):
        z = [x_wide[pl.ds(c * modes + m, tall, stride=2 * modes), :] for c in range(2)]
        x = jnp.concatenate(
            [
                jnp.concatenate([z[c][:, f * half : (f + 1) * half] for c in range(2)], axis=1)
                for f in range(fold)
            ],
            axis=0,
        ).astype(BF16)
        value = lax.dot_general(x, leg[m], first, preferred_element_type=F32)
        harm[m] = value
        for c in range(2):
            pred = value[c * half : c * half + var_count]
            true = value[c * half + var_count : (c + 1) * half]
            power_sums = [
                power_sums[0] + pred * pred,
                power_sums[1] + true * true,
                power_sums[2] + pred * true,
            ]
    for i in range(3):
        for p in range(procs):
            power[p, i * each : (i + 1) * each] = power_sums[i][p * each : (p + 1) * each]
    sent = [
        copy(power.at[peer], parts.at[k], ref.sa.at[k], ref.ra.at[k], places[k])
        for k, peer in enumerate(peers)
    ]
    for made in sent:
        made.start()
    for b in range(blocks):
        normalise(b)
    for b in range(blocks):
        project(b)
    for made in sent:
        made.wait()
    acc, terms_in = ref.acc, ref.terms_in
    total = power[me]
    for k in range(procs - 1):
        total = total + parts[k]
    powers = [total[i * each : (i + 1) * each] for i in range(3)]
    terms, pullback = jax.vjp(amse_terms, *powers)
    grad_pred, _, grad_cross = pullback(jnp.full((each, LDEG), dims.weight, F32))
    acc[...] = jnp.concatenate([2.0 * grad_pred, grad_cross, terms], axis=0)
    terms_in[me] = acc[...]
    sent = [
        copy(acc, terms_in.at[me], ref.sb.at[k], ref.rb.at[k], places[k])
        for k, peer in enumerate(peers)
    ]
    for made in sent:
        made.start()
    attend(0)
    attend(1)
    for made in sent:
        made.wait()
    gp = jnp.concatenate([terms_in[p, :each] for p in range(procs)], axis=0)
    gc = jnp.concatenate([terms_in[p, each : 2 * each] for p in range(procs)], axis=0)

    g_wide, g_out, coeff = ref.g_wide, ref.g_out, ref.coeff
    for m in range(modes):
        value = harm[m]
        grad = jnp.concatenate(
            [
                gp * value[c * half : c * half + var_count]
                + gc * value[c * half + var_count : (c + 1) * half]
                for c in range(2)
            ],
            axis=0,
        ).astype(BF16)
        g_wide[m * lat_all : (m + 1) * lat_all, :half] = lax.dot_general(
            leg[m], grad, NT, preferred_element_type=F32
        )
    for q in range(procs):
        pieces = []
        for a in range(lats):
            at = (a % fold) * tall + q * strips + a // fold
            pieces.append(g_wide[pl.ds(at, modes, stride=lat_all), :])
        g_out[q] = jnp.concatenate(
            [
                jnp.concatenate(
                    [piece[:, c * var_count : (c + 1) * var_count] for piece in pieces], axis=1
                )
                for c in range(2)
            ],
            axis=0,
        ).astype(BF16)
    crossing = [
        copy(
            g_out.at[peer], coeff.at[core_count, me], ref.se.at[k], ref.re.at[k], cross_places[k]
        )
        for k, peer in enumerate([me] + peers)
    ]
    sent = [
        copy(g_out.at[peer], coeff.at[0, me], ref.sc.at[k], ref.rc.at[k], places[k])
        for k, peer in enumerate(peers)
    ]
    crossing[0].start()
    for k in range(procs - 1):
        crossing[k + 1].start()
        sent[k].start()
    coeff[0, me] = g_out[me]
    for b in range(2, blocks):
        attend(b)
    for b in range(blocks):
        unroll(b)
    on_row = lax.broadcasted_iota(jnp.int32, (each, var_count), 0)
    on_col = lax.broadcasted_iota(jnp.int32, (each, var_count), 1)
    amse = jnp.zeros((1, var_count), F32)
    for p in range(procs):
        sums = jnp.sum(terms_in[p, 2 * each :], axis=-1, keepdims=True) / dims.terms
        spots = jnp.where(on_col == on_row + p * each, sums, 0.0)
        amse = amse + jnp.sum(spots, axis=0, keepdims=True)
    ref.amse[...] = amse

    for made in sent + crossing:
        made.wait_recv()
    other = (me, loss, 1 - core)
    passed = [
        copy(coeff.at[0], coeff.at[1 + 2 * core], ref.sd.at[0], ref.rd.at[0], other),
        copy(coeff.at[2], coeff.at[3 - 2 * core], ref.sd.at[1], ref.rd.at[1], other),
    ]
    for made in passed:
        made.start()
    own = jnp.concatenate([coeff[0, p] for p in range(procs)], axis=0)
    by_var = permutation(lats * var_count, lambda j: lax.rem(j, lats) * var_count + j // lats)
    own = jnp.dot(own, by_var, preferred_element_type=F32).astype(BF16)
    grid = lax.dot_general(own, basis[0], first, preferred_element_type=F32)
    ref.field_grad[...] = grid + lax.dot_general(
        own, basis[1], first, preferred_element_type=F32
    )
    for made in sent + crossing:
        made.wait_send()
    for made in passed:
        made.wait()
    for made in sent_mix:
        made.wait()

    by_row = ref.by_row
    deep, band = 2 * modes, lats // WR * var_count
    for g in range(group_count):
        for p in range(procs):
            for r in range(WR):
                at = (r * group_count + g) * band
                by_row[p * deep : (p + 1) * deep, at : at + band] = coeff[
                    g, p, :, r * band : (r + 1) * band
                ]

    part, got, mid, far = ref.part, ref.got, ref.mid, ref.far
    grad_wide, direct = ref.grad_wide, ref.direct
    cuts = dims.cuts

    def near_copies(b, c):
        at = pl.ds(cuts[c][0], cuts[c][1])
        return [
            copy(
                part.at[b, peer, :, at],
                got.at[b, k, :, at],
                ref.s1.at[b, c, k],
                ref.r1.at[b, c, k],
                place("vars", peer, sizes),
            )
            for k, peer in enumerate(near)
        ]

    def away_copies(b, c):
        at = pl.ds(cuts[c][0], cuts[c][1])
        return [
            copy(
                mid.at[b, peer, at],
                far.at[b, k, at],
                ref.s2.at[b, c, k],
                ref.r2.at[b, c, k],
                place("loss", peer, sizes),
            )
            for k, peer in enumerate(away)
        ]

    def pass_on(b, c):
        for made in near_copies(b, c):
            made.wait()
        at = pl.ds(cuts[c][0], cuts[c][1])
        for j in range(loss_count):
            value = part[b, core, j, at].astype(F32)
            for k in range(core_count - 1):
                value = value + got[b, k, j, at].astype(F32)
            mid[b, j, at] = value.astype(BF16)
        for made in away_copies(b, c):
            made.start()

    mixer = mix[...].reshape(-1, width)
    span = 4 * var_count

    def block(b):
        pieces = []
        for o in range(4):
            y = jnp.dot(f_rolled[b, o], by_row[...], preferred_element_type=F32)
            wide_span = y.shape[1] // WR
            pieces.append(
                jnp.concatenate(
                    [y[:, r * wide_span : (r + 1) * wide_span] for r in range(WR)], axis=0
                ).astype(BF16)
            )
        tiles = jnp.concatenate(pieces, axis=1)
        grad_out = jnp.dot(tiles, mixer, preferred_element_type=F32).astype(BF16)
        own_tiles = jnp.concatenate([piece[:, :span] for piece in pieces], axis=1)
        direct[...] = jnp.dot(own_tiles, ref.decoder[...], preferred_element_type=F32)

        if b > 0:
            for c in range(len(cuts)):
                pass_on(b - 1, c)

        grads = [[], [], []]
        for h in range(heads):
            q, k, v = (qkv[b, i * heads + h] for i in range(3))
            go = grad_out[:, h * HEAD : (h + 1) * HEAD]
            weights = soft[b, h]
            grads[2].append(
                lax.dot_general(
                    weights.astype(BF16), go, first, preferred_element_type=F32
                ).astype(BF16)
            )
            grad_weights = lax.dot_general(go, v, NT, preferred_element_type=F32)
            inner = jnp.sum(weights * grad_weights, axis=-1, keepdims=True)
            score_round = (weights * (grad_weights - inner) * scale).astype(BF16)
            grads[0].append(jnp.dot(score_round, k, preferred_element_type=F32).astype(BF16))
            grads[1].append(
                lax.dot_general(score_round, q, first, preferred_element_type=F32).astype(BF16)
            )
        stacked = jnp.concatenate(grads[0] + grads[1] + grads[2], axis=1)
        grad_wide[...] = jnp.dot(stacked, w_flat[...], preferred_element_type=F32)
        for c, (start, size) in enumerate(cuts):
            at = start
            while at < start + size:
                step = min(48, start + size - at)
                scaled = grad_wide[at : at + step] * gain
                normed = wide[b, at : at + step]
                local = inv[b, at : at + step, :1] * (
                    scaled
                    - jnp.mean(scaled, axis=-1, keepdims=True)
                    - normed * jnp.mean(scaled * normed, axis=-1, keepdims=True)
                )
                local = (local + direct[at : at + step]).astype(BF16)
                for l in range(loss_count):
                    for v in range(core_count):
                        lane = (l * core_count + v) * share
                        part[b, v, l, at : at + step] = local[:, lane : lane + share]
                at += step
            for made in near_copies(b, c):
                made.start()

    for b in range(blocks):
        block(b)
    for c in range(len(cuts)):
        pass_on(blocks - 1, c)
    outs = [jnp.zeros((col_count, share), F32) for _ in range(WR)]
    for b in range(blocks):
        for c in range(len(cuts)):
            for made in away_copies(b, c):
                made.wait()
        value = mid[b, loss].astype(F32)
        for k in range(loss_count - 1):
            value = value + far[b, k].astype(F32)
        value = value.astype(BF16)
        for r in range(WR):
            outs[r] = outs[r] + jnp.dot(back[b, r], value, preferred_element_type=F32)
    for r in range(WR):
        ref.input_grad[r] = outs[r].astype(BF16)


def fused(shift, inputs, sizes, cols, weight, lats, collective_id):
    procs = sizes["proc"]
    loss_count, core_count = sizes["loss"], sizes["vars"]
    group_count = loss_count * core_count
    modes, lat_all, _ = inputs.legendre.shape
    var_count = inputs.pred.shape[0] // lats
    each = var_count // procs
    half = 2 * var_count
    row_count, col_count, model = inputs.tokens.shape
    blocks = row_count // WR * col_count // cols
    rows = WR * cols
    width = inputs.wproj.shape[0] // group_count
    heads = width // HEAD
    share = model // group_count
    cut = rows // 2 // 16 * 16 + 16 if rows // 2 % 16 else rows // 2
    cuts = ((0, cut), (cut, rows - cut))
    dims = types.SimpleNamespace(
        procs=procs,
        modes=modes,
        vars=var_count,
        lats=lats,
        blocks=blocks,
        cols=cols,
        heads=heads,
        share=share,
        weight=weight,
        terms=LDEG * modes * procs,
        loads=tuple(vars(inputs)),
        cuts=cuts,
    )
    dma = pltpu.SemaphoreType.DMA
    band = lats * var_count
    outs = dict(
        amse=((1, var_count), F32),
        field_grad=((var_count * lats, LON), F32),
        input_grad=((row_count, col_count, share), BF16),
    )
    scratch = dict(
        y_out=((procs, 2 * modes, lats * half), BF16),
        y_in=((procs, 2 * modes, lats * half), BF16),
        x_wide=((procs * lats * half // 128 * 2 * modes, 128), F32),
        leg=(inputs.legendre.shape, BF16),
        harm=((modes, 2 * half, LDEG), F32),
        power=((procs, 3 * each, LDEG), F32),
        parts=((procs - 1, 3 * each, LDEG), F32),
        acc=((3 * each, LDEG), F32),
        terms_in=((procs, 3 * each, LDEG), F32),
        g_wide=((modes * lat_all, 128), F32),
        g_out=((procs, 2 * modes, band), BF16),
        coeff=((group_count, procs, 2 * modes, band), BF16),
        by_row=((2 * modes * procs, group_count * band), BF16),
        mix_out=((group_count, 4, 4 * var_count, width), BF16),
        mix=((4, group_count, 4 * var_count, width), BF16),
        wide=((blocks, rows, model), F32),
        inv=((blocks, rows, 128), F32),
        norm_out=((blocks, rows, model), BF16),
        qkv=((blocks, 3 * heads, rows, HEAD), BF16),
        soft=((blocks, heads, rows, rows), F32),
        f_rolled=((blocks, 4, cols, 2 * modes * procs), BF16),
        back=((blocks, WR, col_count, rows), BF16),
        grad_wide=((rows, model), F32),
        part=((blocks, core_count, loss_count, rows, share), BF16),
        direct=((rows, model), F32),
        decoder=((16 * var_count, model), BF16),
        got=((blocks, core_count - 1, loss_count, rows, share), BF16),
        mid=((blocks, loss_count, rows, share), BF16),
        far=((blocks, loss_count - 1, rows, share), BF16),
    )
    ring, mates = (procs - 1,), (group_count - 1,)
    near, away = (blocks, len(cuts), core_count - 1), (blocks, len(cuts), loss_count - 1)
    sems = dict(load_sems=(len(vars(inputs)),))
    sems.update(sy=ring, ry=ring, sa=ring, ra=ring, sb=ring, rb=ring, sc=ring, rc=ring)
    sems.update(sd=(2,), rd=(2,), se=(procs,), re=(procs,), sm=mates, rm=mates)
    sems.update(s1=near, r1=near, s2=away, r2=away)
    names = ["shift"] + [name + "_hbm" for name in vars(inputs)] + list(outs) + list(vars(inputs))
    names += list(scratch) + list(sems)
    return pl.pallas_call(
        functools.partial(fused_kernel, sizes, dims, tuple(names)),
        out_shape=tuple(jax.ShapeDtypeStruct(shape, kind) for shape, kind in outs.values()),
        in_specs=[pl.BlockSpec(memory_space=pltpu.SMEM)]
        + [pl.BlockSpec(memory_space=pl.ANY)] * len(vars(inputs)),
        out_specs=(VMEM,) * len(outs),
        scratch_shapes=[pltpu.VMEM(x.shape, x.dtype) for x in vars(inputs).values()]
        + [pltpu.VMEM(shape, kind) for shape, kind in scratch.values()]
        + [dma(shape) for shape in sems.values()],
        compiler_params=pltpu.CompilerParams(
            collective_id=collective_id,
            has_side_effects=True,
            vmem_limit_bytes=60 * 1024 * 1024,
        ),
        name="fused",
    )(shift, *vars(inputs).values())


def settle_kernel(count, *refs):
    for i in range(count):
        refs[count + i][...] = refs[i][...]


def settle(*arrays):
    count = len(arrays)
    return pl.pallas_call(
        functools.partial(settle_kernel, count),
        out_shape=tuple(jax.ShapeDtypeStruct(x.shape, x.dtype) for x in arrays),
        in_specs=[VMEM] * count,
        out_specs=(VMEM,) * count,
        name="settle",
    )(*arrays)


def body(tokens, shift, w_qkv, w_proj, ln_gain, w_dec, prediction, target, legendre):
    sizes = {name: lax.axis_size(name) for name in ("proc", "loss", "vars")}
    procs = sizes["proc"]
    group_count = sizes["loss"] * sizes["vars"]
    modes, lat_all, _ = legendre.shape
    var_count, lats = prediction.shape[0], prediction.shape[1]
    row_count, col_count, model = tokens.shape
    cols = 120
    fits = (
        row_count == WR
        and sizes["loss"] == 2
        and sizes["vars"] == 2
        and lats == 8
        and var_count == 16
        and modes == 16
        and lat_all == procs * lats
        and var_count % procs == 0
        and model % (128 * group_count) == 0
    )
    if not fits:
        return body_general(
            tokens, shift, w_qkv, w_proj, ln_gain, w_dec, prediction, target, legendre
        )
    modes_all = modes * procs
    weight = lat_all * LON / (VARS * LDEG * modes_all)
    rows = fourier_basis(modes_all).transpose(0, 2, 1).reshape(2, procs, modes, LON)
    rows = rows.transpose(1, 0, 2, 3).reshape(2 * modes_all, LON).astype(np.float32)
    high = rows.astype(jnp.bfloat16)
    low = (rows - high.astype(np.float32)).astype(jnp.bfloat16)
    inputs = types.SimpleNamespace(
        basis=jnp.asarray(np.stack([high, low])),
        pred=prediction.reshape(-1, LON),
        target=target.reshape(-1, LON),
        dec=w_dec.reshape(-1, 4, model),
        wproj=w_proj.reshape(-1, model),
        legendre=legendre,
        tokens=tokens,
        columns=jnp.asarray(rows.T.reshape(col_count, 4, -1).transpose(1, 0, 2), BF16),
        gain=ln_gain.reshape(-1, 128),
        w=w_qkv.transpose(1, 2, 3, 0).reshape(-1, model),
    )
    amse, field_grad, input_grad = settle(
        *fused(shift, inputs, sizes, cols, weight, lats, 7)
    )
    return (amse.reshape(-1), field_grad.reshape(var_count, lats, LON), input_grad)


def solution(mesh):
    return jax.shard_map(
        body,
        mesh=mesh,
        in_specs=(
            P("proc", None, None),
            P(),
            P(None, None, ("loss", "vars"), None),
            P(),
            P(),
            P(("loss", "vars"), None, None, None),
            P(("loss", "vars"), "proc", None),
            P(("loss", "vars"), "proc", None),
            P("proc", None, None),
        ),
        out_specs=(
            P(("loss", "vars")),
            P(("loss", "vars"), "proc", None),
            P("proc", None, ("loss", "vars")),
        ),
        check_vma=False,
    )
```

```python
import functools
import math
import types

import jax
import jax.numpy as jnp
import numpy as np
from jax import lax
from jax.experimental import pallas as pl
from jax.experimental.pallas import tpu as pltpu
from jax.sharding import PartitionSpec as P

HEAD = 96
VARS = 64
LON = 1440
LDEG = 384
WR = 2
WC = 12

EPSILON = 1e-06
NORM_EPSILON = 1e-05
HIGHEST = lax.Precision.HIGHEST
MESH = pl.DeviceIdType.MESH
F32 = jnp.float32
BF16 = jnp.bfloat16
VMEM = pl.BlockSpec(memory_space=pltpu.VMEM)
NT = (((1,), (1,)), ((), ()))


def fourier_basis(mode_count):
    column = np.arange(LON, dtype=np.int64)
    wavenumber = np.arange(mode_count, dtype=np.int64)
    phase = (column[:, None] * wavenumber[None, :] % LON) * (2.0 * math.pi / LON)
    return np.stack([np.cos(phase), -np.sin(phase)]) / math.sqrt(LON)


def amse_terms(power_pred, power_true, crossed):
    amp_pred = jnp.sqrt(power_pred + EPSILON)
    amp_true = jnp.sqrt(power_true + EPSILON)
    return (amp_pred - amp_true) ** 2 + 2.0 * jnp.maximum(power_pred, power_true) * (
        1.0 - crossed / (amp_pred * amp_true)
    )


def place(axis, index, sizes):
    proc, loss, var = (lax.axis_index(name) for name in ("proc", "loss", "vars"))
    if axis == "proc":
        return (index, loss, var)
    if axis == "loss":
        return (proc, index, var)
    if axis == "vars":
        return (proc, loss, index)
    return (proc, index // sizes["vars"], lax.rem(index, sizes["vars"]))


def rank(axis, sizes):
    if axis == "group":
        return lax.axis_index("loss") * sizes["vars"] + lax.axis_index("vars")
    return lax.axis_index(axis)


def greet(pairs):
    barrier = pltpu.get_barrier_semaphore()
    for device in pairs:
        pl.semaphore_signal(barrier, inc=1, device_id=device, device_id_type=MESH)
    pl.semaphore_wait(barrier, len(pairs))


def exchange_kernel(axis, count, sizes, spread, x_ref, out_ref, send, recv, own):
    me = rank(axis, sizes)
    peers = [lax.rem(me + k, count) for k in range(1, count)]
    greet([place(axis, peer, sizes) for peer in peers])
    copies = []
    for k, peer in enumerate(peers):
        copies.append(
            pltpu.make_async_remote_copy(
                src_ref=x_ref if spread else x_ref.at[peer],
                dst_ref=out_ref.at[k + 1] if spread else out_ref.at[me],
                send_sem=send.at[k],
                recv_sem=recv.at[k],
                device_id=place(axis, peer, sizes),
                device_id_type=MESH,
            )
        )
        copies[-1].start()
    if spread:
        local = pltpu.make_async_copy(x_ref, out_ref.at[0], own)
    else:
        local = pltpu.make_async_copy(x_ref.at[me], out_ref.at[me], own)
    local.start()
    local.wait()
    for copy in copies:
        copy.wait()


def exchange(x, axis, sizes, collective_id, spread=False):
    count = sizes["loss"] * sizes["vars"] if axis == "group" else sizes[axis]
    shape = (count,) + x.shape if spread else x.shape
    return pl.pallas_call(
        functools.partial(exchange_kernel, axis, count, sizes, spread),
        out_shape=jax.ShapeDtypeStruct(shape, x.dtype),
        in_specs=[VMEM],
        out_specs=VMEM,
        scratch_shapes=[
            pltpu.SemaphoreType.DMA((count - 1,)),
            pltpu.SemaphoreType.DMA((count - 1,)),
            pltpu.SemaphoreType.DMA,
        ],
        compiler_params=pltpu.CompilerParams(
            collective_id=collective_id, has_side_effects=True
        ),
        name="exchange_%d" % collective_id,
    )(x)


def harmonics_kernel(modes, var_count, spectra_ref, legendre_ref, harm_ref, power_ref):
    half = 2 * var_count
    sums = [jnp.zeros((half, LDEG), F32) for _ in range(3)]
    for m in range(modes):
        harm = jnp.dot(
            spectra_ref[m], legendre_ref[m], precision=HIGHEST, preferred_element_type=F32
        )
        harm_ref[m] = harm
        pred, true = harm[:half], harm[half:]
        sums = [sums[0] + pred * pred, sums[1] + true * true, sums[2] + pred * true]
    for i in range(3):
        power_ref[i] = sums[i][:var_count] + sums[i][var_count:]


def harmonics(spectra, legendre):
    modes, rows, _ = spectra.shape
    var_count = rows // 4
    return pl.pallas_call(
        functools.partial(harmonics_kernel, modes, var_count),
        out_shape=(
            jax.ShapeDtypeStruct((modes, rows, LDEG), F32),
            jax.ShapeDtypeStruct((3, var_count, LDEG), F32),
        ),
        in_specs=[VMEM, VMEM],
        out_specs=(VMEM, VMEM),
        name="harmonics",
    )(spectra, legendre)


def spectral_kernel(
    modes,
    sizes,
    var_count,
    weight,
    spectra_ref,
    legendre_ref,
    terms_ref,
    banded_ref,
    coeff_ref,
    harm,
    power,
    parts,
    acc,
    rows,
    outgoing,
    narrow,
    sa,
    ra,
    sb,
    rb,
    sc,
    rc,
    sd,
    rd,
):
    procs = sizes["proc"]
    group_count = sizes["loss"] * sizes["vars"]
    me, team = rank("proc", sizes), rank("group", sizes)
    peers = [lax.rem(me + k, procs) for k in range(1, procs)]
    mates = [lax.rem(team + k, group_count) for k in range(1, group_count)]
    greet(
        [place("proc", peer, sizes) for peer in peers]
        + [place("group", mate, sizes) for mate in mates]
    )
    half = 2 * var_count
    each = var_count // procs

    def copy(src, dst, send, recv, device):
        return pltpu.make_async_remote_copy(
            src_ref=src,
            dst_ref=dst,
            send_sem=send,
            recv_sem=recv,
            device_id=device,
            device_id_type=MESH,
        )

    sums = [jnp.zeros((half, LDEG), F32) for _ in range(3)]
    for m in range(modes):
        value = jnp.dot(
            spectra_ref[m], legendre_ref[m], precision=HIGHEST, preferred_element_type=F32
        )
        harm[m] = value
        pred, true = value[:half], value[half:]
        sums = [sums[0] + pred * pred, sums[1] + true * true, sums[2] + pred * true]
    for i in range(3):
        total = sums[i][:var_count] + sums[i][var_count:]
        for p in range(procs):
            power[p, i * each : (i + 1) * each] = total[p * each : (p + 1) * each]

    sent = [
        copy(power.at[peer], parts.at[k], sa.at[k], ra.at[k], place("proc", peer, sizes))
        for k, peer in enumerate(peers)
    ]
    for made in sent:
        made.start()
    for made in sent:
        made.wait()
    total = power[me]
    for k in range(procs - 1):
        total = total + parts[k]
    powers = [total[i * each : (i + 1) * each] for i in range(3)]
    terms, pullback = jax.vjp(amse_terms, *powers)
    grad_pred, _, grad_cross = pullback(jnp.full((each, LDEG), weight, F32))
    acc[...] = jnp.concatenate([2.0 * grad_pred, grad_cross, terms], axis=0)
    terms_ref[me] = acc[...]
    sent = [
        copy(acc, terms_ref.at[me], sb.at[k], rb.at[k], place("proc", peer, sizes))
        for k, peer in enumerate(peers)
    ]
    for made in sent:
        made.start()
    for made in sent:
        made.wait()
    gp = jnp.concatenate([terms_ref[p, :each] for p in range(procs)] * 2, axis=0)
    gc = jnp.concatenate([terms_ref[p, each : 2 * each] for p in range(procs)] * 2, axis=0)

    lats = legendre_ref.shape[1]
    own = lats // procs
    for m in range(modes):
        value = harm[m]
        grad = gp * value[:half] + gc * value[half:]
        rows[m * half : (m + 1) * half, :lats] = lax.dot_general(
            grad, legendre_ref[m], NT, precision=HIGHEST, preferred_element_type=F32
        )
    by_var = [rows[pl.ds(v, 2 * modes, stride=var_count), :] for v in range(var_count)]
    for q in range(procs):
        outgoing[q] = jnp.concatenate(
            [
                by_var[v][:, q * own + 4 * r : q * own + 4 * r + 4]
                for r in range(own // 4)
                for v in range(var_count)
            ],
            axis=1,
        )
    sent = [
        copy(outgoing.at[peer], banded_ref.at[me], sc.at[k], rc.at[k], place("proc", peer, sizes))
        for k, peer in enumerate(peers)
    ]
    for made in sent:
        made.start()
    banded_ref[me] = outgoing[me]

    passed = []
    for k in range(procs):
        source = lax.rem(me + procs - k, procs)
        if k > 0:
            sent[k - 1].wait_recv()
        value = banded_ref[source].astype(BF16)
        narrow[source] = value
        coeff_ref[0, source] = value
        for j, mate in enumerate(mates):
            passed.append(
                copy(
                    narrow.at[source],
                    coeff_ref.at[j + 1, source],
                    sd.at[k, j],
                    rd.at[k, j],
                    place("group", mate, sizes),
                )
            )
            passed[-1].start()
    for made in sent:
        made.wait_send()
    for made in passed:
        made.wait()


def spectral(spectra, legendre, sizes, weight, collective_id):
    procs = sizes["proc"]
    group_count = sizes["loss"] * sizes["vars"]
    modes, rows, lats = spectra.shape
    var_count = rows // 4
    each = var_count // procs
    block = (procs, 2 * modes, var_count * lats // procs)
    dma = pltpu.SemaphoreType.DMA
    return pl.pallas_call(
        functools.partial(spectral_kernel, modes, sizes, var_count, weight),
        out_shape=(
            jax.ShapeDtypeStruct((procs, 3 * each, LDEG), F32),
            jax.ShapeDtypeStruct(block, F32),
            jax.ShapeDtypeStruct((group_count,) + block, BF16),
        ),
        in_specs=[VMEM, VMEM],
        out_specs=(VMEM, VMEM, VMEM),
        scratch_shapes=[
            pltpu.VMEM((modes, rows, LDEG), F32),
            pltpu.VMEM((procs, 3 * each, LDEG), F32),
            pltpu.VMEM((procs - 1, 3 * each, LDEG), F32),
            pltpu.VMEM((3 * each, LDEG), F32),
            pltpu.VMEM((2 * modes * var_count, pl.cdiv(lats, 128) * 128), F32),
            pltpu.VMEM(block, F32),
            pltpu.VMEM(block, BF16),
        ]
        + [dma((procs - 1,)) for _ in range(6)]
        + [dma((procs, group_count - 1)) for _ in range(2)],
        compiler_params=pltpu.CompilerParams(
            collective_id=collective_id, has_side_effects=True
        ),
        name="spectral",
    )(spectra, legendre)


def attention_kernel(
    heads,
    cols,
    blocks,
    sizes,
    f_ref,
    coeff_ref,
    mix_ref,
    proj_ref,
    tok_ref,
    gain_ref,
    w_ref,
    out_ref,
    part,
    kept,
    got,
    mid,
    far,
    s1,
    r1,
    s2,
    r2,
):
    loss_count, var_count = sizes["loss"], sizes["vars"]
    loss, var = lax.axis_index("loss"), lax.axis_index("vars")
    near = [lax.rem(var + k, var_count) for k in range(1, var_count)]
    away = [lax.rem(loss + k, loss_count) for k in range(1, loss_count)]
    step = pl.program_id(0)
    rows = WR * cols

    @pl.when(step == 0)
    def _():
        greet(
            [place("vars", peer, sizes) for peer in near]
            + [place("loss", peer, sizes) for peer in away]
        )

    def near_copies(b):
        return [
            pltpu.make_async_remote_copy(
                src_ref=part.at[b, peer],
                dst_ref=got.at[b, k],
                send_sem=s1.at[b, k],
                recv_sem=r1.at[b, k],
                device_id=place("vars", peer, sizes),
                device_id_type=MESH,
            )
            for k, peer in enumerate(near)
        ]

    def away_copies(b):
        return [
            pltpu.make_async_remote_copy(
                src_ref=mid.at[b, peer],
                dst_ref=far.at[b, k],
                send_sem=s2.at[b, k],
                recv_sem=r2.at[b, k],
                device_id=place("loss", peer, sizes),
                device_id_type=MESH,
            )
            for k, peer in enumerate(away)
        ]

    def pass_on(b):
        for made in near_copies(b):
            made.wait()
        for j in range(loss_count):
            value = part[b, var, j].astype(F32)
            for k in range(var_count - 1):
                value = value + got[b, k, j].astype(F32)
            mid[b, j] = value.astype(BF16)
        for made in away_copies(b):
            made.start()

    pieces = []
    for o in range(4):
        y = jnp.dot(f_ref[o], coeff_ref[0], preferred_element_type=F32)
        half = y.shape[1] // WR
        pieces.append(
            jnp.concatenate([y[:, r * half : (r + 1) * half] for r in range(WR)], axis=0).astype(BF16)
        )
    tiles = jnp.concatenate(pieces, axis=1)
    mixed = jnp.dot(tiles, mix_ref[...], preferred_element_type=F32)
    width = heads * HEAD
    grad_out = mixed[:, :width].astype(BF16)
    kept[step] = mixed[:, width:]

    window_i = lax.rem(lax.broadcasted_iota(jnp.int32, (rows, rows), 0), cols) // WC
    window_j = lax.rem(lax.broadcasted_iota(jnp.int32, (rows, rows), 1), cols) // WC
    same = window_i == window_j
    scale = HEAD ** (-0.5)
    grads = [[], [], []]
    for h in range(heads):
        q, k, v = (
            proj_ref[0, :, (i * heads + h) * HEAD : (i * heads + h + 1) * HEAD] for i in range(3)
        )
        go = grad_out[:, h * HEAD : (h + 1) * HEAD]
        scores = lax.dot_general(q, k, NT, preferred_element_type=F32) * scale
        weights = jnp.where(same, jnp.exp(scores), 0.0)
        weights = weights / jnp.sum(weights, axis=-1, keepdims=True)
        rounded = weights.astype(BF16)
        first = (((0,), (0,)), ((), ()))
        grads[2].append(
            lax.dot_general(rounded, go, first, preferred_element_type=F32).astype(BF16)
        )
        grad_weights = lax.dot_general(go, v, NT, preferred_element_type=F32)
        inner = jnp.sum(weights * grad_weights, axis=-1, keepdims=True)
        score_round = (weights * (grad_weights - inner) * scale).astype(BF16)
        grads[0].append(jnp.dot(score_round, k, preferred_element_type=F32).astype(BF16))
        grads[1].append(
            lax.dot_general(score_round, q, first, preferred_element_type=F32).astype(BF16)
        )
    stacked = jnp.concatenate(grads[0] + grads[1] + grads[2], axis=1)
    grad_normed = lax.dot_general(stacked, w_ref[...], NT, preferred_element_type=F32)

    values = tok_ref[0].astype(F32)
    centred = values - jnp.mean(values, axis=-1, keepdims=True)
    inv_std = lax.rsqrt(jnp.mean(centred * centred, axis=-1, keepdims=True) + NORM_EPSILON)
    normed = centred * inv_std
    scaled = grad_normed * gain_ref[...]
    local = inv_std * (
        scaled
        - jnp.mean(scaled, axis=-1, keepdims=True)
        - normed * jnp.mean(scaled * normed, axis=-1, keepdims=True)
    )
    local = local.astype(BF16)
    share = local.shape[1] // (loss_count * var_count)
    for l in range(loss_count):
        for v in range(var_count):
            at = (l * var_count + v) * share
            part[step, v, l] = local[:, at : at + share]
    for made in near_copies(step):
        made.start()

    @pl.when(step > 0)
    def _():
        pass_on(step - 1)

    @pl.when(step == blocks - 1)
    def _():
        pass_on(blocks - 1)
        for b in range(blocks):
            for made in away_copies(b):
                made.wait()
            value = mid[b, loss].astype(F32)
            for k in range(loss_count - 1):
                value = value + far[b, k].astype(F32)
            out_ref[b] = value.astype(BF16)


def attention_backward(f_rolled, coeff, mix, projected, tokens, gain, w_flat, sizes, collective_id):
    blocks, rows, model = tokens.shape
    pairs = coeff.shape[0]
    cols = rows // WR
    per_pair = blocks // pairs
    depth = f_rolled.shape[2]
    width = projected.shape[2] // 3
    heads = width // HEAD
    loss_count, var_count = sizes["loss"], sizes["vars"]
    share = model // (loss_count * var_count)

    def whole(shape):
        return pl.BlockSpec(shape, lambda b: (0,) * len(shape))

    def per_block(shape):
        return pl.BlockSpec((1,) + shape, lambda b: (b,) + (0,) * len(shape))

    return pl.pallas_call(
        functools.partial(attention_kernel, heads, cols, blocks, sizes),
        grid=(blocks,),
        in_specs=[
            pl.BlockSpec((4, cols, depth), lambda b: (0, lax.rem(b, per_pair), 0)),
            pl.BlockSpec((1,) + coeff.shape[1:], lambda b: (b // per_pair, 0, 0)),
            whole(mix.shape),
            per_block((rows, 3 * width)),
            per_block((rows, model)),
            whole(gain.shape),
            whole(w_flat.shape),
        ],
        out_specs=whole((blocks, rows, share)),
        out_shape=jax.ShapeDtypeStruct((blocks, rows, share), BF16),
        scratch_shapes=[
            pltpu.VMEM((blocks, var_count, loss_count, rows, share), BF16),
            pltpu.VMEM((blocks, rows, share), F32),
            pltpu.VMEM((blocks, var_count - 1, loss_count, rows, share), BF16),
            pltpu.VMEM((blocks, loss_count, rows, share), BF16),
            pltpu.VMEM((blocks, loss_count - 1, rows, share), BF16),
            pltpu.SemaphoreType.DMA((blocks, var_count - 1)),
            pltpu.SemaphoreType.DMA((blocks, var_count - 1)),
            pltpu.SemaphoreType.DMA((blocks, loss_count - 1)),
            pltpu.SemaphoreType.DMA((blocks, loss_count - 1)),
        ],
        compiler_params=pltpu.CompilerParams(
            collective_id=collective_id, has_side_effects=True
        ),
        name="attention_backward",
    )(f_rolled, coeff, mix, projected, tokens, gain, w_flat)


def body_general(tokens, shift, w_qkv, w_proj, ln_gain, w_dec, prediction, target, legendre):
    sizes = {name: lax.axis_size(name) for name in ("proc", "loss", "vars")}
    procs = sizes["proc"]
    groups = (sizes["loss"], sizes["vars"])
    group_count = groups[0] * groups[1]
    modes = legendre.shape[0]
    lat_all = legendre.shape[1]
    modes_all = modes * procs
    var_count, lats = prediction.shape[0], prediction.shape[1]
    basis = fourier_basis(modes_all)
    row_count, col_count, model = tokens.shape
    offset = shift[0]
    head_local = w_qkv.shape[2]
    width = head_local * HEAD
    share = model // group_count

    ordered = basis.transpose(2, 0, 1).reshape(-1, LON)
    to_modes = jnp.asarray(ordered, F32)
    fields = jnp.concatenate([prediction.astype(F32), target]).reshape(-1, LON)
    spectra = lax.dot_general(to_modes, fields, NT, precision=HIGHEST)
    at_owner = exchange(spectra.reshape(procs, 2 * modes, -1), "proc", sizes, 1)
    at_owner = at_owner.reshape(procs, modes, 2, 2, var_count, lats).transpose(1, 3, 2, 4, 0, 5)
    at_owner = at_owner.reshape(modes, 4 * var_count, lat_all)
    weight_grad = lat_all * LON / (VARS * LDEG * modes_all)
    if var_count % procs == 0:
        terms, banded, coeff = spectral(at_owner, legendre, sizes, weight_grad, 2)
        each = var_count // procs
        degree_terms = terms[:, 2 * each :].reshape(var_count, LDEG)
    else:
        harm, power = harmonics(at_owner, legendre)
        power = lax.psum(power, "proc")
        degree_terms, pullback = jax.vjp(amse_terms, power[0], power[1], power[2])
        grad_pred, _, grad_cross = pullback(jnp.full(degree_terms.shape, weight_grad, F32))
        harm = harm.reshape(modes, 2, 2, var_count, LDEG)
        grad_harm = 2.0 * grad_pred * harm[:, 0] + grad_cross * harm[:, 1]
        grad_spectra = jnp.einsum("mcvl,mal->mcva", grad_harm, legendre, precision=HIGHEST)
        grad_spectra = grad_spectra.reshape(modes, 2, var_count, procs, lats // 4, 4)
        grad_spectra = grad_spectra.transpose(3, 0, 1, 4, 2, 5).reshape(procs, 2 * modes, -1)
        banded = exchange(grad_spectra, "proc", sizes, 3)
        coeff = exchange(banded.astype(BF16), "group", sizes, 4, spread=True)
    amse = jnp.sum(degree_terms, axis=-1) / (LDEG * modes_all)
    pairs = row_count // WR
    banded = banded.reshape(2 * modes_all, row_count, var_count, 4).transpose(0, 2, 1, 3)
    coeff = coeff.reshape(group_count, 2 * modes_all, pairs, WR, 4 * var_count)
    coeff = coeff.transpose(2, 1, 3, 0, 4).reshape(pairs, 2 * modes_all, -1)

    field_grad = lax.dot_general(
        banded.reshape(2 * modes_all, -1),
        to_modes,
        (((0,), (0,)), ((), ())),
        precision=HIGHEST,
    ).reshape(var_count, lats, LON)

    decoder = w_dec.transpose(2, 0, 1, 3).reshape(4 * var_count * 4, model)
    through = lax.dot_general(
        decoder, w_proj.reshape(-1, model), NT, preferred_element_type=F32
    ).astype(BF16)
    mix = jnp.concatenate(
        [
            through.reshape(-1, group_count, width),
            decoder.reshape(-1, group_count, share),
        ],
        axis=2,
    ).transpose(1, 0, 2)
    me = rank("group", sizes)
    received = [lax.dynamic_index_in_dim(mix, me, 0, keepdims=False)]
    for k in range(1, group_count):
        block = lax.dynamic_index_in_dim(mix, lax.rem(me + k, group_count), 0, keepdims=False)
        ring = [(g, (g + k) % group_count) for g in range(group_count)]
        received.append(lax.ppermute(block, ("loss", "vars"), ring))
    mix = jnp.stack(received)
    mix = mix.reshape(group_count, 4, 4 * var_count, width + share).transpose(1, 0, 2, 3)
    mix = mix.reshape(-1, width + share)

    cols = 120
    split = (pairs, WR, col_count // cols, cols)
    rolled = jnp.roll(tokens, -offset, axis=1)
    rolled = rolled.reshape(split + (model,)).transpose(0, 2, 1, 3, 4)
    rolled = rolled.reshape(-1, WR * cols, model)
    values = rolled.astype(F32)
    centred = values - jnp.mean(values, axis=-1, keepdims=True)
    inv_std = lax.rsqrt(jnp.mean(centred * centred, axis=-1, keepdims=True) + NORM_EPSILON)
    norm_out = (centred * inv_std * ln_gain).astype(BF16)
    w_flat = w_qkv.reshape(model, 3 * width)
    projected = jnp.einsum(
        "brd,dk->brk", norm_out, w_flat, preferred_element_type=F32
    ).astype(BF16)
    by_column = jnp.asarray(ordered.T.reshape(col_count, 4, -1).transpose(1, 0, 2), BF16)
    f_rolled = jnp.roll(by_column, -offset, axis=1)
    summed = attention_backward(
        f_rolled, coeff, mix, projected, rolled, ln_gain.reshape(1, model), w_flat, sizes, 6
    )
    summed = summed.reshape(pairs, col_count // cols, WR, cols, share).transpose(0, 2, 1, 3, 4)
    input_grad = jnp.roll(summed.reshape(row_count, col_count, share), offset, axis=1)
    return (amse, field_grad, input_grad)


def fused_kernel(sizes, dims, names, *refs):
    ref = types.SimpleNamespace(**dict(zip(names, refs)))
    procs, modes, var_count, lats = dims.procs, dims.modes, dims.vars, dims.lats
    loss_count, core_count = sizes["loss"], sizes["vars"]
    group_count = loss_count * core_count
    lat_all = procs * lats
    each = var_count // procs
    half = 2 * var_count
    fold = 128 // half
    strips = lats // fold
    blocks, cols, heads = dims.blocks, dims.cols, dims.heads
    rows = WR * cols
    width, share = heads * HEAD, dims.share
    me, team = rank("proc", sizes), rank("group", sizes)
    loss, core = lax.axis_index("loss"), lax.axis_index("vars")
    peers = [lax.rem(me + k, procs) for k in range(1, procs)]
    mates = [lax.rem(team + k, group_count) for k in range(1, group_count)]
    near = [lax.rem(core + k, core_count) for k in range(1, core_count)]
    away = [lax.rem(loss + k, loss_count) for k in range(1, loss_count)]
    first = (((0,), (0,)), ((), ()))

    barrier = pltpu.get_barrier_semaphore()
    places = [place("proc", peer, sizes) for peer in peers]
    mate_places = [place("group", mate, sizes) for mate in mates]
    cross_places = [(peer, 1 - loss, core) for peer in [me] + peers]
    for device in places + mate_places + cross_places[1:]:
        pl.semaphore_signal(barrier, inc=1, device_id=device, device_id_type=MESH)

    load = {}
    for i, name in enumerate(dims.loads):
        load[name] = pltpu.make_async_copy(
            getattr(ref, name + "_hbm"), getattr(ref, name), ref.load_sems.at[i]
        )
        load[name].start()
    load = types.SimpleNamespace(**load)

    def copy(src, dst, send, recv, device):
        return pltpu.make_async_remote_copy(
            src_ref=src,
            dst_ref=dst,
            send_sem=send,
            recv_sem=recv,
            device_id=device,
            device_id_type=MESH,
        )

    def permutation(count, source):
        i = lax.broadcasted_iota(jnp.int32, (count, count), 0)
        j = lax.broadcasted_iota(jnp.int32, (count, count), 1)
        return jnp.where(i == source(j), 1.0, 0.0).astype(BF16)

    y_out, y_in, basis = ref.y_out, ref.y_in, ref.basis
    by_lat = permutation(lats * half, lambda j: lax.rem(j, half) * lats + j // half)
    load.basis.wait()
    load.pred.wait()
    load.target.wait()
    both = jnp.concatenate([ref.pred[...], ref.target[...].astype(BF16)], axis=0)
    y = lax.dot_general(basis[0], both, NT, preferred_element_type=F32)
    y = y.astype(BF16)
    y = jnp.dot(y, by_lat, preferred_element_type=F32)
    for p in range(procs):
        y_out[p] = y[p * 2 * modes : (p + 1) * 2 * modes].astype(BF16)
    pl.semaphore_wait(barrier, 2 * procs + group_count - 3)
    sent_y = [
        copy(y_out.at[peer], y_in.at[me], ref.sy.at[k], ref.ry.at[k], places[k])
        for k, peer in enumerate(peers)
    ]
    for made in sent_y:
        made.start()
    y_in[me] = y_out[me]

    wproj, mix_out, mix = ref.wproj, ref.mix_out, ref.mix
    count = 16 * var_count
    i = lax.broadcasted_iota(jnp.int32, (count, count), 0)
    j = lax.broadcasted_iota(jnp.int32, (count, count), 1)
    o, a, v = i // (4 * var_count), lax.rem(i // var_count, 4), lax.rem(i, var_count)
    order = jnp.where(j == v * 16 + a * 4 + o, 1.0, 0.0).astype(BF16)
    load.dec.wait()
    decoder = jnp.dot(
        order, ref.dec[...].reshape(count, -1), preferred_element_type=F32
    ).astype(BF16)
    ref.decoder[...] = decoder
    load.wproj.wait()
    for g in range(group_count):
        through = lax.dot_general(
            decoder, wproj[g * width : (g + 1) * width], NT, preferred_element_type=F32
        ).astype(BF16)
        for o in range(4):
            at = o * 4 * var_count
            mix_out[g, o] = through[at : at + 4 * var_count]
    sent_mix = [
        copy(
            mix_out.at[mate], mix.at[:, k + 1], ref.sm.at[k], ref.rm.at[k], mate_places[k]
        )
        for k, mate in enumerate(mates)
    ]
    for made in sent_mix:
        made.start()
    for o in range(4):
        mix[o, 0] = mix_out[team, o]

    leg, legendre = ref.leg, ref.legendre
    i = lax.broadcasted_iota(jnp.int32, (lat_all, lat_all), 0)
    j = lax.broadcasted_iota(jnp.int32, (lat_all, lat_all), 1)
    tall = lat_all // fold
    by_fold = jnp.where(j == lax.rem(i, tall) * fold + i // tall, 1.0, 0.0).astype(BF16)
    load.legendre.wait()
    for m in range(modes):
        leg[m] = jnp.dot(
            by_fold, legendre[m].astype(BF16), preferred_element_type=F32
        ).astype(BF16)

    tokens, wide, norm_out, qkv = ref.tokens, ref.wide, ref.norm_out, ref.qkv
    inv, w_flat, columns, f_rolled = ref.inv, ref.w, ref.columns, ref.f_rolled
    row_count, col_count = tokens.shape[0], tokens.shape[1]
    offset = lax.rem(ref.shift[0], col_count)
    for made in (load.tokens, load.gain, load.w, load.columns):
        made.wait()
    gain = jnp.concatenate(
        [ref.gain[i : i + 1] for i in range(ref.gain.shape[0])], axis=1
    )

    def roll(b):
        i = lax.broadcasted_iota(jnp.int32, (cols, col_count), 0) + (b * cols + offset)
        j = lax.broadcasted_iota(jnp.int32, (cols, col_count), 1)
        pick = jnp.where((i == j) | (i == j + col_count), 1.0, 0.0).astype(BF16)
        for r in range(row_count):
            wide[b, r * cols : (r + 1) * cols] = jnp.dot(
                pick, tokens[r], preferred_element_type=F32
            )
        f_rolled[b] = jnp.concatenate(
            [jnp.dot(pick, columns[o], preferred_element_type=F32) for o in range(4)], axis=0
        ).astype(BF16)

    def normalise(b):
        step = 48
        for at in range(0, rows, step):
            part_rows = slice(at, at + step)
            values = wide[b, part_rows]
            centred = values - jnp.mean(values, axis=-1, keepdims=True)
            inv_std = lax.rsqrt(
                jnp.mean(centred * centred, axis=-1, keepdims=True) + NORM_EPSILON
            )
            normed = centred * inv_std
            wide[b, part_rows] = normed
            inv[b, part_rows] = jnp.broadcast_to(inv_std, (step, 128))
            norm_out[b, part_rows] = (normed * gain).astype(BF16)

    def project(b):
        projected = lax.dot_general(
            norm_out[b], w_flat[...], NT, preferred_element_type=F32
        ).astype(BF16)
        for i in range(3 * heads):
            qkv[b, i] = projected[:, i * HEAD : (i + 1) * HEAD]

    scale = HEAD ** (-0.5)
    soft = ref.soft
    window_i = lax.rem(lax.broadcasted_iota(jnp.int32, (rows, rows), 0), cols) // WC
    window_j = lax.rem(lax.broadcasted_iota(jnp.int32, (rows, rows), 1), cols) // WC
    same = window_i == window_j

    def attend(b):
        for h in range(heads):
            scores = (
                lax.dot_general(qkv[b, h], qkv[b, heads + h], NT, preferred_element_type=F32)
                * scale
            )
            weights = jnp.where(same, jnp.exp(scores), 0.0)
            soft[b, h] = weights / jnp.sum(weights, axis=-1, keepdims=True)

    back = ref.back

    def unroll(b):
        i = lax.broadcasted_iota(jnp.int32, (col_count, rows), 0)
        j = lax.broadcasted_iota(jnp.int32, (col_count, rows), 1)
        for r in range(WR):
            to = j - r * cols + b * cols + offset
            here = (j // cols == r) & ((to == i) | (to == i + col_count))
            back[b, r] = jnp.where(here, 1.0, 0.0).astype(BF16)

    for b in range(blocks):
        roll(b)

    x_wide, harm, power, parts = ref.x_wide, ref.harm, ref.power, ref.parts
    for made in sent_y:
        made.wait()
    for p in range(procs):
        for h in range(strips):
            at = (p * strips + h) * 2 * modes
            x_wide[at : at + 2 * modes] = y_in[p, :, h * 128 : (h + 1) * 128].astype(F32)
    power_sums = [jnp.zeros((var_count, LDEG), F32) for _ in range(3)]
    for m in range(modes):
        z = [x_wide[pl.ds(c * modes + m, tall, stride=2 * modes), :] for c in range(2)]
        x = jnp.concatenate(
            [
                jnp.concatenate([z[c][:, f * half : (f + 1) * half] for c in range(2)], axis=1)
                for f in range(fold)
            ],
            axis=0,
        ).astype(BF16)
        value = lax.dot_general(x, leg[m], first, preferred_element_type=F32)
        harm[m] = value
        for c in range(2):
            pred = value[c * half : c * half + var_count]
            true = value[c * half + var_count : (c + 1) * half]
            power_sums = [
                power_sums[0] + pred * pred,
                power_sums[1] + true * true,
                power_sums[2] + pred * true,
            ]
    for i in range(3):
        for p in range(procs):
            power[p, i * each : (i + 1) * each] = power_sums[i][p * each : (p + 1) * each]
    sent = [
        copy(power.at[peer], parts.at[k], ref.sa.at[k], ref.ra.at[k], places[k])
        for k, peer in enumerate(peers)
    ]
    for made in sent:
        made.start()
    for b in range(blocks):
        normalise(b)
    for b in range(blocks):
        project(b)
    for made in sent:
        made.wait()
    acc, terms_in = ref.acc, ref.terms_in
    total = power[me]
    for k in range(procs - 1):
        total = total + parts[k]
    powers = [total[i * each : (i + 1) * each] for i in range(3)]
    terms, pullback = jax.vjp(amse_terms, *powers)
    grad_pred, _, grad_cross = pullback(jnp.full((each, LDEG), dims.weight, F32))
    acc[...] = jnp.concatenate([2.0 * grad_pred, grad_cross, terms], axis=0)
    terms_in[me] = acc[...]
    sent = [
        copy(acc, terms_in.at[me], ref.sb.at[k], ref.rb.at[k], places[k])
        for k, peer in enumerate(peers)
    ]
    for made in sent:
        made.start()
    attend(0)
    attend(1)
    for made in sent:
        made.wait()
    gp = jnp.concatenate([terms_in[p, :each] for p in range(procs)], axis=0)
    gc = jnp.concatenate([terms_in[p, each : 2 * each] for p in range(procs)], axis=0)

    g_wide, g_out, coeff = ref.g_wide, ref.g_out, ref.coeff
    for m in range(modes):
        value = harm[m]
        grad = jnp.concatenate(
            [
                gp * value[c * half : c * half + var_count]
                + gc * value[c * half + var_count : (c + 1) * half]
                for c in range(2)
            ],
            axis=0,
        ).astype(BF16)
        g_wide[m * lat_all : (m + 1) * lat_all, :half] = lax.dot_general(
            leg[m], grad, NT, preferred_element_type=F32
        )
    for q in range(procs):
        pieces = []
        for a in range(lats):
            at = (a % fold) * tall + q * strips + a // fold
            pieces.append(g_wide[pl.ds(at, modes, stride=lat_all), :])
        g_out[q] = jnp.concatenate(
            [
                jnp.concatenate(
                    [piece[:, c * var_count : (c + 1) * var_count] for piece in pieces], axis=1
                )
                for c in range(2)
            ],
            axis=0,
        ).astype(BF16)
    crossing = [
        copy(
            g_out.at[peer], coeff.at[core_count, me], ref.se.at[k], ref.re.at[k], cross_places[k]
        )
        for k, peer in enumerate([me] + peers)
    ]
    sent = [
        copy(g_out.at[peer], coeff.at[0, me], ref.sc.at[k], ref.rc.at[k], places[k])
        for k, peer in enumerate(peers)
    ]
    crossing[0].start()
    for k in range(procs - 1):
        crossing[k + 1].start()
        sent[k].start()
    coeff[0, me] = g_out[me]
    for b in range(2, blocks):
        attend(b)
    for b in range(blocks):
        unroll(b)
    on_row = lax.broadcasted_iota(jnp.int32, (each, var_count), 0)
    on_col = lax.broadcasted_iota(jnp.int32, (each, var_count), 1)
    amse = jnp.zeros((1, var_count), F32)
    for p in range(procs):
        sums = jnp.sum(terms_in[p, 2 * each :], axis=-1, keepdims=True) / dims.terms
        spots = jnp.where(on_col == on_row + p * each, sums, 0.0)
        amse = amse + jnp.sum(spots, axis=0, keepdims=True)
    ref.amse[...] = amse

    for made in sent + crossing:
        made.wait_recv()
    other = (me, loss, 1 - core)
    passed = [
        copy(coeff.at[0], coeff.at[1 + 2 * core], ref.sd.at[0], ref.rd.at[0], other),
        copy(coeff.at[2], coeff.at[3 - 2 * core], ref.sd.at[1], ref.rd.at[1], other),
    ]
    for made in passed:
        made.start()
    own = jnp.concatenate([coeff[0, p] for p in range(procs)], axis=0)
    by_var = permutation(lats * var_count, lambda j: lax.rem(j, lats) * var_count + j // lats)
    own = jnp.dot(own, by_var, preferred_element_type=F32).astype(BF16)
    grid = lax.dot_general(own, basis[0], first, preferred_element_type=F32)
    ref.grid[...] = grid
    settled = pltpu.make_async_copy(ref.grid, ref.field_grad, ref.grid_sem)
    settled.start()
    for made in sent + crossing:
        made.wait_send()
    for made in passed:
        made.wait()
    for made in sent_mix:
        made.wait()

    by_row = ref.by_row
    deep, band = 2 * modes, lats // WR * var_count
    for g in range(group_count):
        for p in range(procs):
            for r in range(WR):
                at = (r * group_count + g) * band
                by_row[p * deep : (p + 1) * deep, at : at + band] = coeff[
                    g, p, :, r * band : (r + 1) * band
                ]

    part, got, mid, far = ref.part, ref.got, ref.mid, ref.far
    grad_wide, direct = ref.grad_wide, ref.direct
    cuts = dims.cuts

    def near_copies(b, c):
        at = pl.ds(cuts[c][0], cuts[c][1])
        return [
            copy(
                part.at[b, peer, :, at],
                got.at[b, k, :, at],
                ref.s1.at[b, c, k],
                ref.r1.at[b, c, k],
                place("vars", peer, sizes),
            )
            for k, peer in enumerate(near)
        ]

    def away_copies(b, c):
        at = pl.ds(cuts[c][0], cuts[c][1])
        return [
            copy(
                mid.at[b, peer, at],
                far.at[b, k, at],
                ref.s2.at[b, c, k],
                ref.r2.at[b, c, k],
                place("loss", peer, sizes),
            )
            for k, peer in enumerate(away)
        ]

    def pass_on(b, c):
        for made in near_copies(b, c):
            made.wait()
        at = pl.ds(cuts[c][0], cuts[c][1])
        for j in range(loss_count):
            value = part[b, core, j, at].astype(F32)
            for k in range(core_count - 1):
                value = value + got[b, k, j, at].astype(F32)
            mid[b, j, at] = value.astype(BF16)
        for made in away_copies(b, c):
            made.start()

    def send_on(b):
        for c in range(len(cuts)):
            pass_on(b, c)

    mixer = mix[...].reshape(-1, width)
    span = 4 * var_count

    def prepare(some):
        y = jnp.dot(
            jnp.concatenate([f_rolled[b] for b in some], axis=0),
            by_row[...],
            preferred_element_type=F32,
        )
        wide_span = y.shape[1] // WR
        tiles, own_tiles = [], []
        for n in range(len(some)):
            pieces = []
            for o in range(4):
                at = (n * 4 + o) * cols
                pieces.append(
                    jnp.concatenate(
                        [
                            y[at : at + cols, r * wide_span : (r + 1) * wide_span]
                            for r in range(WR)
                        ],
                        axis=0,
                    ).astype(BF16)
                )
            tiles.append(jnp.concatenate(pieces, axis=1))
            own_tiles.append(jnp.concatenate([piece[:, :span] for piece in pieces], axis=1))
        y = jnp.dot(jnp.concatenate(tiles, axis=0), mixer, preferred_element_type=F32)
        for n, b in enumerate(some):
            ref.grad_out[b] = y[n * rows : (n + 1) * rows].astype(BF16)
        y = jnp.dot(
            jnp.concatenate(own_tiles, axis=0), ref.decoder[...], preferred_element_type=F32
        )
        for n, b in enumerate(some):
            direct[b] = y[n * rows : (n + 1) * rows]

    def block(b):
        prepare([b])
        if b > 0:
            send_on(b - 1)
        grad_out = ref.grad_out[b]
        grads = [[], [], []]
        for h in range(heads):
            q, k, v = (qkv[b, i * heads + h] for i in range(3))
            go = grad_out[:, h * HEAD : (h + 1) * HEAD]
            weights = soft[b, h]
            grads[2].append(
                lax.dot_general(
                    weights.astype(BF16), go, first, preferred_element_type=F32
                ).astype(BF16)
            )
            grad_weights = lax.dot_general(go, v, NT, preferred_element_type=F32)
            inner = jnp.sum(weights * grad_weights, axis=-1, keepdims=True)
            score_round = (weights * (grad_weights - inner) * scale).astype(BF16)
            grads[0].append(jnp.dot(score_round, k, preferred_element_type=F32).astype(BF16))
            grads[1].append(
                lax.dot_general(score_round, q, first, preferred_element_type=F32).astype(BF16)
            )
        stacked = jnp.concatenate(grads[0] + grads[1] + grads[2], axis=1)
        grad_wide[...] = jnp.dot(stacked, w_flat[...], preferred_element_type=F32)
        for c, (start, size) in enumerate(cuts):
            at = start
            while at < start + size:
                step = min(48, start + size - at)
                scaled = grad_wide[at : at + step] * gain
                normed = wide[b, at : at + step]
                local = inv[b, at : at + step, :1] * (
                    scaled
                    - jnp.mean(scaled, axis=-1, keepdims=True)
                    - normed * jnp.mean(scaled * normed, axis=-1, keepdims=True)
                )
                local = (local + direct[b, at : at + step]).astype(BF16)
                for l in range(loss_count):
                    for v in range(core_count):
                        lane = (l * core_count + v) * share
                        part[b, v, l, at : at + step] = local[:, lane : lane + share]
                at += step
            for made in near_copies(b, c):
                made.start()

    for b in range(blocks):
        block(b)
    for c in range(len(cuts)):
        pass_on(blocks - 1, c)
    outs = [jnp.zeros((col_count, share), F32) for _ in range(WR)]
    for b in range(blocks):
        for c in range(len(cuts)):
            for made in away_copies(b, c):
                made.wait()
        value = mid[b, loss].astype(F32)
        for k in range(loss_count - 1):
            value = value + far[b, k].astype(F32)
        value = value.astype(BF16)
        for r in range(WR):
            outs[r] = outs[r] + jnp.dot(back[b, r], value, preferred_element_type=F32)
    for r in range(WR):
        ref.input_grad[r] = outs[r].astype(BF16)
    settled.wait()


def fused(shift, inputs, sizes, cols, weight, lats, collective_id):
    procs = sizes["proc"]
    loss_count, core_count = sizes["loss"], sizes["vars"]
    group_count = loss_count * core_count
    modes, lat_all, _ = inputs.legendre.shape
    var_count = inputs.pred.shape[0] // lats
    each = var_count // procs
    half = 2 * var_count
    row_count, col_count, model = inputs.tokens.shape
    blocks = row_count // WR * col_count // cols
    rows = WR * cols
    width = inputs.wproj.shape[0] // group_count
    heads = width // HEAD
    share = model // group_count
    cut = rows // 2 // 16 * 16 + 16 if rows // 2 % 16 else rows // 2
    cuts = ((0, cut), (cut, rows - cut))
    dims = types.SimpleNamespace(
        procs=procs,
        modes=modes,
        vars=var_count,
        lats=lats,
        blocks=blocks,
        cols=cols,
        heads=heads,
        share=share,
        weight=weight,
        terms=LDEG * modes * procs,
        loads=tuple(vars(inputs)),
        cuts=cuts,
    )
    dma = pltpu.SemaphoreType.DMA
    band = lats * var_count
    outs = dict(
        amse=((1, var_count), F32),
        field_grad=((var_count * lats, LON), F32),
        input_grad=((row_count, col_count, share), BF16),
    )
    scratch = dict(
        y_out=((procs, 2 * modes, lats * half), BF16),
        y_in=((procs, 2 * modes, lats * half), BF16),
        x_wide=((procs * lats * half // 128 * 2 * modes, 128), F32),
        leg=(inputs.legendre.shape, BF16),
        harm=((modes, 2 * half, LDEG), F32),
        power=((procs, 3 * each, LDEG), F32),
        parts=((procs - 1, 3 * each, LDEG), F32),
        acc=((3 * each, LDEG), F32),
        terms_in=((procs, 3 * each, LDEG), F32),
        g_wide=((modes * lat_all, 128), F32),
        g_out=((procs, 2 * modes, band), BF16),
        grid=((var_count * lats, LON), F32),
        coeff=((group_count, procs, 2 * modes, band), BF16),
        by_row=((2 * modes * procs, group_count * band), BF16),
        mix_out=((group_count, 4, 4 * var_count, width), BF16),
        mix=((4, group_count, 4 * var_count, width), BF16),
        wide=((blocks, rows, model), F32),
        inv=((blocks, rows, 128), F32),
        norm_out=((blocks, rows, model), BF16),
        qkv=((blocks, 3 * heads, rows, HEAD), BF16),
        soft=((blocks, heads, rows, rows), F32),
        f_rolled=((blocks, 4 * cols, 2 * modes * procs), BF16),
        back=((blocks, WR, col_count, rows), BF16),
        grad_wide=((rows, model), F32),
        part=((blocks, core_count, loss_count, rows, share), BF16),
        direct=((blocks, rows, model), F32),
        grad_out=((blocks, rows, width), BF16),
        decoder=((16 * var_count, model), BF16),
        got=((blocks, core_count - 1, loss_count, rows, share), BF16),
        mid=((blocks, loss_count, rows, share), BF16),
        far=((blocks, loss_count - 1, rows, share), BF16),
    )
    ring, mates = (procs - 1,), (group_count - 1,)
    near, away = (blocks, len(cuts), core_count - 1), (blocks, len(cuts), loss_count - 1)
    sems = dict(load_sems=(len(vars(inputs)),))
    sems.update(sy=ring, ry=ring, sa=ring, ra=ring, sb=ring, rb=ring, sc=ring, rc=ring)
    sems.update(sd=(2,), rd=(2,), se=(procs,), re=(procs,), sm=mates, rm=mates)
    sems.update(grid_sem=())
    sems.update(s1=near, r1=near, s2=away, r2=away)
    names = ["shift"] + [name + "_hbm" for name in vars(inputs)] + list(outs) + list(vars(inputs))
    names += list(scratch) + list(sems)
    return pl.pallas_call(
        functools.partial(fused_kernel, sizes, dims, tuple(names)),
        out_shape=tuple(jax.ShapeDtypeStruct(shape, kind) for shape, kind in outs.values()),
        in_specs=[pl.BlockSpec(memory_space=pltpu.SMEM)]
        + [pl.BlockSpec(memory_space=pl.ANY)] * len(vars(inputs)),
        out_specs=(VMEM, pl.BlockSpec(memory_space=pl.ANY), VMEM),
        scratch_shapes=[pltpu.VMEM(x.shape, x.dtype) for x in vars(inputs).values()]
        + [pltpu.VMEM(shape, kind) for shape, kind in scratch.values()]
        + [dma(shape) if shape else dma for shape in sems.values()],
        compiler_params=pltpu.CompilerParams(
            collective_id=collective_id,
            has_side_effects=True,
            vmem_limit_bytes=60 * 1024 * 1024,
        ),
        name="fused",
    )(shift, *vars(inputs).values())


def settle_kernel(count, *refs):
    for i in range(count):
        refs[count + i][...] = refs[i][...]


def settle(*arrays):
    count = len(arrays)
    return pl.pallas_call(
        functools.partial(settle_kernel, count),
        out_shape=tuple(jax.ShapeDtypeStruct(x.shape, x.dtype) for x in arrays),
        in_specs=[VMEM] * count,
        out_specs=(VMEM,) * count,
        name="settle",
    )(*arrays)


def body(tokens, shift, w_qkv, w_proj, ln_gain, w_dec, prediction, target, legendre):
    sizes = {name: lax.axis_size(name) for name in ("proc", "loss", "vars")}
    procs = sizes["proc"]
    group_count = sizes["loss"] * sizes["vars"]
    modes, lat_all, _ = legendre.shape
    var_count, lats = prediction.shape[0], prediction.shape[1]
    row_count, col_count, model = tokens.shape
    cols = 120
    fits = (
        row_count == WR
        and sizes["loss"] == 2
        and sizes["vars"] == 2
        and lats == 8
        and var_count == 16
        and modes == 16
        and lat_all == procs * lats
        and var_count % procs == 0
        and model % (128 * group_count) == 0
    )
    if not fits:
        return body_general(
            tokens, shift, w_qkv, w_proj, ln_gain, w_dec, prediction, target, legendre
        )
    modes_all = modes * procs
    weight = lat_all * LON / (VARS * LDEG * modes_all)
    rows = fourier_basis(modes_all).transpose(0, 2, 1).reshape(2, procs, modes, LON)
    rows = rows.transpose(1, 0, 2, 3).reshape(2 * modes_all, LON).astype(np.float32)
    high = rows.astype(jnp.bfloat16)
    inputs = types.SimpleNamespace(
        basis=jnp.asarray(high[None]),
        pred=prediction.reshape(-1, LON),
        target=target.reshape(-1, LON),
        dec=w_dec.reshape(-1, 4, model),
        wproj=w_proj.reshape(-1, model),
        legendre=legendre,
        tokens=tokens,
        columns=jnp.asarray(rows.T.reshape(col_count, 4, -1).transpose(1, 0, 2), BF16),
        gain=ln_gain.reshape(-1, 128),
        w=w_qkv.transpose(1, 2, 3, 0).reshape(-1, model),
    )
    amse, field_grad, input_grad = settle(
        *fused(shift, inputs, sizes, cols, weight, lats, 7)
    )
    return (amse.reshape(-1), field_grad.reshape(var_count, lats, LON), input_grad)


def solution(mesh):
    return jax.shard_map(
        body,
        mesh=mesh,
        in_specs=(
            P("proc", None, None),
            P(),
            P(None, None, ("loss", "vars"), None),
            P(),
            P(),
            P(("loss", "vars"), None, None, None),
            P(("loss", "vars"), "proc", None),
            P(("loss", "vars"), "proc", None),
            P("proc", None, None),
        ),
        out_specs=(
            P(("loss", "vars")),
            P(("loss", "vars"), "proc", None),
            P("proc", None, ("loss", "vars")),
        ),
        check_vma=False,
    )
```
